256 devices in a mesh: vert: 16 (over x, z_hi), tm: 16 (over y, z_lo, core).
Axes of the slice: x: 4, y: 4, z: 8 (z_hi: 4, z_lo: 2; z = z_hi * 2 + z_lo), core: 2. Of those that a mesh axis runs over, the one named last changes fastest.
Arguments:
- source: bfloat16 [20480, 2048], P('vert', 'tm'), may hold values from -6 to 6
- band_taps: bfloat16 [2, 2, 65], replicated, may hold values from -0.75 to 0.75
- smooth_taps: bfloat16 [2, 65], replicated, may hold values from 0.0009 to 0.031
- parcel_ids: int32 [3, 20480], P(None, 'vert'), may hold values from 0 to 999, as said below
Outputs:
- envelope_coupling: float32 [16, 2, 1504, 1504], P('tm', None, 'vert')
The draws below stay inside these ranges and needn't reach their ends.
Inputs may be any that keep to these rules, and one draw needn't show every extreme that they name: `parcel_ids`: row r = 0, 1, 2 gives each vertex's parcel in the atlas of 100, 400 or 1000 parcels (values below that count); every parcel of each atlas has at least one vertex.
All inputs are finite; a program needn't handle non-finite values.
Results may differ from the reference program's by a relative error of at most 0.0053.
Values may be sent and summed in bfloat16 or wider, within the bound.
A program may use at most 64 MiB of HBM per device.

```python
import jax
import jax.numpy as jnp
from jax import lax

P1 = 100
P2 = 400
P3 = 1000
BANDS = 2
TAPS = 65
HALF = 32
LAG = 64
LAG_STEP = 1
NLAG = 129
VERT_DEV = 1280
T_DEV = 128
VERTICES = 20480
TIMES = 2048
PAR = 1504
N_VERT = 16
N_TM = 16


def draw_parcel_ids(key, part):
    levels = []
    for level, limit in enumerate((P1, P2, P3)):
        branch = jax.random.fold_in(key, 11 + level)
        first_key, second_key, third_key = jax.random.split(branch, 3)
        order = jax.random.permutation(first_key, VERTICES).astype(jnp.int32)
        left = jax.random.randint(second_key, (VERTICES,), 0, limit)
        right = jax.random.randint(third_key, (VERTICES,), 0, limit)
        levels.append(jnp.where(order < limit, order, jnp.minimum(left, right)))
    return jnp.stack(levels).astype(jnp.int32)


def draw_smooth_taps(key, part):
    branch = jax.random.fold_in(key, 29)
    phase_key, second_key, rough_key, floor_key = jax.random.split(branch, 4)
    phases = jax.random.randint(phase_key, (BANDS, 1), 0, 4).astype(jnp.int32)
    seconds = jax.random.randint(second_key, (BANDS, 1), 0, 8).astype(jnp.int32)
    position = jnp.arange(TAPS, dtype=jnp.int32)[None, :]
    comb = ((position + phases) % 4 == 0).astype(jnp.float32)
    sparse = ((position + seconds) % 8 == 0).astype(jnp.float32)
    pattern = jnp.maximum(comb, 0.6 * sparse)
    rough = jax.random.uniform(rough_key, (BANDS, TAPS), jnp.float32)
    floor_draw = jax.random.uniform(floor_key, (BANDS, TAPS), jnp.float32)
    peak = 0.6 + 0.4 * rough
    floor_level = 0.001 + 0.002 * floor_draw
    values = floor_level + 0.027 * pattern * peak
    return values.astype(jnp.float32).astype(jnp.bfloat16)


def shard_levels(stream_key, shape, shards, low, high):
    loudness, own = 1.0, jax.random.fold_in(stream_key, 6)
    for dim, shards_of in shards:
        heights = jnp.exp(jax.random.uniform(jax.random.fold_in(own, dim), (shards_of,), jnp.float32, low / len(shards), high / len(shards)))
        loudness = loudness * jnp.repeat(heights, shape[dim] // shards_of).reshape([-1 if axis == dim else 1 for axis in range(len(shape))])
    return loudness


def bell_draw(stream_key, extent, scale, most, pieces=(), kind=jnp.bfloat16):
    values = scale * jax.random.normal(stream_key, extent, jnp.float32)
    if pieces:
        values = values * shard_levels(stream_key, extent, pieces, -0.22, 0.18)
    return jnp.clip(values, -most, most).astype(kind)


def setup_inputs(seed: int = 0) -> dict:
    arg_keys = jax.random.split(jax.random.key(seed), 5)
    source = bell_draw(arg_keys[0], (VERTICES, TIMES), 1.0, 6.0, ((0, 16), (1, 16)))
    band_taps = bell_draw(arg_keys[1], (2, BANDS, TAPS), TAPS ** -0.5, 0.75)
    smooth_taps = draw_smooth_taps(jax.random.fold_in(arg_keys[4], 71), 0)
    parcel_ids = draw_parcel_ids(jax.random.fold_in(arg_keys[4], 71), 0)
    return dict(source=source, band_taps=band_taps, smooth_taps=smooth_taps, parcel_ids=parcel_ids)


EPSILON = 1e-05

def resolution_of(parcel):
    first = (parcel >= P1).astype(jnp.int32)
    second = (parcel >= P1 + P2).astype(jnp.int32)
    third = (parcel >= P1 + P2 + P3).astype(jnp.int32)
    return first + second + third

def envelopes_of(padded_tile, band_taps, smooth_taps):
    kernels = band_taps.astype(jnp.float32).reshape(2 * BANDS, 1, TAPS)
    wave = lax.conv_general_dilated(padded_tile.astype(jnp.float32)[:, None, :], kernels, (1,), 'VALID', dimension_numbers=('NCH', 'OIH', 'NCH'), precision=lax.Precision.HIGHEST)
    wave = wave.reshape(padded_tile.shape[0], 2, BANDS, TIMES + 2 * HALF)
    power = (wave[:, 0] * wave[:, 0] + wave[:, 1] * wave[:, 1]).astype(jnp.bfloat16)
    smooth = lax.conv_general_dilated(power.astype(jnp.float32), smooth_taps.astype(jnp.float32)[:, None, :], (1,), 'VALID', dimension_numbers=('NCH', 'OIH', 'NCH'), feature_group_count=BANDS, precision=lax.Precision.HIGHEST)
    return smooth.astype(jnp.bfloat16)

def reference(source, band_taps, smooth_taps, parcel_ids):
    padded = jnp.pad(source, ((0, 0), (2 * HALF, 2 * HALF)))
    offsets = jnp.array([0, P1, P1 + P2], dtype=jnp.int32)
    global_ids = (parcel_ids + offsets[:, None]).astype(jnp.int32)
    tiles = padded.reshape(N_VERT, VERT_DEV, TIMES + 4 * HALF)
    id_tiles = global_ids.reshape(3, N_VERT, VERT_DEV).transpose(1, 0, 2)

    def add_tile(sums, pair):
        tile, tile_ids = pair
        envelope = envelopes_of(tile, band_taps, smooth_taps).astype(jnp.float32).reshape(VERT_DEV, BANDS * TIMES)
        for level in range(3):
            sums = sums + jax.ops.segment_sum(envelope, tile_ids[level], num_segments=PAR)
        return (sums, None)
    sums = lax.scan(add_tile, jnp.zeros((PAR, BANDS * TIMES), jnp.float32), (tiles, id_tiles))[0]
    parcel_env = sums.reshape(PAR, BANDS, TIMES)
    extended = jnp.pad(parcel_env, ((0, 0), (0, 0), (LAG, LAG)))
    level_rows = resolution_of(jnp.arange(PAR, dtype=jnp.int32))
    same = ((level_rows[:, None] == level_rows[None, :]) & (level_rows[:, None] < 3)).astype(jnp.float32)

    def one_window(window):
        start = (window * T_DEV).astype(jnp.int32)
        part = lax.dynamic_slice_in_dim(extended, start, T_DEV + 2 * LAG, 2).astype(jnp.float32)
        level_mean = lax.optimization_barrier(jnp.mean(part[:, :, LAG:LAG + T_DEV], axis=2, keepdims=True))
        rounded = lax.optimization_barrier((part - level_mean).astype(jnp.bfloat16))
        centered = rounded.astype(jnp.float32)
        middle = centered[:, :, LAG:LAG + T_DEV]
        spread = lax.rsqrt(lax.optimization_barrier(jnp.mean(middle * middle, axis=2)) + EPSILON).T

        def add_lag(total, lag_idx):
            shifted = lax.dynamic_slice_in_dim(centered, (lag_idx * LAG_STEP).astype(jnp.int32), T_DEV, 2)
            inner = jnp.einsum('ibt,jbt->bij', middle, shifted, precision=lax.Precision.HIGHEST) / T_DEV
            corr = inner * spread[:, :, None] * spread[:, None, :]
            return (total + corr * corr, None)
        energy = lax.scan(add_lag, jnp.zeros((BANDS, PAR, PAR), jnp.float32), jnp.arange(NLAG, dtype=jnp.int32))[0]
        return energy / NLAG * same[None]
    return lax.map(one_window, jnp.arange(N_TM, dtype=jnp.int32))
```

```python
from functools import partial
import math

import jax
import jax.numpy as jnp
from jax import lax
from jax.experimental import pallas as pl
from jax.experimental.pallas import tpu as pltpu
from jax.sharding import PartitionSpec as P

P1 = 100
P2 = 400
P3 = 1000
BANDS = 2
TAPS = 65
HALF = 32
LAG = 64
LAG_STEP = 1
NLAG = 129

EPSILON = 1e-05

ROW_PAD = 96
LAG_CHUNK = 4
LAG_PAD = 132
COL_TILE = 256


def extended_2(cells, sides, width):
    for axis, dim in sides:
        count = lax.axis_size(axis)
        ends = count - 1
        head = lax.slice_in_dim(cells, 0, width, axis=dim)
        tail = lax.slice_in_dim(cells, cells.shape[dim] - width, cells.shape[dim], axis=dim)
        cells = jnp.concatenate(
            [
                lax.ppermute(tail, axis, [(i, (i + 1) % count) for i in range(ends)]),
                cells,
                lax.ppermute(head, axis, [((i + 1) % count, i) for i in range(ends)]),
            ],
            axis=dim,
        )
    return cells


def toeplitz_band(taps, n_out, n_in):
    period = jnp.concatenate([taps, jnp.zeros((n_in + 1 - taps.shape[0],), taps.dtype)])
    return jnp.tile(period, n_out)[: n_out * n_in].reshape(n_out, n_in)


def resolution_of(parcel):
    first = (parcel >= P1).astype(jnp.int32)
    second = (parcel >= P1 + P2).astype(jnp.int32)
    third = (parcel >= P1 + P2 + P3).astype(jnp.int32)
    return first + second + third


def centered_rows(extended, length):
    level_mean = jnp.mean(extended[:, :, LAG : LAG + length], axis=2, keepdims=True)
    centered = (extended - level_mean).astype(jnp.bfloat16)
    middle = centered[:, :, LAG : LAG + length]
    middle_wide = middle.astype(jnp.float32)
    spread = lax.rsqrt(jnp.mean(middle_wide * middle_wide, axis=2) + EPSILON)
    return (centered, middle, spread)


def fold_kernel(mid_ref, vt_ref, out_ref, lhs_ref):
    cols = vt_ref.shape[1]
    chunk_rows = LAG_CHUNK * ROW_PAD
    base = mid_ref[...].astype(jnp.float32)

    def fill(q, carry):
        rolled = pltpu.roll(base, q, 1)
        lhs_ref[pl.ds(pl.multiple_of(q * ROW_PAD, ROW_PAD), ROW_PAD), :] = rolled.astype(lhs_ref.dtype)
        return carry

    lax.fori_loop(0, NLAG, fill, 0)
    lhs_ref[NLAG * ROW_PAD :, :] = jnp.zeros(
        ((LAG_PAD - NLAG) * ROW_PAD, lhs_ref.shape[1]), lhs_ref.dtype
    )

    def column(c, carry):
        first = pl.multiple_of(c * COL_TILE, COL_TILE)
        rhs = vt_ref[:, pl.ds(first, COL_TILE)]

        def body(k, acc):
            start = pl.multiple_of(k * chunk_rows, chunk_rows)
            rows = lhs_ref[pl.ds(start, chunk_rows), :]
            r = jnp.dot(rows, rhs, preferred_element_type=jnp.float32)
            r = r * r
            return acc + r.reshape(LAG_CHUNK, ROW_PAD, COL_TILE).sum(axis=0)

        acc = lax.fori_loop(
            0, LAG_PAD // LAG_CHUNK, body, jnp.zeros((ROW_PAD, COL_TILE), jnp.float32)
        )
        out_ref[:, pl.ds(first, COL_TILE)] = acc
        return carry

    lax.fori_loop(0, cols // COL_TILE, column, 0)


def lagged_energy(mid, vt):
    bands, rows, k = mid.shape
    cols = vt.shape[2]
    flops = 2 * bands * LAG_PAD * rows * k * cols
    return pl.pallas_call(
        fold_kernel,
        out_shape=jax.ShapeDtypeStruct((bands, rows, cols), jnp.float32),
        grid=(bands,),
        in_specs=[
            pl.BlockSpec((None, rows, k), lambda b: (b, 0, 0)),
            pl.BlockSpec((None, k, cols), lambda b: (b, 0, 0)),
        ],
        out_specs=pl.BlockSpec((None, rows, cols), lambda b: (b, 0, 0)),
        scratch_shapes=[pltpu.VMEM((LAG_PAD * rows, k), jnp.bfloat16)],
        compiler_params=pltpu.CompilerParams(vmem_limit_bytes=48 * 1024 * 1024),
        cost_estimate=pl.CostEstimate(
            flops=flops, bytes_accessed=2 * (mid.size + vt.size) + 4 * bands * rows * cols,
            transcendentals=0,
        ),
    )(mid, vt)


def local(source, band_taps, smooth_taps, parcel_ids):
    vert_dev, t_dev = source.shape
    owners = lax.axis_size("vert")
    total_par = (P1 + P2 + P3 + owners - 1) // owners * owners
    par_dev = total_par // owners
    n_mid = t_dev + 2 * HALF
    n_in = t_dev + 4 * HALF
    first_rows = jax.vmap(partial(toeplitz_band, n_out=n_mid, n_in=n_in))(
        band_taps.reshape(2 * BANDS, TAPS)
    )
    first_mat = first_rows.transpose(2, 0, 1).reshape(n_in, 2 * BANDS * n_mid)
    second_rows = jax.vmap(partial(toeplitz_band, n_out=t_dev, n_in=n_mid))(smooth_taps)
    second_mat = second_rows.transpose(0, 2, 1)
    widened = extended_2(source, (("tm", 1),), 2 * HALF)
    block_rows = math.gcd(vert_dev, 128)

    def filter_block(block):
        wave = jnp.dot(block, first_mat, preferred_element_type=jnp.float32).reshape(
            block_rows, 2, BANDS, n_mid
        )
        power = (wave[:, 0] * wave[:, 0] + wave[:, 1] * wave[:, 1]).astype(jnp.bfloat16)
        return jnp.einsum(
            "vbu,but->vbt", power, second_mat, preferred_element_type=jnp.float32
        ).astype(jnp.bfloat16)

    envelope = lax.map(filter_block, widened.reshape(vert_dev // block_rows, block_rows, n_in))
    flat_env = envelope.reshape(vert_dev, BANDS * t_dev)
    offsets = jnp.array([0, P1, P1 + P2], dtype=jnp.int32)
    global_ids = parcel_ids + offsets[:, None]
    owner_start = lax.axis_index("vert") * par_dev

    wanted = lax.iota(jnp.int32, total_par)
    hits = jnp.sum(
        (global_ids[:, None, :] == wanted[None, :, None]).astype(jnp.bfloat16), axis=0
    )
    pooled = jnp.dot(hits, flat_env, preferred_element_type=jnp.float32)
    own_sums = lax.psum_scatter(pooled, "vert", scatter_dimension=0, tiled=True)
    own_env = own_sums.reshape(par_dev, BANDS, t_dev)
    own_ext = extended_2(own_env, (("tm", 2),), LAG)
    centered, own_middle, own_spread = centered_rows(own_ext, t_dev)

    gathered = lax.all_gather(centered.transpose(1, 0, 2), "vert", axis=1, tiled=True)
    vis_mid = gathered[:, :, LAG : LAG + t_dev].astype(jnp.float32)
    vis_spread = lax.rsqrt(jnp.mean(vis_mid * vis_mid, axis=2) + EPSILON)
    cols = -(-total_par // COL_TILE) * COL_TILE
    vt = jnp.pad(gathered, ((0, 0), (0, cols - total_par), (0, 0))).transpose(0, 2, 1)
    mid = jnp.pad(
        own_middle.transpose(1, 0, 2), ((0, 0), (0, ROW_PAD - par_dev), (0, t_dev))
    )
    energy = lagged_energy(mid, vt)[:, :par_dev, :total_par]

    scale = own_spread.T[:, :, None] * vis_spread[:, None, :] / t_dev
    own_level = resolution_of(owner_start + lax.iota(jnp.int32, par_dev))
    all_level = resolution_of(lax.iota(jnp.int32, total_par))
    same = ((own_level[:, None] == all_level[None, :]) & (own_level[:, None] < 3)).astype(
        jnp.float32
    )
    coupling = energy * scale * scale * same[None] / NLAG
    return coupling[None]


def solution(mesh):
    return jax.shard_map(
        local,
        mesh=mesh,
        in_specs=(P("vert", "tm"), P(), P(), P(None, "vert")),
        out_specs=P("tm", None, "vert", None),
        check_vma=False,
    )
```

```python
from functools import partial
import math

import jax
import jax.numpy as jnp
from jax import lax
from jax.experimental import pallas as pl
from jax.experimental.pallas import tpu as pltpu
from jax.sharding import PartitionSpec as P

P1 = 100
P2 = 400
P3 = 1000
BANDS = 2
TAPS = 65
HALF = 32
LAG = 64
LAG_STEP = 1
NLAG = 129

EPSILON = 1e-05

ROW_PAD = 96
LAG_CHUNKS = 11
LAG_PAD = 132
COL_TILE = 256


def extended_2(cells, sides, width):
    for axis, dim in sides:
        count = lax.axis_size(axis)
        ends = count - 1
        head = lax.slice_in_dim(cells, 0, width, axis=dim)
        tail = lax.slice_in_dim(cells, cells.shape[dim] - width, cells.shape[dim], axis=dim)
        cells = jnp.concatenate(
            [
                lax.ppermute(tail, axis, [(i, (i + 1) % count) for i in range(ends)]),
                cells,
                lax.ppermute(head, axis, [((i + 1) % count, i) for i in range(ends)]),
            ],
            axis=dim,
        )
    return cells


def toeplitz_band(taps, n_out, n_in):
    period = jnp.concatenate([taps, jnp.zeros((n_in + 1 - taps.shape[0],), taps.dtype)])
    return jnp.tile(period, n_out)[: n_out * n_in].reshape(n_out, n_in)


def resolution_of(parcel):
    first = (parcel >= P1).astype(jnp.int32)
    second = (parcel >= P1 + P2).astype(jnp.int32)
    third = (parcel >= P1 + P2 + P3).astype(jnp.int32)
    return first + second + third


def centered_rows(extended, length):
    level_mean = jnp.mean(extended[:, :, LAG : LAG + length], axis=2, keepdims=True)
    centered = (extended - level_mean).astype(jnp.bfloat16)
    middle = centered[:, :, LAG : LAG + length]
    middle_wide = middle.astype(jnp.float32)
    spread = lax.rsqrt(jnp.mean(middle_wide * middle_wide, axis=2) + EPSILON)
    return (centered, middle, spread)


def fold_kernel(mid_ref, vt_ref, out_ref, lhs_ref):
    cols = vt_ref.shape[1]
    base = mid_ref[...].astype(jnp.float32)
    for q in range(NLAG):
        lhs_ref[q * ROW_PAD : (q + 1) * ROW_PAD, :] = pltpu.roll(base, q, 1).astype(lhs_ref.dtype)
    lhs_ref[NLAG * ROW_PAD :, :] = jnp.zeros(
        ((LAG_PAD - NLAG) * ROW_PAD, lhs_ref.shape[1]), lhs_ref.dtype
    )
    step = LAG_PAD // LAG_CHUNKS

    def column(c, carry):
        first = pl.multiple_of(c * COL_TILE, COL_TILE)
        rhs = vt_ref[:, pl.ds(first, COL_TILE)]
        acc = jnp.zeros((ROW_PAD, COL_TILE), jnp.float32)
        for h in range(LAG_CHUNKS):
            rows = lhs_ref[h * step * ROW_PAD : (h + 1) * step * ROW_PAD, :]
            r = jnp.dot(rows, rhs, preferred_element_type=jnp.float32)
            acc = acc + (r * r).reshape(step, ROW_PAD, COL_TILE).sum(axis=0)
        out_ref[:, pl.ds(first, COL_TILE)] = acc
        return carry

    lax.fori_loop(0, cols // COL_TILE, column, 0)


def lagged_energy(mid, vt):
    bands, rows, k = mid.shape
    cols = vt.shape[2]
    flops = 2 * bands * LAG_PAD * rows * k * cols
    return pl.pallas_call(
        fold_kernel,
        out_shape=jax.ShapeDtypeStruct((bands, rows, cols), jnp.float32),
        grid=(bands,),
        in_specs=[
            pl.BlockSpec((None, rows, k), lambda b: (b, 0, 0)),
            pl.BlockSpec((None, k, cols), lambda b: (b, 0, 0)),
        ],
        out_specs=pl.BlockSpec((None, rows, cols), lambda b: (b, 0, 0)),
        scratch_shapes=[pltpu.VMEM((LAG_PAD * rows, k), jnp.bfloat16)],
        compiler_params=pltpu.CompilerParams(vmem_limit_bytes=48 * 1024 * 1024),
        cost_estimate=pl.CostEstimate(
            flops=flops, bytes_accessed=2 * (mid.size + vt.size) + 4 * bands * rows * cols,
            transcendentals=0,
        ),
    )(mid, vt)


def local(source, band_taps, smooth_taps, parcel_ids):
    vert_dev, t_dev = source.shape
    owners = lax.axis_size("vert")
    total_par = (P1 + P2 + P3 + owners - 1) // owners * owners
    par_dev = total_par // owners
    n_mid = t_dev + 2 * HALF
    n_in = t_dev + 4 * HALF
    first_rows = jax.vmap(partial(toeplitz_band, n_out=n_mid, n_in=n_in))(
        band_taps.reshape(2 * BANDS, TAPS)
    )
    first_mat = first_rows.transpose(2, 0, 1).reshape(n_in, 2 * BANDS * n_mid)
    second_rows = jax.vmap(partial(toeplitz_band, n_out=t_dev, n_in=n_mid))(smooth_taps)
    second_mat = second_rows.transpose(0, 2, 1)
    widened = extended_2(source, (("tm", 1),), 2 * HALF)
    block_rows = math.gcd(vert_dev, 128)

    def filter_block(block):
        wave = jnp.dot(block, first_mat, preferred_element_type=jnp.float32).reshape(
            block_rows, 2, BANDS, n_mid
        )
        power = (wave[:, 0] * wave[:, 0] + wave[:, 1] * wave[:, 1]).astype(jnp.bfloat16)
        return jnp.einsum(
            "vbu,but->vbt", power, second_mat, preferred_element_type=jnp.float32
        ).astype(jnp.bfloat16)

    envelope = lax.map(filter_block, widened.reshape(vert_dev // block_rows, block_rows, n_in))
    flat_env = envelope.reshape(vert_dev, BANDS * t_dev)
    offsets = jnp.array([0, P1, P1 + P2], dtype=jnp.int32)
    global_ids = parcel_ids + offsets[:, None]
    owner_start = lax.axis_index("vert") * par_dev

    wanted = lax.iota(jnp.int32, total_par)
    hits = jnp.sum(
        (global_ids[:, None, :] == wanted[None, :, None]).astype(jnp.bfloat16), axis=0
    )
    pooled = jnp.dot(hits, flat_env, preferred_element_type=jnp.float32)
    own_sums = lax.psum_scatter(pooled, "vert", scatter_dimension=0, tiled=True)
    own_env = own_sums.reshape(par_dev, BANDS, t_dev)
    own_ext = extended_2(own_env, (("tm", 2),), LAG)
    centered, own_middle, own_spread = centered_rows(own_ext, t_dev)

    gathered = lax.all_gather(centered.transpose(1, 0, 2), "vert", axis=1, tiled=True)
    vis_mid = gathered[:, :, LAG : LAG + t_dev].astype(jnp.float32)
    vis_spread = lax.rsqrt(jnp.mean(vis_mid * vis_mid, axis=2) + EPSILON)
    cols = -(-total_par // COL_TILE) * COL_TILE
    vt = jnp.pad(gathered, ((0, 0), (0, cols - total_par), (0, 0))).transpose(0, 2, 1)
    mid = jnp.pad(
        own_middle.transpose(1, 0, 2), ((0, 0), (0, ROW_PAD - par_dev), (0, t_dev))
    )
    energy = lagged_energy(mid, vt)[:, :par_dev, :total_par]

    scale = own_spread.T[:, :, None] * vis_spread[:, None, :] / t_dev
    own_level = resolution_of(owner_start + lax.iota(jnp.int32, par_dev))
    all_level = resolution_of(lax.iota(jnp.int32, total_par))
    same = ((own_level[:, None] == all_level[None, :]) & (own_level[:, None] < 3)).astype(
        jnp.float32
    )
    coupling = energy * scale * scale * same[None] / NLAG
    return coupling[None]


def solution(mesh):
    return jax.shard_map(
        local,
        mesh=mesh,
        in_specs=(P("vert", "tm"), P(), P(), P(None, "vert")),
        out_specs=P("tm", None, "vert", None),
        check_vma=False,
    )
```

```python
from functools import partial
import math

import jax
import jax.numpy as jnp
from jax import lax
from jax.experimental import pallas as pl
from jax.experimental.pallas import tpu as pltpu
from jax.sharding import PartitionSpec as P

P1 = 100
P2 = 400
P3 = 1000
BANDS = 2
TAPS = 65
HALF = 32
LAG = 64
LAG_STEP = 1
NLAG = 129

EPSILON = 1e-05

ROW_PAD = 96
LAG_CHUNKS = 11
LAG_PAD = 132
COL_TILE = 256


def extended_2(cells, sides, width):
    for axis, dim in sides:
        count = lax.axis_size(axis)
        ends = count - 1
        head = lax.slice_in_dim(cells, 0, width, axis=dim)
        tail = lax.slice_in_dim(cells, cells.shape[dim] - width, cells.shape[dim], axis=dim)
        cells = jnp.concatenate(
            [
                lax.ppermute(tail, axis, [(i, (i + 1) % count) for i in range(ends)]),
                cells,
                lax.ppermute(head, axis, [((i + 1) % count, i) for i in range(ends)]),
            ],
            axis=dim,
        )
    return cells


def toeplitz_band(taps, n_out, n_in):
    period = jnp.concatenate([taps, jnp.zeros((n_in + 1 - taps.shape[0],), taps.dtype)])
    return jnp.tile(period, n_out)[: n_out * n_in].reshape(n_out, n_in)


def resolution_of(parcel):
    first = (parcel >= P1).astype(jnp.int32)
    second = (parcel >= P1 + P2).astype(jnp.int32)
    third = (parcel >= P1 + P2 + P3).astype(jnp.int32)
    return first + second + third


def centered_rows(extended, length):
    level_mean = jnp.mean(extended[:, :, LAG : LAG + length], axis=2, keepdims=True)
    centered = (extended - level_mean).astype(jnp.bfloat16)
    middle = centered[:, :, LAG : LAG + length]
    middle_wide = middle.astype(jnp.float32)
    spread = lax.rsqrt(jnp.mean(middle_wide * middle_wide, axis=2) + EPSILON)
    return (centered, middle, spread)


def fold_kernel(mid_ref, vt_ref, out_ref, lhs_ref):
    cols = vt_ref.shape[1]
    base = mid_ref[...].astype(jnp.float32)
    for q in range(NLAG):
        lhs_ref[q * ROW_PAD : (q + 1) * ROW_PAD, :] = pltpu.roll(base, q, 1).astype(lhs_ref.dtype)
    lhs_ref[NLAG * ROW_PAD :, :] = jnp.zeros(
        ((LAG_PAD - NLAG) * ROW_PAD, lhs_ref.shape[1]), lhs_ref.dtype
    )
    step = LAG_PAD // LAG_CHUNKS

    def column(c, carry):
        first = pl.multiple_of(c * COL_TILE, COL_TILE)
        rhs = vt_ref[:, pl.ds(first, COL_TILE)]
        acc = jnp.zeros((ROW_PAD, COL_TILE), jnp.float32)
        for h in range(LAG_CHUNKS):
            rows = lhs_ref[h * step * ROW_PAD : (h + 1) * step * ROW_PAD, :]
            r = jnp.dot(rows, rhs, preferred_element_type=jnp.float32)
            acc = acc + (r * r).reshape(step, ROW_PAD, COL_TILE).sum(axis=0)
        out_ref[:, pl.ds(first, COL_TILE)] = acc
        return carry

    lax.fori_loop(0, cols // COL_TILE, column, 0)


def lagged_energy(mid, vt):
    bands, rows, k = mid.shape
    cols = vt.shape[2]
    flops = 2 * bands * LAG_PAD * rows * k * cols
    return pl.pallas_call(
        fold_kernel,
        out_shape=jax.ShapeDtypeStruct((bands, rows, cols), jnp.float32),
        grid=(bands,),
        in_specs=[
            pl.BlockSpec((None, rows, k), lambda b: (b, 0, 0)),
            pl.BlockSpec((None, k, cols), lambda b: (b, 0, 0)),
        ],
        out_specs=pl.BlockSpec((None, rows, cols), lambda b: (b, 0, 0)),
        scratch_shapes=[pltpu.VMEM((LAG_PAD * rows, k), jnp.bfloat16)],
        compiler_params=pltpu.CompilerParams(vmem_limit_bytes=48 * 1024 * 1024),
        cost_estimate=pl.CostEstimate(
            flops=flops, bytes_accessed=2 * (mid.size + vt.size) + 4 * bands * rows * cols,
            transcendentals=0,
        ),
    )(mid, vt)


def exchange_kernel(spread, x_ref, out_ref, send_sems, recv_sems, local_sem):
    n = out_ref.shape[0]
    me = lax.axis_index("vert")
    tm = lax.axis_index("tm")
    barrier = pltpu.get_barrier_semaphore()
    for k in range(1, n):
        peer = lax.rem(me + k, n)
        pl.semaphore_signal(
            barrier, inc=1, device_id=(peer, tm), device_id_type=pl.DeviceIdType.MESH
        )
    pl.semaphore_wait(barrier, n - 1)
    copies = []
    for k in range(1, n):
        peer = lax.rem(me + k, n)
        copy = pltpu.make_async_remote_copy(
            src_ref=x_ref.at[peer] if spread else x_ref,
            dst_ref=out_ref.at[me],
            send_sem=send_sems.at[k],
            recv_sem=recv_sems.at[k],
            device_id=(peer, tm),
            device_id_type=pl.DeviceIdType.MESH,
        )
        copy.start()
        copies.append(copy)
    own = pltpu.make_async_copy(x_ref.at[me] if spread else x_ref, out_ref.at[me], local_sem)
    own.start()
    own.wait()
    for copy in copies:
        copy.wait()


def exchange(x, n, spread, collective_id):
    block = x.shape[1:] if spread else x.shape
    return pl.pallas_call(
        partial(exchange_kernel, spread),
        out_shape=jax.ShapeDtypeStruct((n,) + block, x.dtype),
        in_specs=[pl.BlockSpec(memory_space=pl.ANY)],
        out_specs=pl.BlockSpec(memory_space=pl.ANY),
        scratch_shapes=[
            pltpu.SemaphoreType.DMA((n,)),
            pltpu.SemaphoreType.DMA((n,)),
            pltpu.SemaphoreType.DMA(()),
        ],
        compiler_params=pltpu.CompilerParams(collective_id=collective_id, has_side_effects=True),
    )(x)


def local(source, band_taps, smooth_taps, parcel_ids):
    vert_dev, t_dev = source.shape
    owners = lax.axis_size("vert")
    total_par = (P1 + P2 + P3 + owners - 1) // owners * owners
    par_dev = total_par // owners
    n_mid = t_dev + 2 * HALF
    n_in = t_dev + 4 * HALF
    first_rows = jax.vmap(partial(toeplitz_band, n_out=n_mid, n_in=n_in))(
        band_taps.reshape(2 * BANDS, TAPS)
    )
    first_mat = first_rows.transpose(2, 0, 1).reshape(n_in, 2 * BANDS * n_mid)
    second_rows = jax.vmap(partial(toeplitz_band, n_out=t_dev, n_in=n_mid))(smooth_taps)
    second_mat = second_rows.transpose(0, 2, 1)
    widened = extended_2(source, (("tm", 1),), 2 * HALF)
    block_rows = math.gcd(vert_dev, 128)

    def filter_block(block):
        wave = jnp.dot(block, first_mat, preferred_element_type=jnp.float32).reshape(
            block_rows, 2, BANDS, n_mid
        )
        power = (wave[:, 0] * wave[:, 0] + wave[:, 1] * wave[:, 1]).astype(jnp.bfloat16)
        return jnp.einsum(
            "vbu,but->vbt", power, second_mat, preferred_element_type=jnp.float32
        ).astype(jnp.bfloat16)

    envelope = lax.map(filter_block, widened.reshape(vert_dev // block_rows, block_rows, n_in))
    flat_env = envelope.reshape(vert_dev, BANDS * t_dev)
    offsets = jnp.array([0, P1, P1 + P2], dtype=jnp.int32)
    global_ids = parcel_ids + offsets[:, None]
    owner_start = lax.axis_index("vert") * par_dev

    wanted = lax.iota(jnp.int32, total_par)
    hits = jnp.sum(
        (global_ids[:, None, :] == wanted[None, :, None]).astype(jnp.bfloat16), axis=0
    )
    pooled = jnp.dot(hits, flat_env, preferred_element_type=jnp.float32)
    parts = exchange(pooled.reshape(owners, par_dev, BANDS * t_dev), owners, True, 0)
    own_sums = jnp.sum(parts, axis=0)
    own_env = own_sums.reshape(par_dev, BANDS, t_dev)
    own_ext = extended_2(own_env, (("tm", 2),), LAG)
    centered, own_middle, own_spread = centered_rows(own_ext, t_dev)

    blocks = exchange(centered.transpose(1, 0, 2), owners, False, 1)
    gathered = blocks.transpose(1, 0, 2, 3).reshape(BANDS, total_par, 2 * LAG + t_dev)
    vis_mid = gathered[:, :, LAG : LAG + t_dev].astype(jnp.float32)
    vis_spread = lax.rsqrt(jnp.mean(vis_mid * vis_mid, axis=2) + EPSILON)
    cols = -(-total_par // COL_TILE) * COL_TILE
    vt = jnp.pad(gathered, ((0, 0), (0, cols - total_par), (0, 0))).transpose(0, 2, 1)
    mid = jnp.pad(
        own_middle.transpose(1, 0, 2), ((0, 0), (0, ROW_PAD - par_dev), (0, t_dev))
    )
    energy = lagged_energy(mid, vt)[:, :par_dev, :total_par]

    scale = own_spread.T[:, :, None] * vis_spread[:, None, :] / t_dev
    own_level = resolution_of(owner_start + lax.iota(jnp.int32, par_dev))
    all_level = resolution_of(lax.iota(jnp.int32, total_par))
    same = ((own_level[:, None] == all_level[None, :]) & (own_level[:, None] < 3)).astype(
        jnp.float32
    )
    coupling = energy * scale * scale * same[None] / NLAG
    return coupling[None]


def solution(mesh):
    return jax.shard_map(
        local,
        mesh=mesh,
        in_specs=(P("vert", "tm"), P(), P(), P(None, "vert")),
        out_specs=P("tm", None, "vert", None),
        check_vma=False,
    )
```

```python
from functools import partial
import math

import jax
import jax.numpy as jnp
from jax import lax
from jax.experimental import pallas as pl
from jax.experimental.pallas import tpu as pltpu
from jax.sharding import PartitionSpec as P

P1 = 100
P2 = 400
P3 = 1000
BANDS = 2
TAPS = 65
HALF = 32
LAG = 64
LAG_STEP = 1
NLAG = 129

EPSILON = 1e-05

ROW_PAD = 96
LAG_CHUNKS = 11
LAG_PAD = 132
COL_TILE = 256
VERT_MINOR = 4


def extended_2(cells, sides, width):
    for axis, dim in sides:
        count = lax.axis_size(axis)
        ends = count - 1
        head = lax.slice_in_dim(cells, 0, width, axis=dim)
        tail = lax.slice_in_dim(cells, cells.shape[dim] - width, cells.shape[dim], axis=dim)
        cells = jnp.concatenate(
            [
                lax.ppermute(tail, axis, [(i, (i + 1) % count) for i in range(ends)]),
                cells,
                lax.ppermute(head, axis, [((i + 1) % count, i) for i in range(ends)]),
            ],
            axis=dim,
        )
    return cells


def toeplitz_band(taps, n_out, n_in):
    period = jnp.concatenate([taps, jnp.zeros((n_in + 1 - taps.shape[0],), taps.dtype)])
    return jnp.tile(period, n_out)[: n_out * n_in].reshape(n_out, n_in)


def resolution_of(parcel):
    first = (parcel >= P1).astype(jnp.int32)
    second = (parcel >= P1 + P2).astype(jnp.int32)
    third = (parcel >= P1 + P2 + P3).astype(jnp.int32)
    return first + second + third


def centered_rows(extended, length):
    level_mean = jnp.mean(extended[:, :, LAG : LAG + length], axis=2, keepdims=True)
    centered = (extended - level_mean).astype(jnp.bfloat16)
    middle = centered[:, :, LAG : LAG + length]
    middle_wide = middle.astype(jnp.float32)
    spread = lax.rsqrt(jnp.mean(middle_wide * middle_wide, axis=2) + EPSILON)
    return (centered, middle, spread)


def fold_kernel(mid_ref, vt_ref, out_ref, lhs_ref):
    cols = vt_ref.shape[1]
    base = mid_ref[...].astype(jnp.float32)
    for q in range(NLAG):
        lhs_ref[q * ROW_PAD : (q + 1) * ROW_PAD, :] = pltpu.roll(base, q, 1).astype(lhs_ref.dtype)
    lhs_ref[NLAG * ROW_PAD :, :] = jnp.zeros(
        ((LAG_PAD - NLAG) * ROW_PAD, lhs_ref.shape[1]), lhs_ref.dtype
    )
    step = LAG_PAD // LAG_CHUNKS

    def column(c, carry):
        first = pl.multiple_of(c * COL_TILE, COL_TILE)
        rhs = vt_ref[:, pl.ds(first, COL_TILE)]
        acc = jnp.zeros((ROW_PAD, COL_TILE), jnp.float32)
        for h in range(LAG_CHUNKS):
            rows = lhs_ref[h * step * ROW_PAD : (h + 1) * step * ROW_PAD, :]
            r = jnp.dot(rows, rhs, preferred_element_type=jnp.float32)
            acc = acc + (r * r).reshape(step, ROW_PAD, COL_TILE).sum(axis=0)
        out_ref[:, pl.ds(first, COL_TILE)] = acc
        return carry

    lax.fori_loop(0, cols // COL_TILE, column, 0)


def lagged_energy(mid, vt):
    bands, rows, k = mid.shape
    cols = vt.shape[2]
    flops = 2 * bands * LAG_PAD * rows * k * cols
    return pl.pallas_call(
        fold_kernel,
        out_shape=jax.ShapeDtypeStruct((bands, rows, cols), jnp.float32),
        grid=(bands,),
        in_specs=[
            pl.BlockSpec((None, rows, k), lambda b: (b, 0, 0)),
            pl.BlockSpec((None, k, cols), lambda b: (b, 0, 0)),
        ],
        out_specs=pl.BlockSpec((None, rows, cols), lambda b: (b, 0, 0)),
        scratch_shapes=[pltpu.VMEM((LAG_PAD * rows, k), jnp.bfloat16)],
        compiler_params=pltpu.CompilerParams(vmem_limit_bytes=48 * 1024 * 1024),
        cost_estimate=pl.CostEstimate(
            flops=flops, bytes_accessed=2 * (mid.size + vt.size) + 4 * bands * rows * cols,
            transcendentals=0,
        ),
    )(mid, vt)


def mesh_peers(nx, nz):
    me = lax.axis_index("vert")
    tm = lax.axis_index("tm")
    mx, mz = me // nz, me % nz
    return me, tm, mx, mz


def greet(mx, mz, tm, nx, nz):
    barrier = pltpu.get_barrier_semaphore()
    for k in range(1, nx):
        pl.semaphore_signal(
            barrier, inc=1, device_id=(lax.rem(mx + k, nx) * nz + mz, tm),
            device_id_type=pl.DeviceIdType.MESH,
        )
    for k in range(1, nz):
        pl.semaphore_signal(
            barrier, inc=1, device_id=(mx * nz + lax.rem(mz + k, nz), tm),
            device_id_type=pl.DeviceIdType.MESH,
        )
    pl.semaphore_wait(barrier, nx + nz - 2)


def reduce_kernel(nx, nz, x_ref, out_ref, recv_a, part, recv_b, a_send, a_recv, b_send, b_recv):
    me, tm, mx, mz = mesh_peers(nx, nz)
    greet(mx, mz, tm, nx, nz)
    copies = []
    for k in range(1, nx):
        px = lax.rem(mx + k, nx)
        copy = pltpu.make_async_remote_copy(
            src_ref=x_ref.at[pl.ds(px * nz, nz)], dst_ref=recv_a.at[k - 1],
            send_sem=a_send.at[k - 1], recv_sem=a_recv.at[k - 1],
            device_id=(px * nz + mz, tm), device_id_type=pl.DeviceIdType.MESH,
        )
        copy.start()
        copies.append(copy)
    for copy in copies:
        copy.wait()
    acc = x_ref[pl.ds(mx * nz, nz)]
    for k in range(1, nx):
        acc = acc + recv_a[k - 1]
    part[...] = acc
    copies = []
    for k in range(1, nz):
        pz = lax.rem(mz + k, nz)
        copy = pltpu.make_async_remote_copy(
            src_ref=part.at[pz], dst_ref=recv_b.at[k - 1],
            send_sem=b_send.at[k - 1], recv_sem=b_recv.at[k - 1],
            device_id=(mx * nz + pz, tm), device_id_type=pl.DeviceIdType.MESH,
        )
        copy.start()
        copies.append(copy)
    for copy in copies:
        copy.wait()
    total = part[mz]
    for k in range(1, nz):
        total = total + recv_b[k - 1]
    out_ref[...] = total


def reduce_to_owner(x, nx, nz):
    n, rows, w = x.shape
    return pl.pallas_call(
        partial(reduce_kernel, nx, nz),
        out_shape=jax.ShapeDtypeStruct((rows, w), x.dtype),
        in_specs=[pl.BlockSpec(memory_space=pltpu.VMEM)],
        out_specs=pl.BlockSpec(memory_space=pltpu.VMEM),
        scratch_shapes=[
            pltpu.VMEM((nx - 1, nz, rows, w), x.dtype),
            pltpu.VMEM((nz, rows, w), x.dtype),
            pltpu.VMEM((nz - 1, rows, w), x.dtype),
            pltpu.SemaphoreType.DMA((nx - 1,)),
            pltpu.SemaphoreType.DMA((nx - 1,)),
            pltpu.SemaphoreType.DMA((nz - 1,)),
            pltpu.SemaphoreType.DMA((nz - 1,)),
        ],
        compiler_params=pltpu.CompilerParams(collective_id=0, has_side_effects=True),
    )(x)


def gather_kernel(nx, nz, x_ref, out_ref, a_send, a_recv, b_send, b_recv, local_sem):
    me, tm, mx, mz = mesh_peers(nx, nz)
    greet(mx, mz, tm, nx, nz)
    own = pltpu.make_async_copy(x_ref, out_ref.at[me], local_sem)
    own.start()
    copies = []
    for k in range(1, nz):
        pz = lax.rem(mz + k, nz)
        copy = pltpu.make_async_remote_copy(
            src_ref=x_ref, dst_ref=out_ref.at[me],
            send_sem=a_send.at[k - 1], recv_sem=a_recv.at[k - 1],
            device_id=(mx * nz + pz, tm), device_id_type=pl.DeviceIdType.MESH,
        )
        copy.start()
        copies.append(copy)
    own.wait()
    for copy in copies:
        copy.wait()
    copies = []
    for k in range(1, nx):
        px = lax.rem(mx + k, nx)
        copy = pltpu.make_async_remote_copy(
            src_ref=out_ref.at[pl.ds(mx * nz, nz)], dst_ref=out_ref.at[pl.ds(mx * nz, nz)],
            send_sem=b_send.at[k - 1], recv_sem=b_recv.at[k - 1],
            device_id=(px * nz + mz, tm), device_id_type=pl.DeviceIdType.MESH,
        )
        copy.start()
        copies.append(copy)
    for copy in copies:
        copy.wait()


def gather_all(x, nx, nz):
    return pl.pallas_call(
        partial(gather_kernel, nx, nz),
        out_shape=jax.ShapeDtypeStruct((nx * nz,) + x.shape, x.dtype),
        in_specs=[pl.BlockSpec(memory_space=pl.ANY)],
        out_specs=pl.BlockSpec(memory_space=pl.ANY),
        scratch_shapes=[
            pltpu.SemaphoreType.DMA((nz - 1,)),
            pltpu.SemaphoreType.DMA((nz - 1,)),
            pltpu.SemaphoreType.DMA((nx - 1,)),
            pltpu.SemaphoreType.DMA((nx - 1,)),
            pltpu.SemaphoreType.DMA(()),
        ],
        compiler_params=pltpu.CompilerParams(collective_id=1, has_side_effects=True),
    )(x)


def local(source, band_taps, smooth_taps, parcel_ids):
    vert_dev, t_dev = source.shape
    owners = lax.axis_size("vert")
    total_par = (P1 + P2 + P3 + owners - 1) // owners * owners
    par_dev = total_par // owners
    n_mid = t_dev + 2 * HALF
    n_in = t_dev + 4 * HALF
    first_rows = jax.vmap(partial(toeplitz_band, n_out=n_mid, n_in=n_in))(
        band_taps.reshape(2 * BANDS, TAPS)
    )
    first_mat = first_rows.transpose(2, 0, 1).reshape(n_in, 2 * BANDS * n_mid)
    second_rows = jax.vmap(partial(toeplitz_band, n_out=t_dev, n_in=n_mid))(smooth_taps)
    second_mat = second_rows.transpose(0, 2, 1)
    widened = extended_2(source, (("tm", 1),), 2 * HALF)
    block_rows = math.gcd(vert_dev, 128)

    def filter_block(block):
        wave = jnp.dot(block, first_mat, preferred_element_type=jnp.float32).reshape(
            block_rows, 2, BANDS, n_mid
        )
        power = (wave[:, 0] * wave[:, 0] + wave[:, 1] * wave[:, 1]).astype(jnp.bfloat16)
        return jnp.einsum(
            "vbu,but->vbt", power, second_mat, preferred_element_type=jnp.float32
        ).astype(jnp.bfloat16)

    envelope = lax.map(filter_block, widened.reshape(vert_dev // block_rows, block_rows, n_in))
    flat_env = envelope.reshape(vert_dev, BANDS * t_dev)
    offsets = jnp.array([0, P1, P1 + P2], dtype=jnp.int32)
    global_ids = parcel_ids + offsets[:, None]
    owner_start = lax.axis_index("vert") * par_dev

    wanted = lax.iota(jnp.int32, total_par)
    hits = jnp.sum(
        (global_ids[:, None, :] == wanted[None, :, None]).astype(jnp.bfloat16), axis=0
    )
    pooled = jnp.dot(hits, flat_env, preferred_element_type=jnp.float32)
    nx = owners // VERT_MINOR
    own_sums = reduce_to_owner(pooled.reshape(owners, par_dev, BANDS * t_dev), nx, VERT_MINOR)
    own_env = own_sums.reshape(par_dev, BANDS, t_dev)
    own_ext = extended_2(own_env, (("tm", 2),), LAG)
    centered, own_middle, own_spread = centered_rows(own_ext, t_dev)

    blocks = gather_all(centered.transpose(1, 0, 2), nx, VERT_MINOR)
    gathered = blocks.transpose(1, 0, 2, 3).reshape(BANDS, total_par, 2 * LAG + t_dev)
    vis_mid = gathered[:, :, LAG : LAG + t_dev].astype(jnp.float32)
    vis_spread = lax.rsqrt(jnp.mean(vis_mid * vis_mid, axis=2) + EPSILON)
    cols = -(-total_par // COL_TILE) * COL_TILE
    vt = jnp.pad(gathered, ((0, 0), (0, cols - total_par), (0, 0))).transpose(0, 2, 1)
    mid = jnp.pad(
        own_middle.transpose(1, 0, 2), ((0, 0), (0, ROW_PAD - par_dev), (0, t_dev))
    )
    energy = lagged_energy(mid, vt)[:, :par_dev, :total_par]

    scale = own_spread.T[:, :, None] * vis_spread[:, None, :] / t_dev
    own_level = resolution_of(owner_start + lax.iota(jnp.int32, par_dev))
    all_level = resolution_of(lax.iota(jnp.int32, total_par))
    same = ((own_level[:, None] == all_level[None, :]) & (own_level[:, None] < 3)).astype(
        jnp.float32
    )
    coupling = energy * scale * scale * same[None] / NLAG
    return coupling[None]


def solution(mesh):
    return jax.shard_map(
        local,
        mesh=mesh,
        in_specs=(P("vert", "tm"), P(), P(), P(None, "vert")),
        out_specs=P("tm", None, "vert", None),
        check_vma=False,
    )
```

```python
from functools import partial
import math

import jax
import jax.numpy as jnp
from jax import lax
from jax.experimental import pallas as pl
from jax.experimental.pallas import tpu as pltpu
from jax.sharding import PartitionSpec as P

P1 = 100
P2 = 400
P3 = 1000
BANDS = 2
TAPS = 65
HALF = 32
LAG = 64
LAG_STEP = 1
NLAG = 129

EPSILON = 1e-05

ROW_PAD = 96
LAG_CHUNKS = 11
LAG_PAD = 132
VERT_MINOR = 4


def extended_2(cells, sides, width):
    for axis, dim in sides:
        count = lax.axis_size(axis)
        ends = count - 1
        head = lax.slice_in_dim(cells, 0, width, axis=dim)
        tail = lax.slice_in_dim(cells, cells.shape[dim] - width, cells.shape[dim], axis=dim)
        cells = jnp.concatenate(
            [
                lax.ppermute(tail, axis, [(i, (i + 1) % count) for i in range(ends)]),
                cells,
                lax.ppermute(head, axis, [((i + 1) % count, i) for i in range(ends)]),
            ],
            axis=dim,
        )
    return cells


def toeplitz_band(taps, n_out, n_in):
    period = jnp.concatenate([taps, jnp.zeros((n_in + 1 - taps.shape[0],), taps.dtype)])
    return jnp.tile(period, n_out)[: n_out * n_in].reshape(n_out, n_in)


def resolution_of(parcel):
    first = (parcel >= P1).astype(jnp.int32)
    second = (parcel >= P1 + P2).astype(jnp.int32)
    third = (parcel >= P1 + P2 + P3).astype(jnp.int32)
    return first + second + third


def centered_rows(extended, length):
    level_mean = jnp.mean(extended[:, :, LAG : LAG + length], axis=2, keepdims=True)
    centered = (extended - level_mean).astype(jnp.bfloat16)
    middle = centered[:, :, LAG : LAG + length]
    middle_wide = middle.astype(jnp.float32)
    spread = lax.rsqrt(jnp.mean(middle_wide * middle_wide, axis=2) + EPSILON)
    return (centered, middle, spread)


def mesh_peers(nx, nz):
    me = lax.axis_index("vert")
    tm = lax.axis_index("tm")
    mx, mz = me // nz, me % nz
    return me, tm, mx, mz


def greet(mx, mz, tm, nx, nz):
    barrier = pltpu.get_barrier_semaphore()
    for k in range(1, nx):
        pl.semaphore_signal(
            barrier, inc=1, device_id=(lax.rem(mx + k, nx) * nz + mz, tm),
            device_id_type=pl.DeviceIdType.MESH,
        )
    for k in range(1, nz):
        pl.semaphore_signal(
            barrier, inc=1, device_id=(mx * nz + lax.rem(mz + k, nz), tm),
            device_id_type=pl.DeviceIdType.MESH,
        )
    pl.semaphore_wait(barrier, nx + nz - 2)


def reduce_kernel(nx, nz, x_ref, out_ref, recv_a, part, recv_b, a_send, a_recv, b_send, b_recv):
    me, tm, mx, mz = mesh_peers(nx, nz)
    greet(mx, mz, tm, nx, nz)
    copies = []
    for k in range(1, nx):
        px = lax.rem(mx + k, nx)
        copy = pltpu.make_async_remote_copy(
            src_ref=x_ref.at[pl.ds(px * nz, nz)], dst_ref=recv_a.at[k - 1],
            send_sem=a_send.at[k - 1], recv_sem=a_recv.at[k - 1],
            device_id=(px * nz + mz, tm), device_id_type=pl.DeviceIdType.MESH,
        )
        copy.start()
        copies.append(copy)
    for copy in copies:
        copy.wait()
    acc = x_ref[pl.ds(mx * nz, nz)]
    for k in range(1, nx):
        acc = acc + recv_a[k - 1]
    part[...] = acc
    copies = []
    for k in range(1, nz):
        pz = lax.rem(mz + k, nz)
        copy = pltpu.make_async_remote_copy(
            src_ref=part.at[pz], dst_ref=recv_b.at[k - 1],
            send_sem=b_send.at[k - 1], recv_sem=b_recv.at[k - 1],
            device_id=(mx * nz + pz, tm), device_id_type=pl.DeviceIdType.MESH,
        )
        copy.start()
        copies.append(copy)
    for copy in copies:
        copy.wait()
    total = part[mz]
    for k in range(1, nz):
        total = total + recv_b[k - 1]
    out_ref[...] = total


def reduce_to_owner(x, nx, nz):
    n, rows, w = x.shape
    return pl.pallas_call(
        partial(reduce_kernel, nx, nz),
        out_shape=jax.ShapeDtypeStruct((rows, w), x.dtype),
        in_specs=[pl.BlockSpec(memory_space=pltpu.VMEM)],
        out_specs=pl.BlockSpec(memory_space=pltpu.VMEM),
        scratch_shapes=[
            pltpu.VMEM((nx - 1, nz, rows, w), x.dtype),
            pltpu.VMEM((nz, rows, w), x.dtype),
            pltpu.VMEM((nz - 1, rows, w), x.dtype),
            pltpu.SemaphoreType.DMA((nx - 1,)),
            pltpu.SemaphoreType.DMA((nx - 1,)),
            pltpu.SemaphoreType.DMA((nz - 1,)),
            pltpu.SemaphoreType.DMA((nz - 1,)),
        ],
        compiler_params=pltpu.CompilerParams(collective_id=0, has_side_effects=True),
    )(x)


def fill_lags(mid_ref, lhs_ref, band):
    rows = mid_ref.shape[1]
    base = mid_ref[band].astype(jnp.float32)
    for q in range(NLAG):
        lhs_ref[band, q * rows : (q + 1) * rows, :] = pltpu.roll(base, q, 1).astype(lhs_ref.dtype)
    lhs_ref[band, NLAG * rows :, :] = jnp.zeros(
        ((LAG_PAD - NLAG) * rows, lhs_ref.shape[2]), lhs_ref.dtype
    )


def fold_group(g, group, lhs_ref, gath, out_ref, sums_ref, t_dev):
    rows = out_ref.shape[1]
    step = LAG_PAD // LAG_CHUNKS
    first = pl.multiple_of(g * group, 128)
    for band in range(out_ref.shape[0]):
        block = gath[band, pl.ds(first, group), :].astype(jnp.float32)
        rhs_wide = block.T
        rhs = rhs_wide.astype(jnp.bfloat16)
        middle = rhs_wide[LAG : LAG + t_dev, :]
        sums_ref[band, :, pl.ds(first, group)] = jnp.sum(middle * middle, axis=0, keepdims=True)
        acc = jnp.zeros((rows, group), jnp.float32)
        for h in range(LAG_CHUNKS):
            lhs = lhs_ref[band, h * step * rows : (h + 1) * step * rows, :]
            r = jnp.dot(lhs, rhs, preferred_element_type=jnp.float32)
            acc = acc + (r * r).reshape(step, rows, group).sum(axis=0)
        out_ref[band, :, pl.ds(first, group)] = acc


def gather_fold_kernel(nx, nz, t_dev, own_ref, mid_ref, out_ref, sums_ref, gath, lhs_ref,
                       a_send, a_recv, b_send, b_recv, local_sem):
    me, tm, mx, mz = mesh_peers(nx, nz)
    rows = own_ref.shape[1]
    group = nz * rows
    greet(mx, mz, tm, nx, nz)
    mine = gath.at[:, pl.ds(me * rows, rows), :]
    own = pltpu.make_async_copy(own_ref, mine, local_sem)
    own.start()
    copies = []
    for k in range(1, nz):
        copy = pltpu.make_async_remote_copy(
            src_ref=own_ref, dst_ref=mine,
            send_sem=a_send.at[k - 1], recv_sem=a_recv.at[k - 1],
            device_id=(mx * nz + lax.rem(mz + k, nz), tm), device_id_type=pl.DeviceIdType.MESH,
        )
        copy.start()
        copies.append(copy)
    for band in range(mid_ref.shape[0]):
        fill_lags(mid_ref, lhs_ref, band)
    own.wait()
    for copy in copies:
        copy.wait()
    ours = gath.at[:, pl.ds(mx * group, group), :]
    copies = []
    for k in range(1, nx):
        copy = pltpu.make_async_remote_copy(
            src_ref=ours, dst_ref=ours,
            send_sem=b_send.at[k - 1], recv_sem=b_recv.at[k - 1],
            device_id=(lax.rem(mx + k, nx) * nz + mz, tm), device_id_type=pl.DeviceIdType.MESH,
        )
        copy.start()
        copies.append(copy)
    fold_group(mx, group, lhs_ref, gath, out_ref, sums_ref, t_dev)

    def landed(k, carry):
        pltpu.make_async_remote_copy(
            src_ref=ours, dst_ref=ours,
            send_sem=b_send.at[k - 1], recv_sem=b_recv.at[k - 1],
            device_id=(lax.rem(mx + k, nx) * nz + mz, tm), device_id_type=pl.DeviceIdType.MESH,
        ).wait_recv()
        fold_group(lax.rem(mx + nx - k, nx), group, lhs_ref, gath, out_ref, sums_ref, t_dev)
        return carry

    lax.fori_loop(1, nx, landed, 0)
    for copy in copies:
        copy.wait_send()


def gather_fold(own, mid, nx, nz, t_dev):
    bands, rows, width = own.shape
    cols = nx * nz * rows
    flops = 2 * bands * LAG_PAD * rows * width * cols
    return pl.pallas_call(
        partial(gather_fold_kernel, nx, nz, t_dev),
        out_shape=(
            jax.ShapeDtypeStruct((bands, rows, cols), jnp.float32),
            jax.ShapeDtypeStruct((bands, 1, cols), jnp.float32),
        ),
        in_specs=[pl.BlockSpec(memory_space=pltpu.VMEM)] * 2,
        out_specs=(pl.BlockSpec(memory_space=pltpu.VMEM),) * 2,
        scratch_shapes=[
            pltpu.VMEM((bands, cols, width), own.dtype),
            pltpu.VMEM((bands, LAG_PAD * rows, width), jnp.bfloat16),
            pltpu.SemaphoreType.DMA((nz - 1,)),
            pltpu.SemaphoreType.DMA((nz - 1,)),
            pltpu.SemaphoreType.DMA((nx - 1,)),
            pltpu.SemaphoreType.DMA((nx - 1,)),
            pltpu.SemaphoreType.DMA(()),
        ],
        compiler_params=pltpu.CompilerParams(
            collective_id=1, has_side_effects=True, vmem_limit_bytes=48 * 1024 * 1024
        ),
        cost_estimate=pl.CostEstimate(
            flops=flops, bytes_accessed=2 * (own.size + mid.size) + 4 * bands * (rows + 1) * cols,
            transcendentals=0,
        ),
    )(own, mid)


def local(source, band_taps, smooth_taps, parcel_ids):
    vert_dev, t_dev = source.shape
    owners = lax.axis_size("vert")
    total_par = (P1 + P2 + P3 + owners - 1) // owners * owners
    par_dev = total_par // owners
    n_mid = t_dev + 2 * HALF
    n_in = t_dev + 4 * HALF
    first_rows = jax.vmap(partial(toeplitz_band, n_out=n_mid, n_in=n_in))(
        band_taps.reshape(2 * BANDS, TAPS)
    )
    first_mat = first_rows.transpose(2, 0, 1).reshape(n_in, 2 * BANDS * n_mid)
    second_rows = jax.vmap(partial(toeplitz_band, n_out=t_dev, n_in=n_mid))(smooth_taps)
    second_mat = second_rows.transpose(0, 2, 1)
    widened = extended_2(source, (("tm", 1),), 2 * HALF)
    block_rows = math.gcd(vert_dev, 128)

    def filter_block(block):
        wave = jnp.dot(block, first_mat, preferred_element_type=jnp.float32).reshape(
            block_rows, 2, BANDS, n_mid
        )
        power = (wave[:, 0] * wave[:, 0] + wave[:, 1] * wave[:, 1]).astype(jnp.bfloat16)
        return jnp.einsum(
            "vbu,but->vbt", power, second_mat, preferred_element_type=jnp.float32
        ).astype(jnp.bfloat16)

    envelope = lax.map(filter_block, widened.reshape(vert_dev // block_rows, block_rows, n_in))
    flat_env = envelope.reshape(vert_dev, BANDS * t_dev)
    offsets = jnp.array([0, P1, P1 + P2], dtype=jnp.int32)
    global_ids = parcel_ids + offsets[:, None]
    owner_start = lax.axis_index("vert") * par_dev

    wanted = lax.iota(jnp.int32, total_par)
    hits = jnp.sum(
        (global_ids[:, None, :] == wanted[None, :, None]).astype(jnp.bfloat16), axis=0
    )
    pooled = jnp.dot(hits, flat_env, preferred_element_type=jnp.float32)
    nx = owners // VERT_MINOR
    own_sums = reduce_to_owner(pooled.reshape(owners, par_dev, BANDS * t_dev), nx, VERT_MINOR)
    own_env = own_sums.reshape(par_dev, BANDS, t_dev)
    own_ext = extended_2(own_env, (("tm", 2),), LAG)
    centered, own_middle, own_spread = centered_rows(own_ext, t_dev)

    own = jnp.pad(centered.transpose(1, 0, 2), ((0, 0), (0, ROW_PAD - par_dev), (0, 0)))
    mid = jnp.pad(
        own_middle.transpose(1, 0, 2), ((0, 0), (0, ROW_PAD - par_dev), (0, t_dev))
    )
    padded_energy, sums = gather_fold(own, mid, nx, VERT_MINOR, t_dev)
    energy = padded_energy.reshape(BANDS, ROW_PAD, owners, ROW_PAD)[:, :par_dev, :, :par_dev]
    energy = energy.reshape(BANDS, par_dev, total_par)
    vis_sums = sums.reshape(BANDS, owners, ROW_PAD)[:, :, :par_dev].reshape(BANDS, total_par)
    vis_spread = lax.rsqrt(vis_sums / t_dev + EPSILON)

    scale = own_spread.T[:, :, None] * vis_spread[:, None, :] / t_dev
    own_level = resolution_of(owner_start + lax.iota(jnp.int32, par_dev))
    all_level = resolution_of(lax.iota(jnp.int32, total_par))
    same = ((own_level[:, None] == all_level[None, :]) & (own_level[:, None] < 3)).astype(
        jnp.float32
    )
    coupling = energy * scale * scale * same[None] / NLAG
    return coupling[None]


def solution(mesh):
    return jax.shard_map(
        local,
        mesh=mesh,
        in_specs=(P("vert", "tm"), P(), P(), P(None, "vert")),
        out_specs=P("tm", None, "vert", None),
        check_vma=False,
    )
```

```python
from functools import partial
import math

import jax
import jax.numpy as jnp
from jax import lax
from jax.experimental import pallas as pl
from jax.experimental.pallas import tpu as pltpu
from jax.sharding import PartitionSpec as P

P1 = 100
P2 = 400
P3 = 1000
BANDS = 2
TAPS = 65
HALF = 32
LAG = 64
LAG_STEP = 1
NLAG = 129

EPSILON = 1e-05

ROW_PAD = 96
LAG_CHUNKS = 11
LAG_PAD = 132
VERT_MINOR = 4


def extended_2(cells, sides, width):
    for axis, dim in sides:
        count = lax.axis_size(axis)
        ends = count - 1
        head = lax.slice_in_dim(cells, 0, width, axis=dim)
        tail = lax.slice_in_dim(cells, cells.shape[dim] - width, cells.shape[dim], axis=dim)
        cells = jnp.concatenate(
            [
                lax.ppermute(tail, axis, [(i, (i + 1) % count) for i in range(ends)]),
                cells,
                lax.ppermute(head, axis, [((i + 1) % count, i) for i in range(ends)]),
            ],
            axis=dim,
        )
    return cells


def toeplitz_band(taps, n_out, n_in):
    period = jnp.concatenate([taps, jnp.zeros((n_in + 1 - taps.shape[0],), taps.dtype)])
    return jnp.tile(period, n_out)[: n_out * n_in].reshape(n_out, n_in)


def resolution_of(parcel):
    first = (parcel >= P1).astype(jnp.int32)
    second = (parcel >= P1 + P2).astype(jnp.int32)
    third = (parcel >= P1 + P2 + P3).astype(jnp.int32)
    return first + second + third


def centered_rows(extended, length):
    level_mean = jnp.mean(extended[:, :, LAG : LAG + length], axis=2, keepdims=True)
    centered = (extended - level_mean).astype(jnp.bfloat16)
    middle = centered[:, :, LAG : LAG + length]
    middle_wide = middle.astype(jnp.float32)
    spread = lax.rsqrt(jnp.mean(middle_wide * middle_wide, axis=2) + EPSILON)
    return (centered, middle, spread)


def mesh_peers(nx, nz):
    me = lax.axis_index("vert")
    tm = lax.axis_index("tm")
    mx, mz = me // nz, me % nz
    return me, tm, mx, mz


def greet(mx, mz, tm, nx, nz):
    barrier = pltpu.get_barrier_semaphore()
    for k in range(1, nx):
        pl.semaphore_signal(
            barrier, inc=1, device_id=(lax.rem(mx + k, nx) * nz + mz, tm),
            device_id_type=pl.DeviceIdType.MESH,
        )
    for k in range(1, nz):
        pl.semaphore_signal(
            barrier, inc=1, device_id=(mx * nz + lax.rem(mz + k, nz), tm),
            device_id_type=pl.DeviceIdType.MESH,
        )
    pl.semaphore_wait(barrier, nx + nz - 2)


def reduce_kernel(nx, nz, x_ref, out_ref, recv_a, part, recv_b, a_send, a_recv, b_send, b_recv):
    me, tm, mx, mz = mesh_peers(nx, nz)
    greet(mx, mz, tm, nx, nz)
    copies = []
    for k in range(1, nx):
        px = lax.rem(mx + k, nx)
        copy = pltpu.make_async_remote_copy(
            src_ref=x_ref.at[pl.ds(px * nz, nz)], dst_ref=recv_a.at[k - 1],
            send_sem=a_send.at[k - 1], recv_sem=a_recv.at[k - 1],
            device_id=(px * nz + mz, tm), device_id_type=pl.DeviceIdType.MESH,
        )
        copy.start()
        copies.append(copy)
    for copy in copies:
        copy.wait()
    acc = x_ref[pl.ds(mx * nz, nz)]
    for k in range(1, nx):
        acc = acc + recv_a[k - 1]
    part[...] = acc
    copies = []
    for k in range(1, nz):
        pz = lax.rem(mz + k, nz)
        copy = pltpu.make_async_remote_copy(
            src_ref=part.at[pz], dst_ref=recv_b.at[k - 1],
            send_sem=b_send.at[k - 1], recv_sem=b_recv.at[k - 1],
            device_id=(mx * nz + pz, tm), device_id_type=pl.DeviceIdType.MESH,
        )
        copy.start()
        copies.append(copy)
    for copy in copies:
        copy.wait()
    total = part[mz]
    for k in range(1, nz):
        total = total + recv_b[k - 1]
    out_ref[...] = total


def reduce_to_owner(x, nx, nz):
    n, rows, w = x.shape
    return pl.pallas_call(
        partial(reduce_kernel, nx, nz),
        out_shape=jax.ShapeDtypeStruct((rows, w), x.dtype),
        in_specs=[pl.BlockSpec(memory_space=pltpu.VMEM)],
        out_specs=pl.BlockSpec(memory_space=pltpu.VMEM),
        scratch_shapes=[
            pltpu.VMEM((nx - 1, nz, rows, w), x.dtype),
            pltpu.VMEM((nz, rows, w), x.dtype),
            pltpu.VMEM((nz - 1, rows, w), x.dtype),
            pltpu.SemaphoreType.DMA((nx - 1,)),
            pltpu.SemaphoreType.DMA((nx - 1,)),
            pltpu.SemaphoreType.DMA((nz - 1,)),
            pltpu.SemaphoreType.DMA((nz - 1,)),
        ],
        compiler_params=pltpu.CompilerParams(collective_id=0, has_side_effects=True),
    )(x)


def fill_lags(mid_ref, lhs_ref, band):
    rows = mid_ref.shape[1]
    base = mid_ref[band].astype(jnp.float32)
    for q in range(NLAG):
        lhs_ref[band, q * rows : (q + 1) * rows, :] = pltpu.roll(base, q, 1).astype(lhs_ref.dtype)
    lhs_ref[band, NLAG * rows :, :] = jnp.zeros(
        ((LAG_PAD - NLAG) * rows, lhs_ref.shape[2]), lhs_ref.dtype
    )


def fold_group(g, group, lhs_ref, gath, out_ref, sums_ref, t_dev):
    rows = out_ref.shape[1]
    step = LAG_PAD // LAG_CHUNKS
    first = pl.multiple_of(g * group, 128)

    def one_band(band, carry):
        block = gath[band, pl.ds(first, group), :].astype(jnp.float32)
        rhs_wide = block.T
        rhs = rhs_wide.astype(jnp.bfloat16)
        middle = rhs_wide[LAG : LAG + t_dev, :]
        sums_ref[band, :, pl.ds(first, group)] = jnp.sum(middle * middle, axis=0, keepdims=True)
        acc = jnp.zeros((rows, group), jnp.float32)
        for h in range(LAG_CHUNKS):
            lhs = lhs_ref[band, h * step * rows : (h + 1) * step * rows, :]
            r = jnp.dot(lhs, rhs, preferred_element_type=jnp.float32)
            acc = acc + (r * r).reshape(step, rows, group).sum(axis=0)
        out_ref[band, :, pl.ds(first, group)] = acc
        return carry

    lax.fori_loop(0, out_ref.shape[0], one_band, 0)


def gather_fold_kernel(nx, nz, t_dev, own_ref, mid_ref, out_ref, sums_ref, gath, lhs_ref,
                       a_send, a_recv, b_send, b_recv, local_sem):
    me, tm, mx, mz = mesh_peers(nx, nz)
    rows = own_ref.shape[1]
    group = nz * rows
    greet(mx, mz, tm, nx, nz)
    mine = gath.at[:, pl.ds(me * rows, rows), :]
    own = pltpu.make_async_copy(own_ref, mine, local_sem)
    own.start()
    copies = []
    for k in range(1, nz):
        copy = pltpu.make_async_remote_copy(
            src_ref=own_ref, dst_ref=mine,
            send_sem=a_send.at[k - 1], recv_sem=a_recv.at[k - 1],
            device_id=(mx * nz + lax.rem(mz + k, nz), tm), device_id_type=pl.DeviceIdType.MESH,
        )
        copy.start()
        copies.append(copy)
    for band in range(mid_ref.shape[0]):
        fill_lags(mid_ref, lhs_ref, band)
    own.wait()
    for copy in copies:
        copy.wait()
    left, right = lax.rem(mx + nx - 1, nx), lax.rem(mx + 1, nx)
    half = group // 2

    def ring_copy(start, size, peer, slot):
        rows_at = gath.at[:, pl.ds(start, size), :]
        return pltpu.make_async_remote_copy(
            src_ref=rows_at, dst_ref=rows_at,
            send_sem=b_send.at[slot], recv_sem=b_recv.at[slot],
            device_id=(peer * nz + mz, tm), device_id_type=pl.DeviceIdType.MESH,
        )

    near = [ring_copy(mx * group, group, right, 0), ring_copy(mx * group, group, left, 1)]
    for copy in near:
        copy.start()
    fold_group(mx, group, lhs_ref, gath, out_ref, sums_ref, t_dev)
    for copy in near:
        copy.wait_recv()
    far = [ring_copy(left * group, half, right, 2), ring_copy(right * group + half, half, left, 3)]
    for copy in far:
        copy.start()
    fold_group(left, group, lhs_ref, gath, out_ref, sums_ref, t_dev)
    fold_group(right, group, lhs_ref, gath, out_ref, sums_ref, t_dev)
    for copy in far:
        copy.wait_recv()
    fold_group(lax.rem(mx + 2, nx), group, lhs_ref, gath, out_ref, sums_ref, t_dev)
    for copy in near + far:
        copy.wait_send()


def gather_fold(own, mid, nx, nz, t_dev):
    assert nx == 4
    bands, rows, width = own.shape
    cols = nx * nz * rows
    flops = 2 * bands * LAG_PAD * rows * width * cols
    return pl.pallas_call(
        partial(gather_fold_kernel, nx, nz, t_dev),
        out_shape=(
            jax.ShapeDtypeStruct((bands, rows, cols), jnp.float32),
            jax.ShapeDtypeStruct((bands, 1, cols), jnp.float32),
        ),
        in_specs=[pl.BlockSpec(memory_space=pltpu.VMEM)] * 2,
        out_specs=(pl.BlockSpec(memory_space=pltpu.VMEM),) * 2,
        scratch_shapes=[
            pltpu.VMEM((bands, cols, width), own.dtype),
            pltpu.VMEM((bands, LAG_PAD * rows, width), jnp.bfloat16),
            pltpu.SemaphoreType.DMA((nz - 1,)),
            pltpu.SemaphoreType.DMA((nz - 1,)),
            pltpu.SemaphoreType.DMA((4,)),
            pltpu.SemaphoreType.DMA((4,)),
            pltpu.SemaphoreType.DMA(()),
        ],
        compiler_params=pltpu.CompilerParams(
            collective_id=1, has_side_effects=True, vmem_limit_bytes=48 * 1024 * 1024
        ),
        cost_estimate=pl.CostEstimate(
            flops=flops, bytes_accessed=2 * (own.size + mid.size) + 4 * bands * (rows + 1) * cols,
            transcendentals=0,
        ),
    )(own, mid)


def local(source, band_taps, smooth_taps, parcel_ids):
    vert_dev, t_dev = source.shape
    owners = lax.axis_size("vert")
    total_par = (P1 + P2 + P3 + owners - 1) // owners * owners
    par_dev = total_par // owners
    n_mid = t_dev + 2 * HALF
    n_in = t_dev + 4 * HALF
    first_rows = jax.vmap(partial(toeplitz_band, n_out=n_mid, n_in=n_in))(
        band_taps.reshape(2 * BANDS, TAPS)
    )
    first_mat = first_rows.transpose(2, 0, 1).reshape(n_in, 2 * BANDS * n_mid)
    second_rows = jax.vmap(partial(toeplitz_band, n_out=t_dev, n_in=n_mid))(smooth_taps)
    second_mat = second_rows.transpose(0, 2, 1)
    widened = extended_2(source, (("tm", 1),), 2 * HALF)
    block_rows = math.gcd(vert_dev, 128)

    def filter_block(block):
        wave = jnp.dot(block, first_mat, preferred_element_type=jnp.float32).reshape(
            block_rows, 2, BANDS, n_mid
        )
        power = (wave[:, 0] * wave[:, 0] + wave[:, 1] * wave[:, 1]).astype(jnp.bfloat16)
        return jnp.einsum(
            "vbu,but->vbt", power, second_mat, preferred_element_type=jnp.float32
        ).astype(jnp.bfloat16)

    envelope = lax.map(filter_block, widened.reshape(vert_dev // block_rows, block_rows, n_in))
    flat_env = envelope.reshape(vert_dev, BANDS * t_dev)
    offsets = jnp.array([0, P1, P1 + P2], dtype=jnp.int32)
    global_ids = parcel_ids + offsets[:, None]
    owner_start = lax.axis_index("vert") * par_dev

    wanted = lax.iota(jnp.int32, total_par)
    hits = jnp.sum(
        (global_ids[:, None, :] == wanted[None, :, None]).astype(jnp.bfloat16), axis=0
    )
    pooled = jnp.dot(hits, flat_env, preferred_element_type=jnp.float32)
    nx = owners // VERT_MINOR
    own_sums = reduce_to_owner(pooled.reshape(owners, par_dev, BANDS * t_dev), nx, VERT_MINOR)
    own_env = own_sums.reshape(par_dev, BANDS, t_dev)
    own_ext = extended_2(own_env, (("tm", 2),), LAG)
    centered, own_middle, own_spread = centered_rows(own_ext, t_dev)

    own = jnp.pad(centered.transpose(1, 0, 2), ((0, 0), (0, ROW_PAD - par_dev), (0, 0)))
    mid = jnp.pad(
        own_middle.transpose(1, 0, 2), ((0, 0), (0, ROW_PAD - par_dev), (0, t_dev))
    )
    padded_energy, sums = gather_fold(own, mid, nx, VERT_MINOR, t_dev)
    energy = padded_energy.reshape(BANDS, ROW_PAD, owners, ROW_PAD)[:, :par_dev, :, :par_dev]
    energy = energy.reshape(BANDS, par_dev, total_par)
    vis_sums = sums.reshape(BANDS, owners, ROW_PAD)[:, :, :par_dev].reshape(BANDS, total_par)
    vis_spread = lax.rsqrt(vis_sums / t_dev + EPSILON)

    scale = own_spread.T[:, :, None] * vis_spread[:, None, :] / t_dev
    own_level = resolution_of(owner_start + lax.iota(jnp.int32, par_dev))
    all_level = resolution_of(lax.iota(jnp.int32, total_par))
    same = ((own_level[:, None] == all_level[None, :]) & (own_level[:, None] < 3)).astype(
        jnp.float32
    )
    coupling = energy * scale * scale * same[None] / NLAG
    return coupling[None]


def solution(mesh):
    return jax.shard_map(
        local,
        mesh=mesh,
        in_specs=(P("vert", "tm"), P(), P(), P(None, "vert")),
        out_specs=P("tm", None, "vert", None),
        check_vma=False,
    )
```

```python
from functools import partial
import math

import jax
import jax.numpy as jnp
from jax import lax
from jax.experimental import pallas as pl
from jax.experimental.pallas import tpu as pltpu
from jax.sharding import PartitionSpec as P

P1 = 100
P2 = 400
P3 = 1000
BANDS = 2
TAPS = 65
HALF = 32
LAG = 64
LAG_STEP = 1
NLAG = 129

EPSILON = 1e-05

ROW_PAD = 96
LAG_CHUNKS = 11
LAG_PAD = 132
VERT_MINOR = 4


def extended_2(cells, sides, width):
    for axis, dim in sides:
        count = lax.axis_size(axis)
        ends = count - 1
        head = lax.slice_in_dim(cells, 0, width, axis=dim)
        tail = lax.slice_in_dim(cells, cells.shape[dim] - width, cells.shape[dim], axis=dim)
        cells = jnp.concatenate(
            [
                lax.ppermute(tail, axis, [(i, (i + 1) % count) for i in range(ends)]),
                cells,
                lax.ppermute(head, axis, [((i + 1) % count, i) for i in range(ends)]),
            ],
            axis=dim,
        )
    return cells


def toeplitz_band(taps, n_out, n_in):
    period = jnp.concatenate([taps, jnp.zeros((n_in + 1 - taps.shape[0],), taps.dtype)])
    return jnp.tile(period, n_out)[: n_out * n_in].reshape(n_out, n_in)


def resolution_of(parcel):
    first = (parcel >= P1).astype(jnp.int32)
    second = (parcel >= P1 + P2).astype(jnp.int32)
    third = (parcel >= P1 + P2 + P3).astype(jnp.int32)
    return first + second + third


def centered_rows(extended, length):
    level_mean = jnp.mean(extended[:, :, LAG : LAG + length], axis=2, keepdims=True)
    centered = (extended - level_mean).astype(jnp.bfloat16)
    middle = centered[:, :, LAG : LAG + length]
    middle_wide = middle.astype(jnp.float32)
    spread = lax.rsqrt(jnp.mean(middle_wide * middle_wide, axis=2) + EPSILON)
    return (centered, middle, spread)


def mesh_peers(nx, nz):
    me = lax.axis_index("vert")
    tm = lax.axis_index("tm")
    mx, mz = me // nz, me % nz
    return me, tm, mx, mz


def greet(mx, mz, tm, nx, nz):
    barrier = pltpu.get_barrier_semaphore()
    for k in range(1, nx):
        pl.semaphore_signal(
            barrier, inc=1, device_id=(lax.rem(mx + k, nx) * nz + mz, tm),
            device_id_type=pl.DeviceIdType.MESH,
        )
    for k in range(1, nz):
        pl.semaphore_signal(
            barrier, inc=1, device_id=(mx * nz + lax.rem(mz + k, nz), tm),
            device_id_type=pl.DeviceIdType.MESH,
        )
    pl.semaphore_wait(barrier, nx + nz - 2)


def reduce_kernel(nx, nz, x_ref, out_ref, recv_a, send_a, part, recv_b, a_send, a_recv, b_send, b_recv):
    me, tm, mx, mz = mesh_peers(nx, nz)
    greet(mx, mz, tm, nx, nz)
    hz = nz // 2
    peers = (lax.rem(mx + 1, nx), lax.rem(mx + nx - 1, nx))

    def owners_of(g, d):
        return pl.ds(g * nz + d * hz, hz)

    for s in range(1, nx):
        copies = []
        for d in range(2):
            g = lax.rem(mx + (s if d else nx * s - s), nx)
            if s == 1:
                src = x_ref.at[owners_of(g, d)]
            else:
                send_a[d, s - 2] = recv_a[d, s - 2] + x_ref[owners_of(g, d)]
                src = send_a.at[d, s - 2]
            copy = pltpu.make_async_remote_copy(
                src_ref=src, dst_ref=recv_a.at[d, s - 1],
                send_sem=a_send.at[d, s - 1], recv_sem=a_recv.at[d, s - 1],
                device_id=(peers[d] * nz + mz, tm), device_id_type=pl.DeviceIdType.MESH,
            )
            copy.start()
            copies.append(copy)
        for copy in copies:
            copy.wait()
    for d in range(2):
        part[d * hz : (d + 1) * hz] = recv_a[d, nx - 2] + x_ref[owners_of(mx, d)]
    copies = []
    for k in range(1, nz):
        pz = lax.rem(mz + k, nz)
        copy = pltpu.make_async_remote_copy(
            src_ref=part.at[pz], dst_ref=recv_b.at[k - 1],
            send_sem=b_send.at[k - 1], recv_sem=b_recv.at[k - 1],
            device_id=(mx * nz + pz, tm), device_id_type=pl.DeviceIdType.MESH,
        )
        copy.start()
        copies.append(copy)
    for copy in copies:
        copy.wait()
    total = part[mz]
    for k in range(1, nz):
        total = total + recv_b[k - 1]
    out_ref[...] = total


def reduce_to_owner(x, nx, nz):
    n, rows, w = x.shape
    hz = nz // 2
    return pl.pallas_call(
        partial(reduce_kernel, nx, nz),
        out_shape=jax.ShapeDtypeStruct((rows, w), x.dtype),
        in_specs=[pl.BlockSpec(memory_space=pltpu.VMEM)],
        out_specs=pl.BlockSpec(memory_space=pltpu.VMEM),
        scratch_shapes=[
            pltpu.VMEM((2, nx - 1, hz, rows, w), x.dtype),
            pltpu.VMEM((2, nx - 2, hz, rows, w), x.dtype),
            pltpu.VMEM((nz, rows, w), x.dtype),
            pltpu.VMEM((nz - 1, rows, w), x.dtype),
            pltpu.SemaphoreType.DMA((2, nx - 1)),
            pltpu.SemaphoreType.DMA((2, nx - 1)),
            pltpu.SemaphoreType.DMA((nz - 1,)),
            pltpu.SemaphoreType.DMA((nz - 1,)),
        ],
        compiler_params=pltpu.CompilerParams(collective_id=0, has_side_effects=True),
    )(x)


def fill_lags(mid_ref, lhs_ref, band):
    rows = mid_ref.shape[1]
    base = mid_ref[band].astype(jnp.float32)
    for q in range(NLAG):
        lhs_ref[band, q * rows : (q + 1) * rows, :] = pltpu.roll(base, q, 1).astype(lhs_ref.dtype)
    lhs_ref[band, NLAG * rows :, :] = jnp.zeros(
        ((LAG_PAD - NLAG) * rows, lhs_ref.shape[2]), lhs_ref.dtype
    )


def fold_group(g, group, lhs_ref, gath, out_ref, sums_ref, t_dev):
    rows = out_ref.shape[1]
    step = LAG_PAD // LAG_CHUNKS
    first = pl.multiple_of(g * group, 128)

    def one_band(band, carry):
        block = gath[band, pl.ds(first, group), :].astype(jnp.float32)
        rhs_wide = block.T
        rhs = rhs_wide.astype(jnp.bfloat16)
        middle = rhs_wide[LAG : LAG + t_dev, :]
        sums_ref[band, :, pl.ds(first, group)] = jnp.sum(middle * middle, axis=0, keepdims=True)
        acc = jnp.zeros((rows, group), jnp.float32)
        for h in range(LAG_CHUNKS):
            lhs = lhs_ref[band, h * step * rows : (h + 1) * step * rows, :]
            r = jnp.dot(lhs, rhs, preferred_element_type=jnp.float32)
            acc = acc + (r * r).reshape(step, rows, group).sum(axis=0)
        out_ref[band, :, pl.ds(first, group)] = acc
        return carry

    lax.fori_loop(0, out_ref.shape[0], one_band, 0)


def gather_fold_kernel(nx, nz, t_dev, own_ref, mid_ref, out_ref, sums_ref, gath, lhs_ref,
                       a_send, a_recv, b_send, b_recv, local_sem):
    me, tm, mx, mz = mesh_peers(nx, nz)
    rows = own_ref.shape[1]
    group = nz * rows
    greet(mx, mz, tm, nx, nz)
    mine = gath.at[:, pl.ds(me * rows, rows), :]
    own = pltpu.make_async_copy(own_ref, mine, local_sem)
    own.start()
    copies = []
    for k in range(1, nz):
        copy = pltpu.make_async_remote_copy(
            src_ref=own_ref, dst_ref=mine,
            send_sem=a_send.at[k - 1], recv_sem=a_recv.at[k - 1],
            device_id=(mx * nz + lax.rem(mz + k, nz), tm), device_id_type=pl.DeviceIdType.MESH,
        )
        copy.start()
        copies.append(copy)
    for band in range(mid_ref.shape[0]):
        fill_lags(mid_ref, lhs_ref, band)
    own.wait()
    for copy in copies:
        copy.wait()
    left, right = lax.rem(mx + nx - 1, nx), lax.rem(mx + 1, nx)
    half = group // 2

    def ring_copy(start, size, peer, slot):
        rows_at = gath.at[:, pl.ds(start, size), :]
        return pltpu.make_async_remote_copy(
            src_ref=rows_at, dst_ref=rows_at,
            send_sem=b_send.at[slot], recv_sem=b_recv.at[slot],
            device_id=(peer * nz + mz, tm), device_id_type=pl.DeviceIdType.MESH,
        )

    near = [ring_copy(mx * group, group, right, 0), ring_copy(mx * group, group, left, 1)]
    for copy in near:
        copy.start()
    fold_group(mx, group, lhs_ref, gath, out_ref, sums_ref, t_dev)
    for copy in near:
        copy.wait_recv()
    far = [ring_copy(left * group, half, right, 2), ring_copy(right * group + half, half, left, 3)]
    for copy in far:
        copy.start()
    fold_group(left, group, lhs_ref, gath, out_ref, sums_ref, t_dev)
    fold_group(right, group, lhs_ref, gath, out_ref, sums_ref, t_dev)
    for copy in far:
        copy.wait_recv()
    fold_group(lax.rem(mx + 2, nx), group, lhs_ref, gath, out_ref, sums_ref, t_dev)
    for copy in near + far:
        copy.wait_send()


def gather_fold(own, mid, nx, nz, t_dev):
    assert nx == 4
    bands, rows, width = own.shape
    cols = nx * nz * rows
    flops = 2 * bands * LAG_PAD * rows * width * cols
    return pl.pallas_call(
        partial(gather_fold_kernel, nx, nz, t_dev),
        out_shape=(
            jax.ShapeDtypeStruct((bands, rows, cols), jnp.float32),
            jax.ShapeDtypeStruct((bands, 1, cols), jnp.float32),
        ),
        in_specs=[pl.BlockSpec(memory_space=pltpu.VMEM)] * 2,
        out_specs=(pl.BlockSpec(memory_space=pltpu.VMEM),) * 2,
        scratch_shapes=[
            pltpu.VMEM((bands, cols, width), own.dtype),
            pltpu.VMEM((bands, LAG_PAD * rows, width), jnp.bfloat16),
            pltpu.SemaphoreType.DMA((nz - 1,)),
            pltpu.SemaphoreType.DMA((nz - 1,)),
            pltpu.SemaphoreType.DMA((4,)),
            pltpu.SemaphoreType.DMA((4,)),
            pltpu.SemaphoreType.DMA(()),
        ],
        compiler_params=pltpu.CompilerParams(
            collective_id=1, has_side_effects=True, vmem_limit_bytes=48 * 1024 * 1024
        ),
        cost_estimate=pl.CostEstimate(
            flops=flops, bytes_accessed=2 * (own.size + mid.size) + 4 * bands * (rows + 1) * cols,
            transcendentals=0,
        ),
    )(own, mid)


def local(source, band_taps, smooth_taps, parcel_ids):
    vert_dev, t_dev = source.shape
    owners = lax.axis_size("vert")
    total_par = (P1 + P2 + P3 + owners - 1) // owners * owners
    par_dev = total_par // owners
    n_mid = t_dev + 2 * HALF
    n_in = t_dev + 4 * HALF
    first_rows = jax.vmap(partial(toeplitz_band, n_out=n_mid, n_in=n_in))(
        band_taps.reshape(2 * BANDS, TAPS)
    )
    first_mat = first_rows.transpose(2, 0, 1).reshape(n_in, 2 * BANDS * n_mid)
    second_rows = jax.vmap(partial(toeplitz_band, n_out=t_dev, n_in=n_mid))(smooth_taps)
    second_mat = second_rows.transpose(0, 2, 1)
    widened = extended_2(source, (("tm", 1),), 2 * HALF)
    block_rows = math.gcd(vert_dev, 128)

    def filter_block(block):
        wave = jnp.dot(block, first_mat, preferred_element_type=jnp.float32).reshape(
            block_rows, 2, BANDS, n_mid
        )
        power = (wave[:, 0] * wave[:, 0] + wave[:, 1] * wave[:, 1]).astype(jnp.bfloat16)
        return jnp.einsum(
            "vbu,but->vbt", power, second_mat, preferred_element_type=jnp.float32
        ).astype(jnp.bfloat16)

    envelope = lax.map(filter_block, widened.reshape(vert_dev // block_rows, block_rows, n_in))
    flat_env = envelope.reshape(vert_dev, BANDS * t_dev)
    offsets = jnp.array([0, P1, P1 + P2], dtype=jnp.int32)
    global_ids = parcel_ids + offsets[:, None]
    owner_start = lax.axis_index("vert") * par_dev

    wanted = lax.iota(jnp.int32, total_par)
    hits = jnp.sum(
        (global_ids[:, None, :] == wanted[None, :, None]).astype(jnp.bfloat16), axis=0
    )
    pooled = jnp.dot(hits, flat_env, preferred_element_type=jnp.float32)
    nx = owners // VERT_MINOR
    own_sums = reduce_to_owner(pooled.reshape(owners, par_dev, BANDS * t_dev), nx, VERT_MINOR)
    own_env = own_sums.reshape(par_dev, BANDS, t_dev)
    own_ext = extended_2(own_env, (("tm", 2),), LAG)
    centered, own_middle, own_spread = centered_rows(own_ext, t_dev)

    own = jnp.pad(centered.transpose(1, 0, 2), ((0, 0), (0, ROW_PAD - par_dev), (0, 0)))
    mid = jnp.pad(
        own_middle.transpose(1, 0, 2), ((0, 0), (0, ROW_PAD - par_dev), (0, t_dev))
    )
    padded_energy, sums = gather_fold(own, mid, nx, VERT_MINOR, t_dev)
    energy = padded_energy.reshape(BANDS, ROW_PAD, owners, ROW_PAD)[:, :par_dev, :, :par_dev]
    energy = energy.reshape(BANDS, par_dev, total_par)
    vis_sums = sums.reshape(BANDS, owners, ROW_PAD)[:, :, :par_dev].reshape(BANDS, total_par)
    vis_spread = lax.rsqrt(vis_sums / t_dev + EPSILON)

    scale = own_spread.T[:, :, None] * vis_spread[:, None, :] / t_dev
    own_level = resolution_of(owner_start + lax.iota(jnp.int32, par_dev))
    all_level = resolution_of(lax.iota(jnp.int32, total_par))
    same = ((own_level[:, None] == all_level[None, :]) & (own_level[:, None] < 3)).astype(
        jnp.float32
    )
    coupling = energy * scale * scale * same[None] / NLAG
    return coupling[None]


def solution(mesh):
    return jax.shard_map(
        local,
        mesh=mesh,
        in_specs=(P("vert", "tm"), P(), P(), P(None, "vert")),
        out_specs=P("tm", None, "vert", None),
        check_vma=False,
    )
```

```python
from functools import partial
import math

import jax
import jax.numpy as jnp
from jax import lax
from jax.experimental import pallas as pl
from jax.experimental.pallas import tpu as pltpu
from jax.sharding import PartitionSpec as P

P1 = 100
P2 = 400
P3 = 1000
BANDS = 2
TAPS = 65
HALF = 32
LAG = 64
LAG_STEP = 1
NLAG = 129

EPSILON = 1e-05

ROW_PAD = 96
LAG_CHUNKS = 11
LAG_PAD = 132
VERT_MINOR = 4


def extended_2(cells, sides, width):
    for axis, dim in sides:
        count = lax.axis_size(axis)
        ends = count - 1
        head = lax.slice_in_dim(cells, 0, width, axis=dim)
        tail = lax.slice_in_dim(cells, cells.shape[dim] - width, cells.shape[dim], axis=dim)
        cells = jnp.concatenate(
            [
                lax.ppermute(tail, axis, [(i, (i + 1) % count) for i in range(ends)]),
                cells,
                lax.ppermute(head, axis, [((i + 1) % count, i) for i in range(ends)]),
            ],
            axis=dim,
        )
    return cells


def toeplitz_band(taps, n_out, n_in):
    period = jnp.concatenate([taps, jnp.zeros((n_in + 1 - taps.shape[0],), taps.dtype)])
    return jnp.tile(period, n_out)[: n_out * n_in].reshape(n_out, n_in)


def resolution_of(parcel):
    first = (parcel >= P1).astype(jnp.int32)
    second = (parcel >= P1 + P2).astype(jnp.int32)
    third = (parcel >= P1 + P2 + P3).astype(jnp.int32)
    return first + second + third


def centered_rows(extended, length):
    level_mean = jnp.mean(extended[:, :, LAG : LAG + length], axis=2, keepdims=True)
    centered = (extended - level_mean).astype(jnp.bfloat16)
    middle = centered[:, :, LAG : LAG + length]
    middle_wide = middle.astype(jnp.float32)
    spread = lax.rsqrt(jnp.mean(middle_wide * middle_wide, axis=2) + EPSILON)
    return (centered, middle, spread)


def mesh_peers(nx, nz):
    me = lax.axis_index("vert")
    tm = lax.axis_index("tm")
    mx, mz = me // nz, me % nz
    return me, tm, mx, mz


def greet(mx, mz, tm, nx, nz):
    barrier = pltpu.get_barrier_semaphore()
    for k in range(1, nx):
        pl.semaphore_signal(
            barrier, inc=1, device_id=(lax.rem(mx + k, nx) * nz + mz, tm),
            device_id_type=pl.DeviceIdType.MESH,
        )
    for k in range(1, nz):
        pl.semaphore_signal(
            barrier, inc=1, device_id=(mx * nz + lax.rem(mz + k, nz), tm),
            device_id_type=pl.DeviceIdType.MESH,
        )
    pl.semaphore_wait(barrier, nx + nz - 2)


def reduce_kernel(nx, nz, x_ref, out_ref, recv_a, send_a, part, recv_b, a_send, a_recv, b_send, b_recv):
    me, tm, mx, mz = mesh_peers(nx, nz)
    greet(mx, mz, tm, nx, nz)
    hz = nz // 2
    peers = (lax.rem(mx + 1, nx), lax.rem(mx + nx - 1, nx))

    def owners_of(g, d):
        return pl.ds(g * nz + d * hz, hz)

    for s in range(1, nx):
        copies = []
        for d in range(2):
            g = lax.rem(mx + (s if d else nx * s - s), nx)
            if s == 1:
                src = x_ref.at[owners_of(g, d)]
            else:
                send_a[d, s - 2] = recv_a[d, s - 2] + x_ref[owners_of(g, d)]
                src = send_a.at[d, s - 2]
            copy = pltpu.make_async_remote_copy(
                src_ref=src, dst_ref=recv_a.at[d, s - 1],
                send_sem=a_send.at[d, s - 1], recv_sem=a_recv.at[d, s - 1],
                device_id=(peers[d] * nz + mz, tm), device_id_type=pl.DeviceIdType.MESH,
            )
            copy.start()
            copies.append(copy)
        for copy in copies:
            copy.wait()
    for d in range(2):
        part[d * hz : (d + 1) * hz] = recv_a[d, nx - 2] + x_ref[owners_of(mx, d)]
    copies = []
    for k in range(1, nz):
        pz = lax.rem(mz + k, nz)
        copy = pltpu.make_async_remote_copy(
            src_ref=part.at[pz], dst_ref=recv_b.at[k - 1],
            send_sem=b_send.at[k - 1], recv_sem=b_recv.at[k - 1],
            device_id=(mx * nz + pz, tm), device_id_type=pl.DeviceIdType.MESH,
        )
        copy.start()
        copies.append(copy)
    for copy in copies:
        copy.wait()
    total = part[mz]
    for k in range(1, nz):
        total = total + recv_b[k - 1]
    out_ref[...] = total


def reduce_to_owner(x, nx, nz):
    n, rows, w = x.shape
    hz = nz // 2
    return pl.pallas_call(
        partial(reduce_kernel, nx, nz),
        out_shape=jax.ShapeDtypeStruct((rows, w), x.dtype),
        in_specs=[pl.BlockSpec(memory_space=pltpu.VMEM)],
        out_specs=pl.BlockSpec(memory_space=pltpu.VMEM),
        scratch_shapes=[
            pltpu.VMEM((2, nx - 1, hz, rows, w), x.dtype),
            pltpu.VMEM((2, nx - 2, hz, rows, w), x.dtype),
            pltpu.VMEM((nz, rows, w), x.dtype),
            pltpu.VMEM((nz - 1, rows, w), x.dtype),
            pltpu.SemaphoreType.DMA((2, nx - 1)),
            pltpu.SemaphoreType.DMA((2, nx - 1)),
            pltpu.SemaphoreType.DMA((nz - 1,)),
            pltpu.SemaphoreType.DMA((nz - 1,)),
        ],
        compiler_params=pltpu.CompilerParams(collective_id=0, has_side_effects=True),
    )(x)


def fill_lags(mid_ref, lhs_ref, band):
    rows = mid_ref.shape[1]
    base = mid_ref[band].astype(jnp.float32)
    for q in range(NLAG):
        lhs_ref[band, q * rows : (q + 1) * rows, :] = pltpu.roll(base, q, 1).astype(lhs_ref.dtype)
    lhs_ref[band, NLAG * rows :, :] = jnp.zeros(
        ((LAG_PAD - NLAG) * rows, lhs_ref.shape[2]), lhs_ref.dtype
    )


def fold_group(g, group, lhs_ref, gath, out_ref, sums_ref, t_dev):
    rows = out_ref.shape[1]
    step = LAG_PAD // LAG_CHUNKS
    first = pl.multiple_of(g * group, 128)

    def one_band(band, carry):
        block = gath[band, pl.ds(first, group), :].astype(jnp.float32)
        rhs_wide = block.T
        rhs = rhs_wide.astype(jnp.bfloat16)
        middle = rhs_wide[LAG : LAG + t_dev, :]
        sums_ref[band, :, pl.ds(first, group)] = jnp.sum(middle * middle, axis=0, keepdims=True)
        acc = jnp.zeros((rows, group), jnp.float32)
        for h in range(LAG_CHUNKS):
            lhs = lhs_ref[band, h * step * rows : (h + 1) * step * rows, :]
            r = jnp.dot(lhs, rhs, preferred_element_type=jnp.float32)
            acc = acc + (r * r).reshape(step, rows, group).sum(axis=0)
        out_ref[band, :, pl.ds(first, group)] = acc
        return carry

    lax.fori_loop(0, out_ref.shape[0], one_band, 0)


def gather_fold_kernel(nx, nz, t_dev, own_ref, mid_ref, out_ref, sums_ref, gath, lhs_ref,
                       a_send, a_recv, b_send, b_recv, local_sem):
    me, tm, mx, mz = mesh_peers(nx, nz)
    rows = own_ref.shape[1]
    group = nz * rows
    greet(mx, mz, tm, nx, nz)
    mine = gath.at[:, pl.ds(me * rows, rows), :]
    own = pltpu.make_async_copy(own_ref, mine, local_sem)
    own.start()
    copies = []
    for k in range(1, nz):
        copy = pltpu.make_async_remote_copy(
            src_ref=own_ref, dst_ref=mine,
            send_sem=a_send.at[k - 1], recv_sem=a_recv.at[k - 1],
            device_id=(mx * nz + lax.rem(mz + k, nz), tm), device_id_type=pl.DeviceIdType.MESH,
        )
        copy.start()
        copies.append(copy)
    for band in range(mid_ref.shape[0]):
        fill_lags(mid_ref, lhs_ref, band)
    own.wait()
    for copy in copies:
        copy.wait()
    left, right = lax.rem(mx + nx - 1, nx), lax.rem(mx + 1, nx)
    half = group // 2

    def ring_copy(start, size, peer, slot):
        rows_at = gath.at[:, pl.ds(start, size), :]
        return pltpu.make_async_remote_copy(
            src_ref=rows_at, dst_ref=rows_at,
            send_sem=b_send.at[slot], recv_sem=b_recv.at[slot],
            device_id=(peer * nz + mz, tm), device_id_type=pl.DeviceIdType.MESH,
        )

    near = [ring_copy(mx * group, group, right, 0), ring_copy(mx * group, group, left, 1)]
    for copy in near:
        copy.start()
    fold_group(mx, group, lhs_ref, gath, out_ref, sums_ref, t_dev)
    for copy in near:
        copy.wait_recv()
    far = [ring_copy(left * group, half, right, 2), ring_copy(right * group + half, half, left, 3)]
    for copy in far:
        copy.start()
    fold_group(left, group, lhs_ref, gath, out_ref, sums_ref, t_dev)
    fold_group(right, group, lhs_ref, gath, out_ref, sums_ref, t_dev)
    for copy in far:
        copy.wait_recv()
    fold_group(lax.rem(mx + 2, nx), group, lhs_ref, gath, out_ref, sums_ref, t_dev)
    for copy in near + far:
        copy.wait_send()


def gather_fold(own, mid, nx, nz, t_dev):
    assert nx == 4
    bands, rows, width = own.shape
    cols = nx * nz * rows
    flops = 2 * bands * LAG_PAD * rows * width * cols
    return pl.pallas_call(
        partial(gather_fold_kernel, nx, nz, t_dev),
        out_shape=(
            jax.ShapeDtypeStruct((bands, rows, cols), jnp.float32),
            jax.ShapeDtypeStruct((bands, 1, cols), jnp.float32),
        ),
        in_specs=[pl.BlockSpec(memory_space=pltpu.VMEM)] * 2,
        out_specs=(pl.BlockSpec(memory_space=pltpu.VMEM),) * 2,
        scratch_shapes=[
            pltpu.VMEM((bands, cols, width), own.dtype),
            pltpu.VMEM((bands, LAG_PAD * rows, width), jnp.bfloat16),
            pltpu.SemaphoreType.DMA((nz - 1,)),
            pltpu.SemaphoreType.DMA((nz - 1,)),
            pltpu.SemaphoreType.DMA((4,)),
            pltpu.SemaphoreType.DMA((4,)),
            pltpu.SemaphoreType.DMA(()),
        ],
        compiler_params=pltpu.CompilerParams(
            collective_id=1, has_side_effects=True, vmem_limit_bytes=48 * 1024 * 1024
        ),
        cost_estimate=pl.CostEstimate(
            flops=flops, bytes_accessed=2 * (own.size + mid.size) + 4 * bands * (rows + 1) * cols,
            transcendentals=0,
        ),
    )(own, mid)


def pool_kernel(par_dev, ids_ref, env_ref, out_ref):
    rows = out_ref.shape[0]
    vertices = env_ref.shape[0]
    r = lax.broadcasted_iota(jnp.int32, (rows, vertices), 0)
    wanted = pl.program_id(0) * par_dev + r
    hits = jnp.zeros((rows, vertices), jnp.float32)
    for level in range(ids_ref.shape[0]):
        hits = hits + (ids_ref[level] == wanted).astype(jnp.float32)
    hits = jnp.where(r < par_dev, hits, 0.0).astype(jnp.bfloat16)
    out_ref[...] = jnp.dot(hits, env_ref[...], preferred_element_type=jnp.float32)


def pool(global_ids, flat_env, owners, par_dev):
    levels, vertices = global_ids.shape
    width = flat_env.shape[1]
    return pl.pallas_call(
        partial(pool_kernel, par_dev),
        out_shape=jax.ShapeDtypeStruct((owners, ROW_PAD, width), jnp.float32),
        grid=(owners,),
        in_specs=[
            pl.BlockSpec((levels, 1, vertices), lambda k: (0, 0, 0)),
            pl.BlockSpec((vertices, width), lambda k: (0, 0)),
        ],
        out_specs=pl.BlockSpec((None, ROW_PAD, width), lambda k: (k, 0, 0)),
        cost_estimate=pl.CostEstimate(
            flops=2 * owners * ROW_PAD * vertices * width,
            bytes_accessed=4 * levels * vertices + 2 * vertices * width + 4 * owners * ROW_PAD * width,
            transcendentals=0,
        ),
    )(global_ids.reshape(levels, 1, vertices), flat_env)


def local(source, band_taps, smooth_taps, parcel_ids):
    vert_dev, t_dev = source.shape
    owners = lax.axis_size("vert")
    total_par = (P1 + P2 + P3 + owners - 1) // owners * owners
    par_dev = total_par // owners
    n_mid = t_dev + 2 * HALF
    n_in = t_dev + 4 * HALF
    first_rows = jax.vmap(partial(toeplitz_band, n_out=n_mid, n_in=n_in))(
        band_taps.reshape(2 * BANDS, TAPS)
    )
    first_mat = first_rows.transpose(2, 0, 1).reshape(n_in, 2 * BANDS * n_mid)
    second_rows = jax.vmap(partial(toeplitz_band, n_out=t_dev, n_in=n_mid))(smooth_taps)
    second_mat = second_rows.transpose(0, 2, 1)
    widened = extended_2(source, (("tm", 1),), 2 * HALF)
    block_rows = math.gcd(vert_dev, 128)

    def filter_block(block):
        wave = jnp.dot(block, first_mat, preferred_element_type=jnp.float32).reshape(
            block_rows, 2, BANDS, n_mid
        )
        power = (wave[:, 0] * wave[:, 0] + wave[:, 1] * wave[:, 1]).astype(jnp.bfloat16)
        return jnp.einsum(
            "vbu,but->vbt", power, second_mat, preferred_element_type=jnp.float32
        ).astype(jnp.bfloat16)

    envelope = lax.map(filter_block, widened.reshape(vert_dev // block_rows, block_rows, n_in))
    flat_env = envelope.reshape(vert_dev, BANDS * t_dev)
    offsets = jnp.array([0, P1, P1 + P2], dtype=jnp.int32)
    global_ids = parcel_ids + offsets[:, None]
    owner_start = lax.axis_index("vert") * par_dev

    pooled = pool(global_ids, flat_env, owners, par_dev)
    nx = owners // VERT_MINOR
    own_sums = reduce_to_owner(pooled, nx, VERT_MINOR)[:par_dev]
    own_env = own_sums.reshape(par_dev, BANDS, t_dev)
    own_ext = extended_2(own_env, (("tm", 2),), LAG)
    centered, own_middle, own_spread = centered_rows(own_ext, t_dev)

    own = jnp.pad(centered.transpose(1, 0, 2), ((0, 0), (0, ROW_PAD - par_dev), (0, 0)))
    mid = jnp.pad(
        own_middle.transpose(1, 0, 2), ((0, 0), (0, ROW_PAD - par_dev), (0, t_dev))
    )
    padded_energy, sums = gather_fold(own, mid, nx, VERT_MINOR, t_dev)
    energy = padded_energy.reshape(BANDS, ROW_PAD, owners, ROW_PAD)[:, :par_dev, :, :par_dev]
    energy = energy.reshape(BANDS, par_dev, total_par)
    vis_sums = sums.reshape(BANDS, owners, ROW_PAD)[:, :, :par_dev].reshape(BANDS, total_par)
    vis_spread = lax.rsqrt(vis_sums / t_dev + EPSILON)

    scale = own_spread.T[:, :, None] * vis_spread[:, None, :] / t_dev
    own_level = resolution_of(owner_start + lax.iota(jnp.int32, par_dev))
    all_level = resolution_of(lax.iota(jnp.int32, total_par))
    same = ((own_level[:, None] == all_level[None, :]) & (own_level[:, None] < 3)).astype(
        jnp.float32
    )
    coupling = energy * scale * scale * same[None] / NLAG
    return coupling[None]


def solution(mesh):
    return jax.shard_map(
        local,
        mesh=mesh,
        in_specs=(P("vert", "tm"), P(), P(), P(None, "vert")),
        out_specs=P("tm", None, "vert", None),
        check_vma=False,
    )
```

```python
from functools import partial
import math

import jax
import jax.numpy as jnp
from jax import lax
from jax.experimental import pallas as pl
from jax.experimental.pallas import tpu as pltpu
from jax.sharding import PartitionSpec as P

P1 = 100
P2 = 400
P3 = 1000
BANDS = 2
TAPS = 65
HALF = 32
LAG = 64
LAG_STEP = 1
NLAG = 129

EPSILON = 1e-05

ROW_PAD = 96
LAG_CHUNKS = 11
LAG_PAD = 132
VERT_MINOR = 4


def extended_2(cells, sides, width):
    for axis, dim in sides:
        count = lax.axis_size(axis)
        ends = count - 1
        head = lax.slice_in_dim(cells, 0, width, axis=dim)
        tail = lax.slice_in_dim(cells, cells.shape[dim] - width, cells.shape[dim], axis=dim)
        cells = jnp.concatenate(
            [
                lax.ppermute(tail, axis, [(i, (i + 1) % count) for i in range(ends)]),
                cells,
                lax.ppermute(head, axis, [((i + 1) % count, i) for i in range(ends)]),
            ],
            axis=dim,
        )
    return cells


def toeplitz_band(taps, n_out, n_in):
    period = jnp.concatenate([taps, jnp.zeros((n_in + 1 - taps.shape[0],), taps.dtype)])
    return jnp.tile(period, n_out)[: n_out * n_in].reshape(n_out, n_in)


def resolution_of(parcel):
    first = (parcel >= P1).astype(jnp.int32)
    second = (parcel >= P1 + P2).astype(jnp.int32)
    third = (parcel >= P1 + P2 + P3).astype(jnp.int32)
    return first + second + third


def centered_rows(extended, length):
    level_mean = jnp.mean(extended[:, :, LAG : LAG + length], axis=2, keepdims=True)
    centered = (extended - level_mean).astype(jnp.bfloat16)
    middle = centered[:, :, LAG : LAG + length]
    middle_wide = middle.astype(jnp.float32)
    spread = lax.rsqrt(jnp.mean(middle_wide * middle_wide, axis=2) + EPSILON)
    return (centered, middle, spread)


def mesh_peers(nx, nz):
    me = lax.axis_index("vert")
    tm = lax.axis_index("tm")
    mx, mz = me // nz, me % nz
    return me, tm, mx, mz


def greet(mx, mz, tm, nx, nz, n_tm=0):
    barrier = pltpu.get_barrier_semaphore()
    me = mx * nz + mz
    peers = [(lax.rem(mx + k, nx) * nz + mz, tm) for k in range(1, nx)]
    peers += [(mx * nz + lax.rem(mz + k, nz), tm) for k in range(1, nz)]
    if n_tm:
        peers += [(me, lax.rem(tm + 1, n_tm)), (me, lax.rem(tm + n_tm - 1, n_tm))]
    for peer in peers:
        pl.semaphore_signal(barrier, inc=1, device_id=peer, device_id_type=pl.DeviceIdType.MESH)
    pl.semaphore_wait(barrier, len(peers))


def reduce_kernel(nx, nz, n_tm, x_ref, out_ref, recv_a, send_a, part, recv_b, mine, halo, a_send, a_recv,
                  b_send, b_recv, t_send, t_recv):
    me, tm, mx, mz = mesh_peers(nx, nz)
    greet(mx, mz, tm, nx, nz, n_tm)
    hz = nz // 2
    peers = (lax.rem(mx + 1, nx), lax.rem(mx + nx - 1, nx))

    def owners_of(g, d):
        return pl.ds(g * nz + d * hz, hz)

    for s in range(1, nx):
        copies = []
        for d in range(2):
            g = lax.rem(mx + (s if d else nx * s - s), nx)
            if s == 1:
                src = x_ref.at[owners_of(g, d)]
            else:
                send_a[d, s - 2] = recv_a[d, s - 2] + x_ref[owners_of(g, d)]
                src = send_a.at[d, s - 2]
            copy = pltpu.make_async_remote_copy(
                src_ref=src, dst_ref=recv_a.at[d, s - 1],
                send_sem=a_send.at[d, s - 1], recv_sem=a_recv.at[d, s - 1],
                device_id=(peers[d] * nz + mz, tm), device_id_type=pl.DeviceIdType.MESH,
            )
            copy.start()
            copies.append(copy)
        for copy in copies:
            copy.wait()
    for d in range(2):
        part[d * hz : (d + 1) * hz] = recv_a[d, nx - 2] + x_ref[owners_of(mx, d)]
    copies = []
    for k in range(1, nz):
        pz = lax.rem(mz + k, nz)
        copy = pltpu.make_async_remote_copy(
            src_ref=part.at[pz], dst_ref=recv_b.at[k - 1],
            send_sem=b_send.at[k - 1], recv_sem=b_recv.at[k - 1],
            device_id=(mx * nz + pz, tm), device_id_type=pl.DeviceIdType.MESH,
        )
        copy.start()
        copies.append(copy)
    for copy in copies:
        copy.wait()
    total = part[mz]
    for k in range(1, nz):
        total = total + recv_b[k - 1]
    mine[...] = total
    copies = []
    for d, step in enumerate((1, n_tm - 1)):
        copy = pltpu.make_async_remote_copy(
            src_ref=mine, dst_ref=halo.at[d],
            send_sem=t_send.at[d], recv_sem=t_recv.at[d],
            device_id=(me, lax.rem(tm + step, n_tm)), device_id_type=pl.DeviceIdType.MESH,
        )
        copy.start()
        copies.append(copy)
    out_ref[1] = total
    for copy in copies:
        copy.wait()
    out_ref[0] = halo[0]
    out_ref[2] = halo[1]


def reduce_to_owner(x, nx, nz, n_tm):
    n, rows, w = x.shape
    hz = nz // 2
    return pl.pallas_call(
        partial(reduce_kernel, nx, nz, n_tm),
        out_shape=jax.ShapeDtypeStruct((3, rows, w), x.dtype),
        in_specs=[pl.BlockSpec(memory_space=pltpu.VMEM)],
        out_specs=pl.BlockSpec(memory_space=pltpu.VMEM),
        scratch_shapes=[
            pltpu.VMEM((2, nx - 1, hz, rows, w), x.dtype),
            pltpu.VMEM((2, nx - 2, hz, rows, w), x.dtype),
            pltpu.VMEM((nz, rows, w), x.dtype),
            pltpu.VMEM((nz - 1, rows, w), x.dtype),
            pltpu.VMEM((rows, w), x.dtype),
            pltpu.VMEM((2, rows, w), x.dtype),
            pltpu.SemaphoreType.DMA((2, nx - 1)),
            pltpu.SemaphoreType.DMA((2, nx - 1)),
            pltpu.SemaphoreType.DMA((nz - 1,)),
            pltpu.SemaphoreType.DMA((nz - 1,)),
            pltpu.SemaphoreType.DMA((2,)),
            pltpu.SemaphoreType.DMA((2,)),
        ],
        compiler_params=pltpu.CompilerParams(collective_id=0, has_side_effects=True),
    )(x)


def fill_lags(mid_ref, lhs_ref, band):
    rows = mid_ref.shape[1]
    base = mid_ref[band].astype(jnp.float32)
    for q in range(NLAG):
        lhs_ref[band, q * rows : (q + 1) * rows, :] = pltpu.roll(base, q, 1).astype(lhs_ref.dtype)
    lhs_ref[band, NLAG * rows :, :] = jnp.zeros(
        ((LAG_PAD - NLAG) * rows, lhs_ref.shape[2]), lhs_ref.dtype
    )


def fold_group(g, group, lhs_ref, gath, out_ref, sums_ref, t_dev):
    rows = out_ref.shape[1]
    step = LAG_PAD // LAG_CHUNKS
    first = pl.multiple_of(g * group, 128)

    def one_band(band, carry):
        block = gath[band, pl.ds(first, group), :].astype(jnp.float32)
        rhs_wide = block.T
        rhs = rhs_wide.astype(jnp.bfloat16)
        middle = rhs_wide[LAG : LAG + t_dev, :]
        sums_ref[band, :, pl.ds(first, group)] = jnp.sum(middle * middle, axis=0, keepdims=True)
        acc = jnp.zeros((rows, group), jnp.float32)
        for h in range(LAG_CHUNKS):
            lhs = lhs_ref[band, h * step * rows : (h + 1) * step * rows, :]
            r = jnp.dot(lhs, rhs, preferred_element_type=jnp.float32)
            acc = acc + (r * r).reshape(step, rows, group).sum(axis=0)
        out_ref[band, :, pl.ds(first, group)] = acc
        return carry

    lax.fori_loop(0, out_ref.shape[0], one_band, 0)


def gather_fold_kernel(nx, nz, t_dev, own_ref, mid_ref, out_ref, sums_ref, gath, lhs_ref,
                       a_send, a_recv, b_send, b_recv, local_sem):
    me, tm, mx, mz = mesh_peers(nx, nz)
    rows = own_ref.shape[1]
    group = nz * rows
    greet(mx, mz, tm, nx, nz)
    mine = gath.at[:, pl.ds(me * rows, rows), :]
    own = pltpu.make_async_copy(own_ref, mine, local_sem)
    own.start()
    copies = []
    for k in range(1, nz):
        copy = pltpu.make_async_remote_copy(
            src_ref=own_ref, dst_ref=mine,
            send_sem=a_send.at[k - 1], recv_sem=a_recv.at[k - 1],
            device_id=(mx * nz + lax.rem(mz + k, nz), tm), device_id_type=pl.DeviceIdType.MESH,
        )
        copy.start()
        copies.append(copy)
    for band in range(mid_ref.shape[0]):
        fill_lags(mid_ref, lhs_ref, band)
    own.wait()
    for copy in copies:
        copy.wait()
    left, right = lax.rem(mx + nx - 1, nx), lax.rem(mx + 1, nx)
    half = group // 2

    def ring_copy(start, size, peer, slot):
        rows_at = gath.at[:, pl.ds(start, size), :]
        return pltpu.make_async_remote_copy(
            src_ref=rows_at, dst_ref=rows_at,
            send_sem=b_send.at[slot], recv_sem=b_recv.at[slot],
            device_id=(peer * nz + mz, tm), device_id_type=pl.DeviceIdType.MESH,
        )

    near = [ring_copy(mx * group, group, right, 0), ring_copy(mx * group, group, left, 1)]
    for copy in near:
        copy.start()
    fold_group(mx, group, lhs_ref, gath, out_ref, sums_ref, t_dev)
    for copy in near:
        copy.wait_recv()
    far = [ring_copy(left * group, half, right, 2), ring_copy(right * group + half, half, left, 3)]
    for copy in far:
        copy.start()
    fold_group(left, group, lhs_ref, gath, out_ref, sums_ref, t_dev)
    fold_group(right, group, lhs_ref, gath, out_ref, sums_ref, t_dev)
    for copy in far:
        copy.wait_recv()
    fold_group(lax.rem(mx + 2, nx), group, lhs_ref, gath, out_ref, sums_ref, t_dev)
    for copy in near + far:
        copy.wait_send()


def gather_fold(own, mid, nx, nz, t_dev):
    assert nx == 4
    bands, rows, width = own.shape
    cols = nx * nz * rows
    flops = 2 * bands * LAG_PAD * rows * width * cols
    return pl.pallas_call(
        partial(gather_fold_kernel, nx, nz, t_dev),
        out_shape=(
            jax.ShapeDtypeStruct((bands, rows, cols), jnp.float32),
            jax.ShapeDtypeStruct((bands, 1, cols), jnp.float32),
        ),
        in_specs=[pl.BlockSpec(memory_space=pltpu.VMEM)] * 2,
        out_specs=(pl.BlockSpec(memory_space=pltpu.VMEM),) * 2,
        scratch_shapes=[
            pltpu.VMEM((bands, cols, width), own.dtype),
            pltpu.VMEM((bands, LAG_PAD * rows, width), jnp.bfloat16),
            pltpu.SemaphoreType.DMA((nz - 1,)),
            pltpu.SemaphoreType.DMA((nz - 1,)),
            pltpu.SemaphoreType.DMA((4,)),
            pltpu.SemaphoreType.DMA((4,)),
            pltpu.SemaphoreType.DMA(()),
        ],
        compiler_params=pltpu.CompilerParams(
            collective_id=1, has_side_effects=True, vmem_limit_bytes=48 * 1024 * 1024
        ),
        cost_estimate=pl.CostEstimate(
            flops=flops, bytes_accessed=2 * (own.size + mid.size) + 4 * bands * (rows + 1) * cols,
            transcendentals=0,
        ),
    )(own, mid)


def pool_kernel(par_dev, ids_ref, env_ref, out_ref):
    rows = out_ref.shape[0]
    vertices = env_ref.shape[0]
    r = lax.broadcasted_iota(jnp.int32, (rows, vertices), 0)
    wanted = pl.program_id(0) * par_dev + r
    hits = jnp.zeros((rows, vertices), jnp.float32)
    for level in range(ids_ref.shape[0]):
        hits = hits + (ids_ref[level] == wanted).astype(jnp.float32)
    hits = jnp.where(r < par_dev, hits, 0.0).astype(jnp.bfloat16)
    out_ref[...] = jnp.dot(hits, env_ref[...], preferred_element_type=jnp.float32)


def pool(global_ids, flat_env, owners, par_dev):
    levels, vertices = global_ids.shape
    width = flat_env.shape[1]
    return pl.pallas_call(
        partial(pool_kernel, par_dev),
        out_shape=jax.ShapeDtypeStruct((owners, ROW_PAD, width), jnp.float32),
        grid=(owners,),
        in_specs=[
            pl.BlockSpec((levels, 1, vertices), lambda k: (0, 0, 0)),
            pl.BlockSpec((vertices, width), lambda k: (0, 0)),
        ],
        out_specs=pl.BlockSpec((None, ROW_PAD, width), lambda k: (k, 0, 0)),
        cost_estimate=pl.CostEstimate(
            flops=2 * owners * ROW_PAD * vertices * width,
            bytes_accessed=4 * levels * vertices + 2 * vertices * width + 4 * owners * ROW_PAD * width,
            transcendentals=0,
        ),
    )(global_ids.reshape(levels, 1, vertices), flat_env)


def local(source, band_taps, smooth_taps, parcel_ids):
    vert_dev, t_dev = source.shape
    owners = lax.axis_size("vert")
    total_par = (P1 + P2 + P3 + owners - 1) // owners * owners
    par_dev = total_par // owners
    n_mid = t_dev + 2 * HALF
    n_in = t_dev + 4 * HALF
    first_rows = jax.vmap(partial(toeplitz_band, n_out=n_mid, n_in=n_in))(
        band_taps.reshape(2 * BANDS, TAPS)
    )
    first_mat = first_rows.transpose(2, 0, 1).reshape(n_in, 2 * BANDS * n_mid)
    second_rows = jax.vmap(partial(toeplitz_band, n_out=t_dev, n_in=n_mid))(smooth_taps)
    second_mat = second_rows.transpose(0, 2, 1)
    widened = extended_2(source, (("tm", 1),), 2 * HALF)
    block_rows = math.gcd(vert_dev, 128)

    def filter_block(block):
        wave = jnp.dot(block, first_mat, preferred_element_type=jnp.float32).reshape(
            block_rows, 2, BANDS, n_mid
        )
        power = (wave[:, 0] * wave[:, 0] + wave[:, 1] * wave[:, 1]).astype(jnp.bfloat16)
        return jnp.einsum(
            "vbu,but->vbt", power, second_mat, preferred_element_type=jnp.float32
        ).astype(jnp.bfloat16)

    envelope = lax.map(filter_block, widened.reshape(vert_dev // block_rows, block_rows, n_in))
    flat_env = envelope.reshape(vert_dev, BANDS * t_dev)
    offsets = jnp.array([0, P1, P1 + P2], dtype=jnp.int32)
    global_ids = parcel_ids + offsets[:, None]
    owner_start = lax.axis_index("vert") * par_dev

    pooled = pool(global_ids, flat_env, owners, par_dev)
    nx = owners // VERT_MINOR
    n_tm = lax.axis_size("tm")
    tm = lax.axis_index("tm")
    sums3 = reduce_to_owner(pooled, nx, VERT_MINOR, n_tm)[:, :par_dev].reshape(3, par_dev, BANDS, t_dev)
    before = jnp.where(tm > 0, sums3[0, :, :, t_dev - LAG :], 0.0)
    after = jnp.where(tm < n_tm - 1, sums3[2, :, :, :LAG], 0.0)
    own_ext = jnp.concatenate([before, sums3[1], after], axis=2)
    centered, own_middle, own_spread = centered_rows(own_ext, t_dev)

    own = jnp.pad(centered.transpose(1, 0, 2), ((0, 0), (0, ROW_PAD - par_dev), (0, 0)))
    mid = jnp.pad(
        own_middle.transpose(1, 0, 2), ((0, 0), (0, ROW_PAD - par_dev), (0, t_dev))
    )
    padded_energy, sums = gather_fold(own, mid, nx, VERT_MINOR, t_dev)
    energy = padded_energy.reshape(BANDS, ROW_PAD, owners, ROW_PAD)[:, :par_dev, :, :par_dev]
    energy = energy.reshape(BANDS, par_dev, total_par)
    vis_sums = sums.reshape(BANDS, owners, ROW_PAD)[:, :, :par_dev].reshape(BANDS, total_par)
    vis_spread = lax.rsqrt(vis_sums / t_dev + EPSILON)

    scale = own_spread.T[:, :, None] * vis_spread[:, None, :] / t_dev
    own_level = resolution_of(owner_start + lax.iota(jnp.int32, par_dev))
    all_level = resolution_of(lax.iota(jnp.int32, total_par))
    same = ((own_level[:, None] == all_level[None, :]) & (own_level[:, None] < 3)).astype(
        jnp.float32
    )
    coupling = energy * scale * scale * same[None] / NLAG
    return coupling[None]


def solution(mesh):
    return jax.shard_map(
        local,
        mesh=mesh,
        in_specs=(P("vert", "tm"), P(), P(), P(None, "vert")),
        out_specs=P("tm", None, "vert", None),
        check_vma=False,
    )
```

```python
from functools import partial
import math

import jax
import jax.numpy as jnp
from jax import lax
from jax.experimental import pallas as pl
from jax.experimental.pallas import tpu as pltpu
from jax.sharding import PartitionSpec as P

P1 = 100
P2 = 400
P3 = 1000
BANDS = 2
TAPS = 65
HALF = 32
LAG = 64
LAG_STEP = 1
NLAG = 129

EPSILON = 1e-05

ROW_PAD = 96
LAG_CHUNKS = 11
LAG_PAD = 132
VERT_MINOR = 4


def extended_2(cells, sides, width):
    for axis, dim in sides:
        count = lax.axis_size(axis)
        ends = count - 1
        head = lax.slice_in_dim(cells, 0, width, axis=dim)
        tail = lax.slice_in_dim(cells, cells.shape[dim] - width, cells.shape[dim], axis=dim)
        cells = jnp.concatenate(
            [
                lax.ppermute(tail, axis, [(i, (i + 1) % count) for i in range(ends)]),
                cells,
                lax.ppermute(head, axis, [((i + 1) % count, i) for i in range(ends)]),
            ],
            axis=dim,
        )
    return cells


def toeplitz_band(taps, n_out, n_in):
    period = jnp.concatenate([taps, jnp.zeros((n_in + 1 - taps.shape[0],), taps.dtype)])
    return jnp.tile(period, n_out)[: n_out * n_in].reshape(n_out, n_in)


def resolution_of(parcel):
    first = (parcel >= P1).astype(jnp.int32)
    second = (parcel >= P1 + P2).astype(jnp.int32)
    third = (parcel >= P1 + P2 + P3).astype(jnp.int32)
    return first + second + third


def centered_rows(extended, length):
    level_mean = jnp.mean(extended[:, :, LAG : LAG + length], axis=2, keepdims=True)
    centered = (extended - level_mean).astype(jnp.bfloat16)
    middle = centered[:, :, LAG : LAG + length]
    middle_wide = middle.astype(jnp.float32)
    spread = lax.rsqrt(jnp.mean(middle_wide * middle_wide, axis=2) + EPSILON)
    return (centered, middle, spread)


def mesh_peers(nx, nz):
    me = lax.axis_index("vert")
    tm = lax.axis_index("tm")
    mx, mz = me // nz, me % nz
    return me, tm, mx, mz


def greet(mx, mz, tm, nx, nz, n_tm=0):
    barrier = pltpu.get_barrier_semaphore()
    me = mx * nz + mz
    peers = [(lax.rem(mx + k, nx) * nz + mz, tm) for k in range(1, nx)]
    peers += [(mx * nz + lax.rem(mz + k, nz), tm) for k in range(1, nz)]
    if n_tm:
        peers += [(me, lax.rem(tm + 1, n_tm)), (me, lax.rem(tm + n_tm - 1, n_tm))]
    for peer in peers:
        pl.semaphore_signal(barrier, inc=1, device_id=peer, device_id_type=pl.DeviceIdType.MESH)
    pl.semaphore_wait(barrier, len(peers))


def reduce_kernel(nx, nz, n_tm, x_ref, out_ref, recv_a, send_a, part, recv_b, mine, halo, a_send, a_recv,
                  b_send, b_recv, t_send, t_recv):
    me, tm, mx, mz = mesh_peers(nx, nz)
    greet(mx, mz, tm, nx, nz, n_tm)
    hz = nz // 2
    peers = (lax.rem(mx + 1, nx), lax.rem(mx + nx - 1, nx))

    def owners_of(g, d):
        return pl.ds(g * nz + d * hz, hz)

    for s in range(1, nx):
        copies = []
        for d in range(2):
            g = lax.rem(mx + (s if d else nx * s - s), nx)
            if s == 1:
                src = x_ref.at[owners_of(g, d)]
            else:
                send_a[d, s - 2] = recv_a[d, s - 2] + x_ref[owners_of(g, d)]
                src = send_a.at[d, s - 2]
            copy = pltpu.make_async_remote_copy(
                src_ref=src, dst_ref=recv_a.at[d, s - 1],
                send_sem=a_send.at[d, s - 1], recv_sem=a_recv.at[d, s - 1],
                device_id=(peers[d] * nz + mz, tm), device_id_type=pl.DeviceIdType.MESH,
            )
            copy.start()
            copies.append(copy)
        for copy in copies:
            copy.wait()
    for d in range(2):
        part[d * hz : (d + 1) * hz] = recv_a[d, nx - 2] + x_ref[owners_of(mx, d)]
    copies = []
    for k in range(1, nz):
        pz = lax.rem(mz + k, nz)
        copy = pltpu.make_async_remote_copy(
            src_ref=part.at[pz], dst_ref=recv_b.at[k - 1],
            send_sem=b_send.at[k - 1], recv_sem=b_recv.at[k - 1],
            device_id=(mx * nz + pz, tm), device_id_type=pl.DeviceIdType.MESH,
        )
        copy.start()
        copies.append(copy)
    for copy in copies:
        copy.wait()
    total = part[mz]
    for k in range(1, nz):
        total = total + recv_b[k - 1]
    mine[...] = total
    copies = []
    for d, step in enumerate((1, n_tm - 1)):
        copy = pltpu.make_async_remote_copy(
            src_ref=mine, dst_ref=halo.at[d],
            send_sem=t_send.at[d], recv_sem=t_recv.at[d],
            device_id=(me, lax.rem(tm + step, n_tm)), device_id_type=pl.DeviceIdType.MESH,
        )
        copy.start()
        copies.append(copy)
    out_ref[1] = total
    for copy in copies:
        copy.wait()
    out_ref[0] = halo[0]
    out_ref[2] = halo[1]


def reduce_to_owner(x, nx, nz, n_tm):
    n, rows, w = x.shape
    hz = nz // 2
    return pl.pallas_call(
        partial(reduce_kernel, nx, nz, n_tm),
        out_shape=jax.ShapeDtypeStruct((3, rows, w), x.dtype),
        in_specs=[pl.BlockSpec(memory_space=pltpu.VMEM)],
        out_specs=pl.BlockSpec(memory_space=pltpu.VMEM),
        scratch_shapes=[
            pltpu.VMEM((2, nx - 1, hz, rows, w), x.dtype),
            pltpu.VMEM((2, nx - 2, hz, rows, w), x.dtype),
            pltpu.VMEM((nz, rows, w), x.dtype),
            pltpu.VMEM((nz - 1, rows, w), x.dtype),
            pltpu.VMEM((rows, w), x.dtype),
            pltpu.VMEM((2, rows, w), x.dtype),
            pltpu.SemaphoreType.DMA((2, nx - 1)),
            pltpu.SemaphoreType.DMA((2, nx - 1)),
            pltpu.SemaphoreType.DMA((nz - 1,)),
            pltpu.SemaphoreType.DMA((nz - 1,)),
            pltpu.SemaphoreType.DMA((2,)),
            pltpu.SemaphoreType.DMA((2,)),
        ],
        compiler_params=pltpu.CompilerParams(collective_id=0, has_side_effects=True),
    )(x)


def fill_lags(mid_ref, lhs_ref, band):
    rows = mid_ref.shape[1]
    base = mid_ref[band].astype(jnp.float32)
    for q in range(NLAG):
        lhs_ref[band, q * rows : (q + 1) * rows, :] = pltpu.roll(base, q, 1).astype(lhs_ref.dtype)
    lhs_ref[band, NLAG * rows :, :] = jnp.zeros(
        ((LAG_PAD - NLAG) * rows, lhs_ref.shape[2]), lhs_ref.dtype
    )


def fold_group(g, group, lhs_ref, gath, out_ref, spread_ref, level_ref, t_dev):
    rows = out_ref.shape[1]
    step = LAG_PAD // LAG_CHUNKS
    first = pl.multiple_of(g * group, 128)
    same = (level_ref[:, 0:1] == level_ref[:, pl.ds(pl.multiple_of(g * group + 128, 128), group)]).astype(jnp.float32)

    def one_band(band, carry):
        block = gath[band, pl.ds(first, group), :].astype(jnp.float32)
        rhs_wide = block.T
        rhs = rhs_wide.astype(jnp.bfloat16)
        middle = rhs_wide[LAG : LAG + t_dev, :]
        spread = lax.rsqrt(jnp.sum(middle * middle, axis=0, keepdims=True) / t_dev + EPSILON)
        acc = jnp.zeros((rows, group), jnp.float32)
        for h in range(LAG_CHUNKS):
            lhs = lhs_ref[band, h * step * rows : (h + 1) * step * rows, :]
            r = jnp.dot(lhs, rhs, preferred_element_type=jnp.float32)
            acc = acc + (r * r).reshape(step, rows, group).sum(axis=0)
        scale = spread_ref[band] * spread / t_dev
        out_ref[band, :, pl.ds(first, group)] = acc * (scale * scale) * same / NLAG
        return carry

    lax.fori_loop(0, out_ref.shape[0], one_band, 0)


def gather_fold_kernel(nx, nz, t_dev, own_ref, mid_ref, spread_ref, level_ref, out_ref, gath, lhs_ref,
                       a_send, a_recv, b_send, b_recv, local_sem):
    me, tm, mx, mz = mesh_peers(nx, nz)
    rows = own_ref.shape[1]
    group = nz * rows
    greet(mx, mz, tm, nx, nz)
    mine = gath.at[:, pl.ds(me * rows, rows), :]
    own = pltpu.make_async_copy(own_ref, mine, local_sem)
    own.start()
    copies = []
    for k in range(1, nz):
        copy = pltpu.make_async_remote_copy(
            src_ref=own_ref, dst_ref=mine,
            send_sem=a_send.at[k - 1], recv_sem=a_recv.at[k - 1],
            device_id=(mx * nz + lax.rem(mz + k, nz), tm), device_id_type=pl.DeviceIdType.MESH,
        )
        copy.start()
        copies.append(copy)
    for band in range(mid_ref.shape[0]):
        fill_lags(mid_ref, lhs_ref, band)
    own.wait()
    for copy in copies:
        copy.wait()
    left, right = lax.rem(mx + nx - 1, nx), lax.rem(mx + 1, nx)
    half = group // 2

    def ring_copy(start, size, peer, slot):
        rows_at = gath.at[:, pl.ds(start, size), :]
        return pltpu.make_async_remote_copy(
            src_ref=rows_at, dst_ref=rows_at,
            send_sem=b_send.at[slot], recv_sem=b_recv.at[slot],
            device_id=(peer * nz + mz, tm), device_id_type=pl.DeviceIdType.MESH,
        )

    near = [ring_copy(mx * group, group, right, 0), ring_copy(mx * group, group, left, 1)]
    for copy in near:
        copy.start()
    fold_group(mx, group, lhs_ref, gath, out_ref, spread_ref, level_ref, t_dev)
    for copy in near:
        copy.wait_recv()
    far = [ring_copy(left * group, half, right, 2), ring_copy(right * group + half, half, left, 3)]
    for copy in far:
        copy.start()
    fold_group(left, group, lhs_ref, gath, out_ref, spread_ref, level_ref, t_dev)
    fold_group(right, group, lhs_ref, gath, out_ref, spread_ref, level_ref, t_dev)
    for copy in far:
        copy.wait_recv()
    fold_group(lax.rem(mx + 2, nx), group, lhs_ref, gath, out_ref, spread_ref, level_ref, t_dev)
    for copy in near + far:
        copy.wait_send()


def gather_fold(own, mid, spread, levels, nx, nz, t_dev):
    assert nx == 4
    bands, rows, width = own.shape
    cols = nx * nz * rows
    flops = 2 * bands * LAG_PAD * rows * width * cols
    return pl.pallas_call(
        partial(gather_fold_kernel, nx, nz, t_dev),
        out_shape=jax.ShapeDtypeStruct((bands, rows, cols), jnp.float32),
        in_specs=[pl.BlockSpec(memory_space=pltpu.VMEM)] * 4,
        out_specs=pl.BlockSpec(memory_space=pltpu.VMEM),
        scratch_shapes=[
            pltpu.VMEM((bands, cols, width), own.dtype),
            pltpu.VMEM((bands, LAG_PAD * rows, width), jnp.bfloat16),
            pltpu.SemaphoreType.DMA((nz - 1,)),
            pltpu.SemaphoreType.DMA((nz - 1,)),
            pltpu.SemaphoreType.DMA((4,)),
            pltpu.SemaphoreType.DMA((4,)),
            pltpu.SemaphoreType.DMA(()),
        ],
        compiler_params=pltpu.CompilerParams(
            collective_id=1, has_side_effects=True, vmem_limit_bytes=48 * 1024 * 1024
        ),
        cost_estimate=pl.CostEstimate(
            flops=flops, bytes_accessed=2 * (own.size + mid.size) + 4 * bands * rows * cols,
            transcendentals=0,
        ),
    )(own, mid, spread, levels)


def pool_kernel(par_dev, ids_ref, env_ref, out_ref):
    rows = out_ref.shape[0]
    vertices = env_ref.shape[0]
    r = lax.broadcasted_iota(jnp.int32, (rows, vertices), 0)
    wanted = pl.program_id(0) * par_dev + r
    hits = jnp.zeros((rows, vertices), jnp.float32)
    for level in range(ids_ref.shape[0]):
        hits = hits + (ids_ref[level] == wanted).astype(jnp.float32)
    hits = jnp.where(r < par_dev, hits, 0.0).astype(jnp.bfloat16)
    out_ref[...] = jnp.dot(hits, env_ref[...], preferred_element_type=jnp.float32)


def pool(global_ids, flat_env, owners, par_dev):
    levels, vertices = global_ids.shape
    width = flat_env.shape[1]
    return pl.pallas_call(
        partial(pool_kernel, par_dev),
        out_shape=jax.ShapeDtypeStruct((owners, ROW_PAD, width), jnp.float32),
        grid=(owners,),
        in_specs=[
            pl.BlockSpec((levels, 1, vertices), lambda k: (0, 0, 0)),
            pl.BlockSpec((vertices, width), lambda k: (0, 0)),
        ],
        out_specs=pl.BlockSpec((None, ROW_PAD, width), lambda k: (k, 0, 0)),
        cost_estimate=pl.CostEstimate(
            flops=2 * owners * ROW_PAD * vertices * width,
            bytes_accessed=4 * levels * vertices + 2 * vertices * width + 4 * owners * ROW_PAD * width,
            transcendentals=0,
        ),
    )(global_ids.reshape(levels, 1, vertices), flat_env)


def local(source, band_taps, smooth_taps, parcel_ids):
    vert_dev, t_dev = source.shape
    owners = lax.axis_size("vert")
    total_par = (P1 + P2 + P3 + owners - 1) // owners * owners
    par_dev = total_par // owners
    n_mid = t_dev + 2 * HALF
    n_in = t_dev + 4 * HALF
    first_rows = jax.vmap(partial(toeplitz_band, n_out=n_mid, n_in=n_in))(
        band_taps.reshape(2 * BANDS, TAPS)
    )
    first_mat = first_rows.transpose(2, 0, 1).reshape(n_in, 2 * BANDS * n_mid)
    second_rows = jax.vmap(partial(toeplitz_band, n_out=t_dev, n_in=n_mid))(smooth_taps)
    second_mat = second_rows.transpose(0, 2, 1)
    widened = extended_2(source, (("tm", 1),), 2 * HALF)
    block_rows = math.gcd(vert_dev, 128)

    def filter_block(block):
        wave = jnp.dot(block, first_mat, preferred_element_type=jnp.float32).reshape(
            block_rows, 2, BANDS, n_mid
        )
        power = (wave[:, 0] * wave[:, 0] + wave[:, 1] * wave[:, 1]).astype(jnp.bfloat16)
        return jnp.einsum(
            "vbu,but->vbt", power, second_mat, preferred_element_type=jnp.float32
        ).astype(jnp.bfloat16)

    envelope = lax.map(filter_block, widened.reshape(vert_dev // block_rows, block_rows, n_in))
    flat_env = envelope.reshape(vert_dev, BANDS * t_dev)
    offsets = jnp.array([0, P1, P1 + P2], dtype=jnp.int32)
    global_ids = parcel_ids + offsets[:, None]
    owner_start = lax.axis_index("vert") * par_dev

    pooled = pool(global_ids, flat_env, owners, par_dev)
    nx = owners // VERT_MINOR
    n_tm = lax.axis_size("tm")
    tm = lax.axis_index("tm")
    sums3 = reduce_to_owner(pooled, nx, VERT_MINOR, n_tm)[:, :par_dev].reshape(3, par_dev, BANDS, t_dev)
    before = jnp.where(tm > 0, sums3[0, :, :, t_dev - LAG :], 0.0)
    after = jnp.where(tm < n_tm - 1, sums3[2, :, :, :LAG], 0.0)
    own_ext = jnp.concatenate([before, sums3[1], after], axis=2)
    centered, own_middle, own_spread = centered_rows(own_ext, t_dev)

    own = jnp.pad(centered.transpose(1, 0, 2), ((0, 0), (0, ROW_PAD - par_dev), (0, 0)))
    mid = jnp.pad(
        own_middle.transpose(1, 0, 2), ((0, 0), (0, ROW_PAD - par_dev), (0, t_dev))
    )
    spread = jnp.pad(own_spread.T, ((0, 0), (0, ROW_PAD - par_dev)))[:, :, None]
    r = lax.iota(jnp.int32, ROW_PAD)
    own_level = jnp.where(
        r < par_dev, resolution_of(owner_start + r), -2
    ).astype(jnp.float32)
    own_level = jnp.where(own_level < 3, own_level, -2.0)
    col = lax.iota(jnp.int32, owners * ROW_PAD)
    col_level = jnp.where(
        col % ROW_PAD < par_dev, resolution_of(col // ROW_PAD * par_dev + col % ROW_PAD), -1
    ).astype(jnp.float32)
    levels = jnp.concatenate(
        [jnp.broadcast_to(own_level[:, None], (ROW_PAD, 128)),
         jnp.broadcast_to(col_level[None, :], (ROW_PAD, owners * ROW_PAD))], axis=1
    )
    padded = gather_fold(own, mid, spread, levels, nx, VERT_MINOR, t_dev)
    coupling = padded.reshape(BANDS, ROW_PAD, owners, ROW_PAD)[:, :par_dev, :, :par_dev]
    coupling = coupling.reshape(BANDS, par_dev, total_par)
    return coupling[None]


def solution(mesh):
    return jax.shard_map(
        local,
        mesh=mesh,
        in_specs=(P("vert", "tm"), P(), P(), P(None, "vert")),
        out_specs=P("tm", None, "vert", None),
        check_vma=False,
    )
```

```python
from functools import partial
import math

import jax
import jax.numpy as jnp
from jax import lax
from jax.experimental import pallas as pl
from jax.experimental.pallas import tpu as pltpu
from jax.sharding import PartitionSpec as P

P1 = 100
P2 = 400
P3 = 1000
BANDS = 2
TAPS = 65
HALF = 32
LAG = 64
LAG_STEP = 1
NLAG = 129

EPSILON = 1e-05

ROW_PAD = 96
LAG_CHUNKS = 11
LAG_PAD = 132
VERT_MINOR = 4


def extended_2(cells, sides, width):
    for axis, dim in sides:
        count = lax.axis_size(axis)
        ends = count - 1
        head = lax.slice_in_dim(cells, 0, width, axis=dim)
        tail = lax.slice_in_dim(cells, cells.shape[dim] - width, cells.shape[dim], axis=dim)
        cells = jnp.concatenate(
            [
                lax.ppermute(tail, axis, [(i, (i + 1) % count) for i in range(ends)]),
                cells,
                lax.ppermute(head, axis, [((i + 1) % count, i) for i in range(ends)]),
            ],
            axis=dim,
        )
    return cells


def toeplitz_band(taps, n_out, n_in):
    period = jnp.concatenate([taps, jnp.zeros((n_in + 1 - taps.shape[0],), taps.dtype)])
    return jnp.tile(period, n_out)[: n_out * n_in].reshape(n_out, n_in)


def resolution_of(parcel):
    first = (parcel >= P1).astype(jnp.int32)
    second = (parcel >= P1 + P2).astype(jnp.int32)
    third = (parcel >= P1 + P2 + P3).astype(jnp.int32)
    return first + second + third


def centered_rows(extended, length):
    level_mean = jnp.mean(extended[:, :, LAG : LAG + length], axis=2, keepdims=True)
    centered = (extended - level_mean).astype(jnp.bfloat16)
    middle = centered[:, :, LAG : LAG + length]
    middle_wide = middle.astype(jnp.float32)
    spread = lax.rsqrt(jnp.mean(middle_wide * middle_wide, axis=2) + EPSILON)
    return (centered, middle, spread)


def mesh_peers(nx, nz):
    me = lax.axis_index("vert")
    tm = lax.axis_index("tm")
    mx, mz = me // nz, me % nz
    return me, tm, mx, mz


def greet(mx, mz, tm, nx, nz, n_tm=0):
    barrier = pltpu.get_barrier_semaphore()
    me = mx * nz + mz
    peers = [(lax.rem(mx + k, nx) * nz + mz, tm) for k in range(1, nx)]
    peers += [(mx * nz + lax.rem(mz + k, nz), tm) for k in range(1, nz)]
    if n_tm:
        peers += [(me, lax.rem(tm + 1, n_tm)), (me, lax.rem(tm + n_tm - 1, n_tm))]
    for peer in peers:
        pl.semaphore_signal(barrier, inc=1, device_id=peer, device_id_type=pl.DeviceIdType.MESH)
    pl.semaphore_wait(barrier, len(peers))


def reduce_kernel(nx, nz, n_tm, x_ref, out_ref, recv_a, send_a, part, recv_b, mine, halo, a_send, a_recv,
                  b_send, b_recv, t_send, t_recv):
    me, tm, mx, mz = mesh_peers(nx, nz)
    greet(mx, mz, tm, nx, nz, n_tm)
    hz = nz // 2
    peers = (lax.rem(mx + 1, nx), lax.rem(mx + nx - 1, nx))

    def owners_of(g, d):
        return pl.ds(g * nz + d * hz, hz)

    for s in range(1, nx):
        copies = []
        for d in range(2):
            g = lax.rem(mx + (s if d else nx * s - s), nx)
            if s == 1:
                src = x_ref.at[owners_of(g, d)]
            else:
                send_a[d, s - 2] = recv_a[d, s - 2] + x_ref[owners_of(g, d)]
                src = send_a.at[d, s - 2]
            copy = pltpu.make_async_remote_copy(
                src_ref=src, dst_ref=recv_a.at[d, s - 1],
                send_sem=a_send.at[d, s - 1], recv_sem=a_recv.at[d, s - 1],
                device_id=(peers[d] * nz + mz, tm), device_id_type=pl.DeviceIdType.MESH,
            )
            copy.start()
            copies.append(copy)
        for copy in copies:
            copy.wait()
    for d in range(2):
        part[d * hz : (d + 1) * hz] = recv_a[d, nx - 2] + x_ref[owners_of(mx, d)]
    copies = []
    for k in range(1, nz):
        pz = lax.rem(mz + k, nz)
        copy = pltpu.make_async_remote_copy(
            src_ref=part.at[pz], dst_ref=recv_b.at[k - 1],
            send_sem=b_send.at[k - 1], recv_sem=b_recv.at[k - 1],
            device_id=(mx * nz + pz, tm), device_id_type=pl.DeviceIdType.MESH,
        )
        copy.start()
        copies.append(copy)
    for copy in copies:
        copy.wait()
    total = part[mz]
    for k in range(1, nz):
        total = total + recv_b[k - 1]
    mine[...] = total
    copies = []
    for d, step in enumerate((1, n_tm - 1)):
        copy = pltpu.make_async_remote_copy(
            src_ref=mine, dst_ref=halo.at[d],
            send_sem=t_send.at[d], recv_sem=t_recv.at[d],
            device_id=(me, lax.rem(tm + step, n_tm)), device_id_type=pl.DeviceIdType.MESH,
        )
        copy.start()
        copies.append(copy)
    out_ref[1] = total
    for copy in copies:
        copy.wait()
    out_ref[0] = halo[0]
    out_ref[2] = halo[1]


def reduce_to_owner(x, nx, nz, n_tm):
    n, rows, w = x.shape
    hz = nz // 2
    return pl.pallas_call(
        partial(reduce_kernel, nx, nz, n_tm),
        out_shape=jax.ShapeDtypeStruct((3, rows, w), x.dtype),
        in_specs=[pl.BlockSpec(memory_space=pltpu.VMEM)],
        out_specs=pl.BlockSpec(memory_space=pltpu.VMEM),
        scratch_shapes=[
            pltpu.VMEM((2, nx - 1, hz, rows, w), x.dtype),
            pltpu.VMEM((2, nx - 2, hz, rows, w), x.dtype),
            pltpu.VMEM((nz, rows, w), x.dtype),
            pltpu.VMEM((nz - 1, rows, w), x.dtype),
            pltpu.VMEM((rows, w), x.dtype),
            pltpu.VMEM((2, rows, w), x.dtype),
            pltpu.SemaphoreType.DMA((2, nx - 1)),
            pltpu.SemaphoreType.DMA((2, nx - 1)),
            pltpu.SemaphoreType.DMA((nz - 1,)),
            pltpu.SemaphoreType.DMA((nz - 1,)),
            pltpu.SemaphoreType.DMA((2,)),
            pltpu.SemaphoreType.DMA((2,)),
        ],
        compiler_params=pltpu.CompilerParams(collective_id=0, has_side_effects=True),
    )(x)


def fill_lags(mid_ref, lhs_ref, band):
    rows = mid_ref.shape[1]
    base = mid_ref[band].astype(jnp.float32)
    for q in range(NLAG):
        lhs_ref[band, q * rows : (q + 1) * rows, :] = pltpu.roll(base, q, 1).astype(lhs_ref.dtype)
    lhs_ref[band, NLAG * rows :, :] = jnp.zeros(
        ((LAG_PAD - NLAG) * rows, lhs_ref.shape[2]), lhs_ref.dtype
    )


def fold_group(g, group, lhs_ref, gath, out_ref, spread_ref, level_ref, t_dev):
    rows = out_ref.shape[1]
    step = LAG_PAD // LAG_CHUNKS
    first = pl.multiple_of(g * group, 128)
    same = (level_ref[:, 0:1] == level_ref[:, pl.ds(pl.multiple_of(g * group + 128, 128), group)]).astype(jnp.float32)

    def one_band(band, carry):
        block = gath[band, pl.ds(first, group), :].astype(jnp.float32)
        rhs_wide = block.T
        rhs = rhs_wide.astype(jnp.bfloat16)
        middle = rhs_wide[LAG : LAG + t_dev, :]
        spread = lax.rsqrt(jnp.sum(middle * middle, axis=0, keepdims=True) / t_dev + EPSILON)
        acc = jnp.zeros((rows, group), jnp.float32)
        for h in range(LAG_CHUNKS):
            lhs = lhs_ref[band, h * step * rows : (h + 1) * step * rows, :]
            r = jnp.dot(lhs, rhs, preferred_element_type=jnp.float32)
            acc = acc + (r * r).reshape(step, rows, group).sum(axis=0)
        scale = spread_ref[band] * spread / t_dev
        out_ref[band, :, pl.ds(first, group)] = acc * (scale * scale) * same / NLAG
        return carry

    lax.fori_loop(0, out_ref.shape[0], one_band, 0)


def gather_fold_kernel(nx, nz, t_dev, own_ref, mid_ref, spread_ref, level_ref, out_ref, gath, lhs_ref,
                       a_send, a_recv, b_send, b_recv, local_sem):
    me, tm, mx, mz = mesh_peers(nx, nz)
    rows = own_ref.shape[1]
    group = nz * rows
    greet(mx, mz, tm, nx, nz)
    mine = gath.at[:, pl.ds(me * rows, rows), :]
    own = pltpu.make_async_copy(own_ref, mine, local_sem)
    own.start()
    copies = []
    for k in range(1, nz):
        copy = pltpu.make_async_remote_copy(
            src_ref=own_ref, dst_ref=mine,
            send_sem=a_send.at[k - 1], recv_sem=a_recv.at[k - 1],
            device_id=(mx * nz + lax.rem(mz + k, nz), tm), device_id_type=pl.DeviceIdType.MESH,
        )
        copy.start()
        copies.append(copy)
    for band in range(mid_ref.shape[0]):
        fill_lags(mid_ref, lhs_ref, band)
    own.wait()
    for copy in copies:
        copy.wait()
    left, right = lax.rem(mx + nx - 1, nx), lax.rem(mx + 1, nx)
    half = group // 2

    def ring_copy(start, size, peer, slot):
        rows_at = gath.at[:, pl.ds(start, size), :]
        return pltpu.make_async_remote_copy(
            src_ref=rows_at, dst_ref=rows_at,
            send_sem=b_send.at[slot], recv_sem=b_recv.at[slot],
            device_id=(peer * nz + mz, tm), device_id_type=pl.DeviceIdType.MESH,
        )

    near = [ring_copy(mx * group, group, right, 0), ring_copy(mx * group, group, left, 1)]
    for copy in near:
        copy.start()
    fold_group(mx, group, lhs_ref, gath, out_ref, spread_ref, level_ref, t_dev)
    for copy in near:
        copy.wait_recv()
    far = [ring_copy(left * group, half, right, 2), ring_copy(right * group + half, half, left, 3)]
    for copy in far:
        copy.start()
    fold_group(left, group, lhs_ref, gath, out_ref, spread_ref, level_ref, t_dev)
    fold_group(right, group, lhs_ref, gath, out_ref, spread_ref, level_ref, t_dev)
    for copy in far:
        copy.wait_recv()
    fold_group(lax.rem(mx + 2, nx), group, lhs_ref, gath, out_ref, spread_ref, level_ref, t_dev)
    for copy in near + far:
        copy.wait_send()


def gather_fold(own, mid, spread, levels, nx, nz, t_dev):
    assert nx == 4
    bands, rows, width = own.shape
    cols = nx * nz * rows
    flops = 2 * bands * LAG_PAD * rows * width * cols
    return pl.pallas_call(
        partial(gather_fold_kernel, nx, nz, t_dev),
        out_shape=jax.ShapeDtypeStruct((bands, rows, cols), jnp.float32),
        in_specs=[pl.BlockSpec(memory_space=pltpu.VMEM)] * 4,
        out_specs=pl.BlockSpec(memory_space=pltpu.VMEM),
        scratch_shapes=[
            pltpu.VMEM((bands, cols, width), own.dtype),
            pltpu.VMEM((bands, LAG_PAD * rows, width), jnp.bfloat16),
            pltpu.SemaphoreType.DMA((nz - 1,)),
            pltpu.SemaphoreType.DMA((nz - 1,)),
            pltpu.SemaphoreType.DMA((4,)),
            pltpu.SemaphoreType.DMA((4,)),
            pltpu.SemaphoreType.DMA(()),
        ],
        compiler_params=pltpu.CompilerParams(
            collective_id=1, has_side_effects=True, vmem_limit_bytes=48 * 1024 * 1024
        ),
        cost_estimate=pl.CostEstimate(
            flops=flops, bytes_accessed=2 * (own.size + mid.size) + 4 * bands * rows * cols,
            transcendentals=0,
        ),
    )(own, mid, spread, levels)


def pool_kernel(par_dev, per_step, ids_ref, env_ref, out_ref):
    rows = out_ref.shape[1]
    r = lax.broadcasted_iota(jnp.int32, (rows, 1), 0)
    env = env_ref[...]
    for o in range(per_step):
        wanted = jnp.where(r < par_dev, (pl.program_id(0) * per_step + o) * par_dev + r, -1)
        hits = (ids_ref[0] == wanted).astype(jnp.float32)
        for level in range(1, ids_ref.shape[0]):
            hits = hits + (ids_ref[level] == wanted).astype(jnp.float32)
        out_ref[o] = jnp.dot(hits.astype(jnp.bfloat16), env, preferred_element_type=jnp.float32)


def pool(global_ids, flat_env, owners, par_dev):
    levels, vertices = global_ids.shape
    width = flat_env.shape[1]
    per_step = 4
    return pl.pallas_call(
        partial(pool_kernel, par_dev, per_step),
        out_shape=jax.ShapeDtypeStruct((owners, ROW_PAD, width), jnp.float32),
        grid=(owners // per_step,),
        in_specs=[
            pl.BlockSpec((levels, 1, vertices), lambda k: (0, 0, 0)),
            pl.BlockSpec((vertices, width), lambda k: (0, 0)),
        ],
        out_specs=pl.BlockSpec((per_step, ROW_PAD, width), lambda k: (k, 0, 0)),
        cost_estimate=pl.CostEstimate(
            flops=2 * owners * ROW_PAD * vertices * width,
            bytes_accessed=4 * levels * vertices + 2 * vertices * width + 4 * owners * ROW_PAD * width,
            transcendentals=0,
        ),
    )(global_ids.reshape(levels, 1, vertices), flat_env)


def local(source, band_taps, smooth_taps, parcel_ids):
    vert_dev, t_dev = source.shape
    owners = lax.axis_size("vert")
    total_par = (P1 + P2 + P3 + owners - 1) // owners * owners
    par_dev = total_par // owners
    n_mid = t_dev + 2 * HALF
    n_in = t_dev + 4 * HALF
    first_rows = jax.vmap(partial(toeplitz_band, n_out=n_mid, n_in=n_in))(
        band_taps.reshape(2 * BANDS, TAPS)
    )
    first_mat = first_rows.transpose(2, 0, 1).reshape(n_in, 2 * BANDS * n_mid)
    second_rows = jax.vmap(partial(toeplitz_band, n_out=t_dev, n_in=n_mid))(smooth_taps)
    second_mat = second_rows.transpose(0, 2, 1)
    widened = extended_2(source, (("tm", 1),), 2 * HALF)
    block_rows = math.gcd(vert_dev, 128)

    def filter_block(block):
        wave = jnp.dot(block, first_mat, preferred_element_type=jnp.float32).reshape(
            block_rows, 2, BANDS, n_mid
        )
        power = (wave[:, 0] * wave[:, 0] + wave[:, 1] * wave[:, 1]).astype(jnp.bfloat16)
        return jnp.einsum(
            "vbu,but->vbt", power, second_mat, preferred_element_type=jnp.float32
        ).astype(jnp.bfloat16)

    envelope = lax.map(filter_block, widened.reshape(vert_dev // block_rows, block_rows, n_in))
    flat_env = envelope.reshape(vert_dev, BANDS * t_dev)
    offsets = jnp.array([0, P1, P1 + P2], dtype=jnp.int32)
    global_ids = parcel_ids + offsets[:, None]
    owner_start = lax.axis_index("vert") * par_dev

    pooled = pool(global_ids, flat_env, owners, par_dev)
    nx = owners // VERT_MINOR
    n_tm = lax.axis_size("tm")
    tm = lax.axis_index("tm")
    sums3 = reduce_to_owner(pooled, nx, VERT_MINOR, n_tm)[:, :par_dev].reshape(3, par_dev, BANDS, t_dev)
    before = jnp.where(tm > 0, sums3[0, :, :, t_dev - LAG :], 0.0)
    after = jnp.where(tm < n_tm - 1, sums3[2, :, :, :LAG], 0.0)
    own_ext = jnp.concatenate([before, sums3[1], after], axis=2)
    centered, own_middle, own_spread = centered_rows(own_ext, t_dev)

    own = jnp.pad(centered.transpose(1, 0, 2), ((0, 0), (0, ROW_PAD - par_dev), (0, 0)))
    mid = jnp.pad(
        own_middle.transpose(1, 0, 2), ((0, 0), (0, ROW_PAD - par_dev), (0, t_dev))
    )
    spread = jnp.pad(own_spread.T, ((0, 0), (0, ROW_PAD - par_dev)))[:, :, None]
    r = lax.iota(jnp.int32, ROW_PAD)
    own_level = jnp.where(
        r < par_dev, resolution_of(owner_start + r), -2
    ).astype(jnp.float32)
    own_level = jnp.where(own_level < 3, own_level, -2.0)
    col = lax.iota(jnp.int32, owners * ROW_PAD)
    col_level = jnp.where(
        col % ROW_PAD < par_dev, resolution_of(col // ROW_PAD * par_dev + col % ROW_PAD), -1
    ).astype(jnp.float32)
    levels = jnp.concatenate(
        [jnp.broadcast_to(own_level[:, None], (ROW_PAD, 128)),
         jnp.broadcast_to(col_level[None, :], (ROW_PAD, owners * ROW_PAD))], axis=1
    )
    padded = gather_fold(own, mid, spread, levels, nx, VERT_MINOR, t_dev)
    coupling = padded.reshape(BANDS, ROW_PAD, owners, ROW_PAD)[:, :par_dev, :, :par_dev]
    coupling = coupling.reshape(BANDS, par_dev, total_par)
    return coupling[None]


def solution(mesh):
    return jax.shard_map(
        local,
        mesh=mesh,
        in_specs=(P("vert", "tm"), P(), P(), P(None, "vert")),
        out_specs=P("tm", None, "vert", None),
        check_vma=False,
    )
```

```python
from functools import partial

import jax
import jax.numpy as jnp
from jax import lax
from jax.experimental import pallas as pl
from jax.experimental.pallas import tpu as pltpu
from jax.sharding import PartitionSpec as P

P1 = 100
P2 = 400
P3 = 1000
BANDS = 2
TAPS = 65
HALF = 32
LAG = 64
LAG_STEP = 1
NLAG = 129

EPSILON = 1e-05

ROW_PAD = 96
LAG_CHUNKS = 11
LAG_PAD = 132
VERT_MINOR = 4


def extended_2(cells, sides, width):
    for axis, dim in sides:
        count = lax.axis_size(axis)
        ends = count - 1
        head = lax.slice_in_dim(cells, 0, width, axis=dim)
        tail = lax.slice_in_dim(cells, cells.shape[dim] - width, cells.shape[dim], axis=dim)
        cells = jnp.concatenate(
            [
                lax.ppermute(tail, axis, [(i, (i + 1) % count) for i in range(ends)]),
                cells,
                lax.ppermute(head, axis, [((i + 1) % count, i) for i in range(ends)]),
            ],
            axis=dim,
        )
    return cells


def toeplitz_band(taps, n_out, n_in):
    period = jnp.concatenate([taps, jnp.zeros((n_in + 1 - taps.shape[0],), taps.dtype)])
    return jnp.tile(period, n_out)[: n_out * n_in].reshape(n_out, n_in)


def resolution_of(parcel):
    first = (parcel >= P1).astype(jnp.int32)
    second = (parcel >= P1 + P2).astype(jnp.int32)
    third = (parcel >= P1 + P2 + P3).astype(jnp.int32)
    return first + second + third


def centered_rows(extended, length):
    level_mean = jnp.mean(extended[:, :, LAG : LAG + length], axis=2, keepdims=True)
    centered = (extended - level_mean).astype(jnp.bfloat16)
    middle = centered[:, :, LAG : LAG + length]
    middle_wide = middle.astype(jnp.float32)
    spread = lax.rsqrt(jnp.mean(middle_wide * middle_wide, axis=2) + EPSILON)
    return (centered, middle, spread)


def mesh_peers(nx, nz):
    me = lax.axis_index("vert")
    tm = lax.axis_index("tm")
    mx, mz = me // nz, me % nz
    return me, tm, mx, mz


def greet(mx, mz, tm, nx, nz, n_tm=0):
    barrier = pltpu.get_barrier_semaphore()
    me = mx * nz + mz
    peers = [(lax.rem(mx + k, nx) * nz + mz, tm) for k in range(1, nx)]
    peers += [(mx * nz + lax.rem(mz + k, nz), tm) for k in range(1, nz)]
    if n_tm:
        peers += [(me, lax.rem(tm + 1, n_tm)), (me, lax.rem(tm + n_tm - 1, n_tm))]
    for peer in peers:
        pl.semaphore_signal(barrier, inc=1, device_id=peer, device_id_type=pl.DeviceIdType.MESH)
    pl.semaphore_wait(barrier, len(peers))


def reduce_kernel(nx, nz, n_tm, x_ref, out_ref, recv_a, send_a, part, recv_b, mine, halo, a_send, a_recv,
                  b_send, b_recv, t_send, t_recv):
    me, tm, mx, mz = mesh_peers(nx, nz)
    greet(mx, mz, tm, nx, nz, n_tm)
    hz = nz // 2
    peers = (lax.rem(mx + 1, nx), lax.rem(mx + nx - 1, nx))

    def owners_of(g, d):
        return pl.ds(g * nz + d * hz, hz)

    for s in range(1, nx):
        copies = []
        for d in range(2):
            g = lax.rem(mx + (s if d else nx * s - s), nx)
            if s == 1:
                src = x_ref.at[owners_of(g, d)]
            else:
                send_a[d, s - 2] = recv_a[d, s - 2] + x_ref[owners_of(g, d)]
                src = send_a.at[d, s - 2]
            copy = pltpu.make_async_remote_copy(
                src_ref=src, dst_ref=recv_a.at[d, s - 1],
                send_sem=a_send.at[d, s - 1], recv_sem=a_recv.at[d, s - 1],
                device_id=(peers[d] * nz + mz, tm), device_id_type=pl.DeviceIdType.MESH,
            )
            copy.start()
            copies.append(copy)
        for copy in copies:
            copy.wait()
    for d in range(2):
        part[d * hz : (d + 1) * hz] = recv_a[d, nx - 2] + x_ref[owners_of(mx, d)]
    copies = []
    for k in range(1, nz):
        pz = lax.rem(mz + k, nz)
        copy = pltpu.make_async_remote_copy(
            src_ref=part.at[pz], dst_ref=recv_b.at[k - 1],
            send_sem=b_send.at[k - 1], recv_sem=b_recv.at[k - 1],
            device_id=(mx * nz + pz, tm), device_id_type=pl.DeviceIdType.MESH,
        )
        copy.start()
        copies.append(copy)
    for copy in copies:
        copy.wait()
    total = part[mz]
    for k in range(1, nz):
        total = total + recv_b[k - 1]
    mine[...] = total
    copies = []
    for d, step in enumerate((1, n_tm - 1)):
        copy = pltpu.make_async_remote_copy(
            src_ref=mine, dst_ref=halo.at[d],
            send_sem=t_send.at[d], recv_sem=t_recv.at[d],
            device_id=(me, lax.rem(tm + step, n_tm)), device_id_type=pl.DeviceIdType.MESH,
        )
        copy.start()
        copies.append(copy)
    out_ref[1] = total
    for copy in copies:
        copy.wait()
    out_ref[0] = halo[0]
    out_ref[2] = halo[1]


def reduce_to_owner(x, nx, nz, n_tm):
    n, rows, w = x.shape
    hz = nz // 2
    return pl.pallas_call(
        partial(reduce_kernel, nx, nz, n_tm),
        out_shape=jax.ShapeDtypeStruct((3, rows, w), x.dtype),
        in_specs=[pl.BlockSpec(memory_space=pltpu.VMEM)],
        out_specs=pl.BlockSpec(memory_space=pltpu.VMEM),
        scratch_shapes=[
            pltpu.VMEM((2, nx - 1, hz, rows, w), x.dtype),
            pltpu.VMEM((2, nx - 2, hz, rows, w), x.dtype),
            pltpu.VMEM((nz, rows, w), x.dtype),
            pltpu.VMEM((nz - 1, rows, w), x.dtype),
            pltpu.VMEM((rows, w), x.dtype),
            pltpu.VMEM((2, rows, w), x.dtype),
            pltpu.SemaphoreType.DMA((2, nx - 1)),
            pltpu.SemaphoreType.DMA((2, nx - 1)),
            pltpu.SemaphoreType.DMA((nz - 1,)),
            pltpu.SemaphoreType.DMA((nz - 1,)),
            pltpu.SemaphoreType.DMA((2,)),
            pltpu.SemaphoreType.DMA((2,)),
        ],
        compiler_params=pltpu.CompilerParams(collective_id=0, has_side_effects=True),
    )(x)


def fill_lags(mid_ref, lhs_ref, band):
    rows = mid_ref.shape[1]
    base = mid_ref[band].astype(jnp.float32)
    for q in range(NLAG):
        lhs_ref[band, q * rows : (q + 1) * rows, :] = pltpu.roll(base, q, 1).astype(lhs_ref.dtype)
    lhs_ref[band, NLAG * rows :, :] = jnp.zeros(
        ((LAG_PAD - NLAG) * rows, lhs_ref.shape[2]), lhs_ref.dtype
    )


def fold_group(g, group, lhs_ref, gath, out_ref, spread_ref, level_ref, t_dev):
    rows = out_ref.shape[1]
    step = LAG_PAD // LAG_CHUNKS
    first = pl.multiple_of(g * group, 128)
    same = (level_ref[:, 0:1] == level_ref[:, pl.ds(pl.multiple_of(g * group + 128, 128), group)]).astype(jnp.float32)

    def one_band(band, carry):
        block = gath[band, pl.ds(first, group), :].astype(jnp.float32)
        rhs_wide = block.T
        rhs = rhs_wide.astype(jnp.bfloat16)
        middle = rhs_wide[LAG : LAG + t_dev, :]
        spread = lax.rsqrt(jnp.sum(middle * middle, axis=0, keepdims=True) / t_dev + EPSILON)
        acc = jnp.zeros((rows, group), jnp.float32)
        for h in range(LAG_CHUNKS):
            lhs = lhs_ref[band, h * step * rows : (h + 1) * step * rows, :]
            r = jnp.dot(lhs, rhs, preferred_element_type=jnp.float32)
            acc = acc + (r * r).reshape(step, rows, group).sum(axis=0)
        scale = spread_ref[band] * spread / t_dev
        out_ref[band, :, pl.ds(first, group)] = acc * (scale * scale) * same / NLAG
        return carry

    lax.fori_loop(0, out_ref.shape[0], one_band, 0)


def gather_fold_kernel(nx, nz, t_dev, own_ref, mid_ref, spread_ref, level_ref, out_ref, gath, lhs_ref,
                       a_send, a_recv, b_send, b_recv, local_sem):
    me, tm, mx, mz = mesh_peers(nx, nz)
    rows = own_ref.shape[1]
    group = nz * rows
    greet(mx, mz, tm, nx, nz)
    mine = gath.at[:, pl.ds(me * rows, rows), :]
    own = pltpu.make_async_copy(own_ref, mine, local_sem)
    own.start()
    copies = []
    for k in range(1, nz):
        copy = pltpu.make_async_remote_copy(
            src_ref=own_ref, dst_ref=mine,
            send_sem=a_send.at[k - 1], recv_sem=a_recv.at[k - 1],
            device_id=(mx * nz + lax.rem(mz + k, nz), tm), device_id_type=pl.DeviceIdType.MESH,
        )
        copy.start()
        copies.append(copy)
    for band in range(mid_ref.shape[0]):
        fill_lags(mid_ref, lhs_ref, band)
    own.wait()
    for copy in copies:
        copy.wait()
    left, right = lax.rem(mx + nx - 1, nx), lax.rem(mx + 1, nx)
    half = group // 2

    def ring_copy(start, size, peer, slot):
        rows_at = gath.at[:, pl.ds(start, size), :]
        return pltpu.make_async_remote_copy(
            src_ref=rows_at, dst_ref=rows_at,
            send_sem=b_send.at[slot], recv_sem=b_recv.at[slot],
            device_id=(peer * nz + mz, tm), device_id_type=pl.DeviceIdType.MESH,
        )

    near = [ring_copy(mx * group, group, right, 0), ring_copy(mx * group, group, left, 1)]
    for copy in near:
        copy.start()
    fold_group(mx, group, lhs_ref, gath, out_ref, spread_ref, level_ref, t_dev)
    for copy in near:
        copy.wait_recv()
    far = [ring_copy(left * group, half, right, 2), ring_copy(right * group + half, half, left, 3)]
    for copy in far:
        copy.start()
    fold_group(left, group, lhs_ref, gath, out_ref, spread_ref, level_ref, t_dev)
    fold_group(right, group, lhs_ref, gath, out_ref, spread_ref, level_ref, t_dev)
    for copy in far:
        copy.wait_recv()
    fold_group(lax.rem(mx + 2, nx), group, lhs_ref, gath, out_ref, spread_ref, level_ref, t_dev)
    for copy in near + far:
        copy.wait_send()


def gather_fold(own, mid, spread, levels, nx, nz, t_dev):
    assert nx == 4
    bands, rows, width = own.shape
    cols = nx * nz * rows
    flops = 2 * bands * LAG_PAD * rows * width * cols
    return pl.pallas_call(
        partial(gather_fold_kernel, nx, nz, t_dev),
        out_shape=jax.ShapeDtypeStruct((bands, rows, cols), jnp.float32),
        in_specs=[pl.BlockSpec(memory_space=pltpu.VMEM)] * 4,
        out_specs=pl.BlockSpec(memory_space=pltpu.VMEM),
        scratch_shapes=[
            pltpu.VMEM((bands, cols, width), own.dtype),
            pltpu.VMEM((bands, LAG_PAD * rows, width), jnp.bfloat16),
            pltpu.SemaphoreType.DMA((nz - 1,)),
            pltpu.SemaphoreType.DMA((nz - 1,)),
            pltpu.SemaphoreType.DMA((4,)),
            pltpu.SemaphoreType.DMA((4,)),
            pltpu.SemaphoreType.DMA(()),
        ],
        compiler_params=pltpu.CompilerParams(
            collective_id=1, has_side_effects=True, vmem_limit_bytes=48 * 1024 * 1024
        ),
        cost_estimate=pl.CostEstimate(
            flops=flops, bytes_accessed=2 * (own.size + mid.size) + 4 * bands * rows * cols,
            transcendentals=0,
        ),
    )(own, mid, spread, levels)


def pool_kernel(par_dev, per_step, ids_ref, env_ref, out_ref):
    rows = out_ref.shape[1]
    r = lax.broadcasted_iota(jnp.int32, (rows, 1), 0)
    env = env_ref[...]
    for o in range(per_step):
        wanted = jnp.where(r < par_dev, (pl.program_id(0) * per_step + o) * par_dev + r, -1)
        hits = (ids_ref[0] == wanted).astype(jnp.float32)
        for level in range(1, ids_ref.shape[0]):
            hits = hits + (ids_ref[level] == wanted).astype(jnp.float32)
        out_ref[o] = jnp.dot(hits.astype(jnp.bfloat16), env, preferred_element_type=jnp.float32)


def pool(global_ids, flat_env, owners, par_dev):
    levels, vertices = global_ids.shape
    width = flat_env.shape[1]
    per_step = 4
    return pl.pallas_call(
        partial(pool_kernel, par_dev, per_step),
        out_shape=jax.ShapeDtypeStruct((owners, ROW_PAD, width), jnp.float32),
        grid=(owners // per_step,),
        in_specs=[
            pl.BlockSpec((levels, 1, vertices), lambda k: (0, 0, 0)),
            pl.BlockSpec((vertices, width), lambda k: (0, 0)),
        ],
        out_specs=pl.BlockSpec((per_step, ROW_PAD, width), lambda k: (k, 0, 0)),
        cost_estimate=pl.CostEstimate(
            flops=2 * owners * ROW_PAD * vertices * width,
            bytes_accessed=4 * levels * vertices + 2 * vertices * width + 4 * owners * ROW_PAD * width,
            transcendentals=0,
        ),
    )(global_ids.reshape(levels, 1, vertices), flat_env)


def local(source, band_taps, smooth_taps, parcel_ids):
    vert_dev, t_dev = source.shape
    owners = lax.axis_size("vert")
    total_par = (P1 + P2 + P3 + owners - 1) // owners * owners
    par_dev = total_par // owners
    n_mid = t_dev + 2 * HALF
    n_in = t_dev + 4 * HALF
    first_rows = jax.vmap(partial(toeplitz_band, n_out=n_mid, n_in=n_in))(
        band_taps.reshape(2 * BANDS, TAPS)
    )
    first_mat = first_rows.transpose(2, 0, 1).reshape(n_in, 2 * BANDS * n_mid)
    second_rows = jax.vmap(partial(toeplitz_band, n_out=t_dev, n_in=n_mid))(smooth_taps)
    second_mat = second_rows.transpose(0, 2, 1)
    widened = extended_2(source, (("tm", 1),), 2 * HALF)
    wave = jnp.dot(widened, first_mat, preferred_element_type=jnp.float32).reshape(
        vert_dev, 2, BANDS, n_mid
    )
    power = (wave[:, 0] * wave[:, 0] + wave[:, 1] * wave[:, 1]).astype(jnp.bfloat16)
    envelope = jnp.einsum(
        "vbu,but->vbt", power, second_mat, preferred_element_type=jnp.float32
    ).astype(jnp.bfloat16)
    flat_env = envelope.reshape(vert_dev, BANDS * t_dev)
    offsets = jnp.array([0, P1, P1 + P2], dtype=jnp.int32)
    global_ids = parcel_ids + offsets[:, None]
    owner_start = lax.axis_index("vert") * par_dev

    pooled = pool(global_ids, flat_env, owners, par_dev)
    nx = owners // VERT_MINOR
    n_tm = lax.axis_size("tm")
    tm = lax.axis_index("tm")
    sums3 = reduce_to_owner(pooled, nx, VERT_MINOR, n_tm)[:, :par_dev].reshape(3, par_dev, BANDS, t_dev)
    before = jnp.where(tm > 0, sums3[0, :, :, t_dev - LAG :], 0.0)
    after = jnp.where(tm < n_tm - 1, sums3[2, :, :, :LAG], 0.0)
    own_ext = jnp.concatenate([before, sums3[1], after], axis=2)
    centered, own_middle, own_spread = centered_rows(own_ext, t_dev)

    own = jnp.pad(centered.transpose(1, 0, 2), ((0, 0), (0, ROW_PAD - par_dev), (0, 0)))
    mid = jnp.pad(
        own_middle.transpose(1, 0, 2), ((0, 0), (0, ROW_PAD - par_dev), (0, t_dev))
    )
    spread = jnp.pad(own_spread.T, ((0, 0), (0, ROW_PAD - par_dev)))[:, :, None]
    r = lax.iota(jnp.int32, ROW_PAD)
    own_level = jnp.where(
        r < par_dev, resolution_of(owner_start + r), -2
    ).astype(jnp.float32)
    own_level = jnp.where(own_level < 3, own_level, -2.0)
    col = lax.iota(jnp.int32, owners * ROW_PAD)
    col_level = jnp.where(
        col % ROW_PAD < par_dev, resolution_of(col // ROW_PAD * par_dev + col % ROW_PAD), -1
    ).astype(jnp.float32)
    levels = jnp.concatenate(
        [jnp.broadcast_to(own_level[:, None], (ROW_PAD, 128)),
         jnp.broadcast_to(col_level[None, :], (ROW_PAD, owners * ROW_PAD))], axis=1
    )
    padded = gather_fold(own, mid, spread, levels, nx, VERT_MINOR, t_dev)
    coupling = padded.reshape(BANDS, ROW_PAD, owners, ROW_PAD)[:, :par_dev, :, :par_dev]
    coupling = coupling.reshape(BANDS, par_dev, total_par)
    return coupling[None]


def solution(mesh):
    return jax.shard_map(
        local,
        mesh=mesh,
        in_specs=(P("vert", "tm"), P(), P(), P(None, "vert")),
        out_specs=P("tm", None, "vert", None),
        check_vma=False,
    )
```

```python
from functools import partial

import jax
import jax.numpy as jnp
from jax import lax
from jax.experimental import pallas as pl
from jax.experimental.pallas import tpu as pltpu
from jax.sharding import PartitionSpec as P

P1 = 100
P2 = 400
P3 = 1000
BANDS = 2
TAPS = 65
HALF = 32
LAG = 64
LAG_STEP = 1
NLAG = 129

EPSILON = 1e-05

ROW_PAD = 96
LAG_CHUNKS = 11
LAG_PAD = 132
VERT_MINOR = 4


def extended_2(cells, sides, width):
    for axis, dim in sides:
        count = lax.axis_size(axis)
        ends = count - 1
        head = lax.slice_in_dim(cells, 0, width, axis=dim)
        tail = lax.slice_in_dim(cells, cells.shape[dim] - width, cells.shape[dim], axis=dim)
        cells = jnp.concatenate(
            [
                lax.ppermute(tail, axis, [(i, (i + 1) % count) for i in range(ends)]),
                cells,
                lax.ppermute(head, axis, [((i + 1) % count, i) for i in range(ends)]),
            ],
            axis=dim,
        )
    return cells


def toeplitz_band(taps, n_out, n_in):
    period = jnp.concatenate([taps, jnp.zeros((n_in + 1 - taps.shape[0],), taps.dtype)])
    return jnp.tile(period, n_out)[: n_out * n_in].reshape(n_out, n_in)


def resolution_of(parcel):
    first = (parcel >= P1).astype(jnp.int32)
    second = (parcel >= P1 + P2).astype(jnp.int32)
    third = (parcel >= P1 + P2 + P3).astype(jnp.int32)
    return first + second + third


def centered_rows(extended, length):
    level_mean = jnp.mean(extended[:, :, LAG : LAG + length], axis=2, keepdims=True)
    centered = (extended - level_mean).astype(jnp.bfloat16)
    middle = centered[:, :, LAG : LAG + length]
    middle_wide = middle.astype(jnp.float32)
    spread = lax.rsqrt(jnp.mean(middle_wide * middle_wide, axis=2) + EPSILON)
    return (centered, middle, spread)


def mesh_peers(nx, nz):
    me = lax.axis_index("vert")
    tm = lax.axis_index("tm")
    mx, mz = me // nz, me % nz
    return me, tm, mx, mz


def greet(mx, mz, tm, nx, nz, n_tm=0):
    barrier = pltpu.get_barrier_semaphore()
    me = mx * nz + mz
    peers = [(lax.rem(mx + k, nx) * nz + mz, tm) for k in range(1, nx)]
    peers += [(mx * nz + lax.rem(mz + k, nz), tm) for k in range(1, nz)]
    if n_tm:
        peers += [(me, lax.rem(tm + 1, n_tm)), (me, lax.rem(tm + n_tm - 1, n_tm))]
    for peer in peers:
        pl.semaphore_signal(barrier, inc=1, device_id=peer, device_id_type=pl.DeviceIdType.MESH)
    pl.semaphore_wait(barrier, len(peers))


def reduce_kernel(nx, nz, n_tm, x_ref, out_ref, recv_a, send_a, part, recv_b, mine, halo, a_send, a_recv,
                  b_send, b_recv, t_send, t_recv):
    me, tm, mx, mz = mesh_peers(nx, nz)
    greet(mx, mz, tm, nx, nz, n_tm)
    hz = nz // 2
    peers = (lax.rem(mx + 1, nx), lax.rem(mx + nx - 1, nx))

    def owners_of(g, d):
        return pl.ds(g * nz + d * hz, hz)

    for s in range(1, nx):
        copies = []
        for d in range(2):
            g = lax.rem(mx + (s if d else nx * s - s), nx)
            if s == 1:
                src = x_ref.at[owners_of(g, d)]
            else:
                send_a[d, s - 2] = recv_a[d, s - 2] + x_ref[owners_of(g, d)]
                src = send_a.at[d, s - 2]
            copy = pltpu.make_async_remote_copy(
                src_ref=src, dst_ref=recv_a.at[d, s - 1],
                send_sem=a_send.at[d, s - 1], recv_sem=a_recv.at[d, s - 1],
                device_id=(peers[d] * nz + mz, tm), device_id_type=pl.DeviceIdType.MESH,
            )
            copy.start()
            copies.append(copy)
        for copy in copies:
            copy.wait()
    for d in range(2):
        part[d * hz : (d + 1) * hz] = recv_a[d, nx - 2] + x_ref[owners_of(mx, d)]
    copies = []
    for k in range(1, nz):
        pz = lax.rem(mz + k, nz)
        copy = pltpu.make_async_remote_copy(
            src_ref=part.at[pz], dst_ref=recv_b.at[k - 1],
            send_sem=b_send.at[k - 1], recv_sem=b_recv.at[k - 1],
            device_id=(mx * nz + pz, tm), device_id_type=pl.DeviceIdType.MESH,
        )
        copy.start()
        copies.append(copy)
    for copy in copies:
        copy.wait()
    total = part[mz]
    for k in range(1, nz):
        total = total + recv_b[k - 1]
    mine[...] = total
    copies = []
    for d, step in enumerate((1, n_tm - 1)):
        copy = pltpu.make_async_remote_copy(
            src_ref=mine, dst_ref=halo.at[d],
            send_sem=t_send.at[d], recv_sem=t_recv.at[d],
            device_id=(me, lax.rem(tm + step, n_tm)), device_id_type=pl.DeviceIdType.MESH,
        )
        copy.start()
        copies.append(copy)
    out_ref[1] = total
    for copy in copies:
        copy.wait()
    out_ref[0] = halo[0]
    out_ref[2] = halo[1]


def reduce_to_owner(x, nx, nz, n_tm):
    n, rows, w = x.shape
    hz = nz // 2
    return pl.pallas_call(
        partial(reduce_kernel, nx, nz, n_tm),
        out_shape=jax.ShapeDtypeStruct((3, rows, w), x.dtype),
        in_specs=[pl.BlockSpec(memory_space=pltpu.VMEM)],
        out_specs=pl.BlockSpec(memory_space=pltpu.VMEM),
        scratch_shapes=[
            pltpu.VMEM((2, nx - 1, hz, rows, w), x.dtype),
            pltpu.VMEM((2, nx - 2, hz, rows, w), x.dtype),
            pltpu.VMEM((nz, rows, w), x.dtype),
            pltpu.VMEM((nz - 1, rows, w), x.dtype),
            pltpu.VMEM((rows, w), x.dtype),
            pltpu.VMEM((2, rows, w), x.dtype),
            pltpu.SemaphoreType.DMA((2, nx - 1)),
            pltpu.SemaphoreType.DMA((2, nx - 1)),
            pltpu.SemaphoreType.DMA((nz - 1,)),
            pltpu.SemaphoreType.DMA((nz - 1,)),
            pltpu.SemaphoreType.DMA((2,)),
            pltpu.SemaphoreType.DMA((2,)),
        ],
        compiler_params=pltpu.CompilerParams(collective_id=0, has_side_effects=True),
    )(x)


def fill_lags(mid_ref, lhs_ref, band):
    rows = mid_ref.shape[1]
    base = mid_ref[band].astype(jnp.float32)
    for q in range(NLAG):
        lhs_ref[band, q * rows : (q + 1) * rows, :] = pltpu.roll(base, q, 1).astype(lhs_ref.dtype)
    lhs_ref[band, NLAG * rows :, :] = jnp.zeros(
        ((LAG_PAD - NLAG) * rows, lhs_ref.shape[2]), lhs_ref.dtype
    )


def fold_group(g, group, lhs_ref, gath, out_ref, spread_ref, level_ref, t_dev):
    rows = lhs_ref.shape[1] // LAG_PAD
    kept = out_ref.shape[1]
    step = LAG_PAD // LAG_CHUNKS
    first = pl.multiple_of(g * group, 128)
    same = (level_ref[:, 0:1] == level_ref[:, pl.ds(pl.multiple_of(g * group + 128, 128), group)]).astype(jnp.float32)

    def one_band(band, carry):
        block = gath[band, pl.ds(first, group), :].astype(jnp.float32)
        rhs_wide = block.T
        rhs = rhs_wide.astype(jnp.bfloat16)
        middle = rhs_wide[LAG : LAG + t_dev, :]
        spread = lax.rsqrt(jnp.sum(middle * middle, axis=0, keepdims=True) / t_dev + EPSILON)
        acc = jnp.zeros((rows, group), jnp.float32)
        for h in range(LAG_CHUNKS):
            lhs = lhs_ref[band, h * step * rows : (h + 1) * step * rows, :]
            r = jnp.dot(lhs, rhs, preferred_element_type=jnp.float32)
            acc = acc + (r * r).reshape(step, rows, group).sum(axis=0)
        scale = spread_ref[band] * spread / t_dev
        out_ref[band, :, pl.ds(first, group)] = (acc * (scale * scale) * same / NLAG)[:kept]
        return carry

    lax.fori_loop(0, out_ref.shape[0], one_band, 0)


def gather_fold_kernel(nx, nz, t_dev, own_ref, mid_ref, spread_ref, level_ref, out_ref, gath, lhs_ref,
                       a_send, a_recv, b_send, b_recv, local_sem):
    me, tm, mx, mz = mesh_peers(nx, nz)
    rows = own_ref.shape[1]
    group = nz * rows
    greet(mx, mz, tm, nx, nz)
    mine = gath.at[:, pl.ds(me * rows, rows), :]
    own = pltpu.make_async_copy(own_ref, mine, local_sem)
    own.start()
    copies = []
    for k in range(1, nz):
        copy = pltpu.make_async_remote_copy(
            src_ref=own_ref, dst_ref=mine,
            send_sem=a_send.at[k - 1], recv_sem=a_recv.at[k - 1],
            device_id=(mx * nz + lax.rem(mz + k, nz), tm), device_id_type=pl.DeviceIdType.MESH,
        )
        copy.start()
        copies.append(copy)
    for band in range(mid_ref.shape[0]):
        fill_lags(mid_ref, lhs_ref, band)
    own.wait()
    for copy in copies:
        copy.wait()
    left, right = lax.rem(mx + nx - 1, nx), lax.rem(mx + 1, nx)
    half = group // 2

    def ring_copy(start, size, peer, slot):
        rows_at = gath.at[:, pl.ds(start, size), :]
        return pltpu.make_async_remote_copy(
            src_ref=rows_at, dst_ref=rows_at,
            send_sem=b_send.at[slot], recv_sem=b_recv.at[slot],
            device_id=(peer * nz + mz, tm), device_id_type=pl.DeviceIdType.MESH,
        )

    near = [ring_copy(mx * group, group, right, 0), ring_copy(mx * group, group, left, 1)]
    for copy in near:
        copy.start()
    fold_group(mx, group, lhs_ref, gath, out_ref, spread_ref, level_ref, t_dev)
    for copy in near:
        copy.wait_recv()
    far = [ring_copy(left * group, half, right, 2), ring_copy(right * group + half, half, left, 3)]
    for copy in far:
        copy.start()
    fold_group(left, group, lhs_ref, gath, out_ref, spread_ref, level_ref, t_dev)
    fold_group(right, group, lhs_ref, gath, out_ref, spread_ref, level_ref, t_dev)
    for copy in far:
        copy.wait_recv()
    fold_group(lax.rem(mx + 2, nx), group, lhs_ref, gath, out_ref, spread_ref, level_ref, t_dev)
    for copy in near + far:
        copy.wait_send()


def gather_fold(own, mid, spread, levels, nx, nz, t_dev, kept):
    assert nx == 4
    bands, rows, width = own.shape
    cols = nx * nz * rows
    flops = 2 * bands * LAG_PAD * rows * width * cols
    return pl.pallas_call(
        partial(gather_fold_kernel, nx, nz, t_dev),
        out_shape=jax.ShapeDtypeStruct((bands, kept, cols), jnp.float32),
        in_specs=[pl.BlockSpec(memory_space=pltpu.VMEM)] * 4,
        out_specs=pl.BlockSpec(memory_space=pltpu.VMEM),
        scratch_shapes=[
            pltpu.VMEM((bands, cols, width), own.dtype),
            pltpu.VMEM((bands, LAG_PAD * rows, width), jnp.bfloat16),
            pltpu.SemaphoreType.DMA((nz - 1,)),
            pltpu.SemaphoreType.DMA((nz - 1,)),
            pltpu.SemaphoreType.DMA((4,)),
            pltpu.SemaphoreType.DMA((4,)),
            pltpu.SemaphoreType.DMA(()),
        ],
        compiler_params=pltpu.CompilerParams(
            collective_id=1, has_side_effects=True, vmem_limit_bytes=48 * 1024 * 1024
        ),
        cost_estimate=pl.CostEstimate(
            flops=flops, bytes_accessed=2 * (own.size + mid.size) + 4 * bands * rows * cols,
            transcendentals=0,
        ),
    )(own, mid, spread, levels)


def pool_kernel(par_dev, per_step, ids_ref, env_ref, out_ref):
    rows = out_ref.shape[1]
    r = lax.broadcasted_iota(jnp.int32, (rows, 1), 0)
    env = env_ref[...]
    for o in range(per_step):
        wanted = jnp.where(r < par_dev, (pl.program_id(0) * per_step + o) * par_dev + r, -1)
        hits = (ids_ref[0] == wanted).astype(jnp.float32)
        for level in range(1, ids_ref.shape[0]):
            hits = hits + (ids_ref[level] == wanted).astype(jnp.float32)
        out_ref[o] = jnp.dot(hits.astype(jnp.bfloat16), env, preferred_element_type=jnp.float32)


def pool(global_ids, flat_env, owners, par_dev):
    levels, vertices = global_ids.shape
    width = flat_env.shape[1]
    per_step = 4
    return pl.pallas_call(
        partial(pool_kernel, par_dev, per_step),
        out_shape=jax.ShapeDtypeStruct((owners, ROW_PAD, width), jnp.float32),
        grid=(owners // per_step,),
        in_specs=[
            pl.BlockSpec((levels, 1, vertices), lambda k: (0, 0, 0)),
            pl.BlockSpec((vertices, width), lambda k: (0, 0)),
        ],
        out_specs=pl.BlockSpec((per_step, ROW_PAD, width), lambda k: (k, 0, 0)),
        cost_estimate=pl.CostEstimate(
            flops=2 * owners * ROW_PAD * vertices * width,
            bytes_accessed=4 * levels * vertices + 2 * vertices * width + 4 * owners * ROW_PAD * width,
            transcendentals=0,
        ),
    )(global_ids.reshape(levels, 1, vertices), flat_env)


def local(source, band_taps, smooth_taps, parcel_ids):
    vert_dev, t_dev = source.shape
    owners = lax.axis_size("vert")
    total_par = (P1 + P2 + P3 + owners - 1) // owners * owners
    par_dev = total_par // owners
    n_mid = t_dev + 2 * HALF
    n_in = t_dev + 4 * HALF
    first_rows = jax.vmap(partial(toeplitz_band, n_out=n_mid, n_in=n_in))(
        band_taps.reshape(2 * BANDS, TAPS)
    )
    first_mat = first_rows.transpose(2, 0, 1).reshape(n_in, 2 * BANDS * n_mid)
    second_rows = jax.vmap(partial(toeplitz_band, n_out=t_dev, n_in=n_mid))(smooth_taps)
    second_mat = second_rows.transpose(0, 2, 1)
    widened = extended_2(source, (("tm", 1),), 2 * HALF)
    wave = jnp.dot(widened, first_mat, preferred_element_type=jnp.float32).reshape(
        vert_dev, 2, BANDS, n_mid
    )
    power = (wave[:, 0] * wave[:, 0] + wave[:, 1] * wave[:, 1]).astype(jnp.bfloat16)
    envelope = jnp.einsum(
        "vbu,but->vbt", power, second_mat, preferred_element_type=jnp.float32
    ).astype(jnp.bfloat16)
    flat_env = envelope.reshape(vert_dev, BANDS * t_dev)
    offsets = jnp.array([0, P1, P1 + P2], dtype=jnp.int32)
    global_ids = parcel_ids + offsets[:, None]
    owner_start = lax.axis_index("vert") * par_dev

    pooled = pool(global_ids, flat_env, owners, par_dev)
    nx = owners // VERT_MINOR
    n_tm = lax.axis_size("tm")
    tm = lax.axis_index("tm")
    sums3 = reduce_to_owner(pooled, nx, VERT_MINOR, n_tm)[:, :par_dev].reshape(3, par_dev, BANDS, t_dev)
    before = jnp.where(tm > 0, sums3[0, :, :, t_dev - LAG :], 0.0)
    after = jnp.where(tm < n_tm - 1, sums3[2, :, :, :LAG], 0.0)
    own_ext = jnp.concatenate([before, sums3[1], after], axis=2)
    centered, own_middle, own_spread = centered_rows(own_ext, t_dev)

    own = jnp.pad(centered.transpose(1, 0, 2), ((0, 0), (0, ROW_PAD - par_dev), (0, 0)))
    mid = jnp.pad(
        own_middle.transpose(1, 0, 2), ((0, 0), (0, ROW_PAD - par_dev), (0, t_dev))
    )
    spread = jnp.pad(own_spread.T, ((0, 0), (0, ROW_PAD - par_dev)))[:, :, None]
    r = lax.iota(jnp.int32, ROW_PAD)
    own_level = jnp.where(
        r < par_dev, resolution_of(owner_start + r), -2
    ).astype(jnp.float32)
    own_level = jnp.where(own_level < 3, own_level, -2.0)
    col = lax.iota(jnp.int32, owners * ROW_PAD)
    col_level = jnp.where(
        col % ROW_PAD < par_dev, resolution_of(col // ROW_PAD * par_dev + col % ROW_PAD), -1
    ).astype(jnp.float32)
    levels = jnp.concatenate(
        [jnp.broadcast_to(own_level[:, None], (ROW_PAD, 128)),
         jnp.broadcast_to(col_level[None, :], (ROW_PAD, owners * ROW_PAD))], axis=1
    )
    padded = gather_fold(own, mid, spread, levels, nx, VERT_MINOR, t_dev, par_dev)
    coupling = padded.reshape(BANDS, par_dev, owners, ROW_PAD)[:, :, :, :par_dev]
    coupling = coupling.reshape(BANDS, par_dev, total_par)
    return coupling[None]


def solution(mesh):
    return jax.shard_map(
        local,
        mesh=mesh,
        in_specs=(P("vert", "tm"), P(), P(), P(None, "vert")),
        out_specs=P("tm", None, "vert", None),
        check_vma=False,
    )
```

```python
from functools import partial

import jax
import jax.numpy as jnp
from jax import lax
from jax.experimental import pallas as pl
from jax.experimental.pallas import tpu as pltpu
from jax.sharding import PartitionSpec as P

P1 = 100
P2 = 400
P3 = 1000
BANDS = 2
TAPS = 65
HALF = 32
LAG = 64
LAG_STEP = 1
NLAG = 129

EPSILON = 1e-05

ROW_PAD = 96
LAG_CHUNKS = 11
LAG_PAD = 132
VERT_MINOR = 4


def extended_2(cells, sides, width):
    for axis, dim in sides:
        count = lax.axis_size(axis)
        ends = count - 1
        head = lax.slice_in_dim(cells, 0, width, axis=dim)
        tail = lax.slice_in_dim(cells, cells.shape[dim] - width, cells.shape[dim], axis=dim)
        cells = jnp.concatenate(
            [
                lax.ppermute(tail, axis, [(i, (i + 1) % count) for i in range(ends)]),
                cells,
                lax.ppermute(head, axis, [((i + 1) % count, i) for i in range(ends)]),
            ],
            axis=dim,
        )
    return cells


def toeplitz_band(taps, n_out, n_in):
    period = jnp.concatenate([taps, jnp.zeros((n_in + 1 - taps.shape[0],), taps.dtype)])
    return jnp.tile(period, n_out)[: n_out * n_in].reshape(n_out, n_in)


def resolution_of(parcel):
    first = (parcel >= P1).astype(jnp.int32)
    second = (parcel >= P1 + P2).astype(jnp.int32)
    third = (parcel >= P1 + P2 + P3).astype(jnp.int32)
    return first + second + third


def centered_rows(extended, length):
    level_mean = jnp.mean(extended[:, :, LAG : LAG + length], axis=2, keepdims=True)
    centered = (extended - level_mean).astype(jnp.bfloat16)
    middle = centered[:, :, LAG : LAG + length]
    middle_wide = middle.astype(jnp.float32)
    spread = lax.rsqrt(jnp.mean(middle_wide * middle_wide, axis=2) + EPSILON)
    return (centered, middle, spread)


def mesh_peers(nx, nz):
    me = lax.axis_index("vert")
    tm = lax.axis_index("tm")
    mx, mz = me // nz, me % nz
    return me, tm, mx, mz


def greet(mx, mz, tm, nx, nz, n_tm=0):
    barrier = pltpu.get_barrier_semaphore()
    me = mx * nz + mz
    peers = [(lax.rem(mx + k, nx) * nz + mz, tm) for k in range(1, nx)]
    peers += [(mx * nz + lax.rem(mz + k, nz), tm) for k in range(1, nz)]
    if n_tm:
        peers += [(me, lax.rem(tm + 1, n_tm)), (me, lax.rem(tm + n_tm - 1, n_tm))]
    for peer in peers:
        pl.semaphore_signal(barrier, inc=1, device_id=peer, device_id_type=pl.DeviceIdType.MESH)
    pl.semaphore_wait(barrier, len(peers))


def reduce_kernel(nx, nz, n_tm, x_ref, out_ref, recv_a, send_a, part, recv_b, mine, halo, a_send, a_recv,
                  b_send, b_recv, t_send, t_recv):
    me, tm, mx, mz = mesh_peers(nx, nz)
    greet(mx, mz, tm, nx, nz, n_tm)
    hz = nz // 2
    peers = (lax.rem(mx + 1, nx), lax.rem(mx + nx - 1, nx))

    def owners_of(g, d):
        return pl.ds(g * nz + d * hz, hz)

    for s in range(1, nx):
        copies = []
        for d in range(2):
            g = lax.rem(mx + (s if d else nx * s - s), nx)
            if s == 1:
                src = x_ref.at[owners_of(g, d)]
            else:
                send_a[d, s - 2] = recv_a[d, s - 2] + x_ref[owners_of(g, d)]
                src = send_a.at[d, s - 2]
            copy = pltpu.make_async_remote_copy(
                src_ref=src, dst_ref=recv_a.at[d, s - 1],
                send_sem=a_send.at[d, s - 1], recv_sem=a_recv.at[d, s - 1],
                device_id=(peers[d] * nz + mz, tm), device_id_type=pl.DeviceIdType.MESH,
            )
            copy.start()
            copies.append(copy)
        for copy in copies:
            copy.wait()
    for d in range(2):
        part[d * hz : (d + 1) * hz] = recv_a[d, nx - 2] + x_ref[owners_of(mx, d)]
    copies = []
    for k in range(1, nz):
        pz = lax.rem(mz + k, nz)
        copy = pltpu.make_async_remote_copy(
            src_ref=part.at[pz], dst_ref=recv_b.at[k - 1],
            send_sem=b_send.at[k - 1], recv_sem=b_recv.at[k - 1],
            device_id=(mx * nz + pz, tm), device_id_type=pl.DeviceIdType.MESH,
        )
        copy.start()
        copies.append(copy)
    for copy in copies:
        copy.wait()
    total = part[mz]
    for k in range(1, nz):
        total = total + recv_b[k - 1]
    mine[...] = total
    copies = []
    for d, step in enumerate((1, n_tm - 1)):
        copy = pltpu.make_async_remote_copy(
            src_ref=mine, dst_ref=halo.at[d],
            send_sem=t_send.at[d], recv_sem=t_recv.at[d],
            device_id=(me, lax.rem(tm + step, n_tm)), device_id_type=pl.DeviceIdType.MESH,
        )
        copy.start()
        copies.append(copy)
    out_ref[1] = total
    for copy in copies:
        copy.wait()
    out_ref[0] = halo[0]
    out_ref[2] = halo[1]


def reduce_to_owner(x, nx, nz, n_tm):
    n, rows, w = x.shape
    hz = nz // 2
    return pl.pallas_call(
        partial(reduce_kernel, nx, nz, n_tm),
        out_shape=jax.ShapeDtypeStruct((3, rows, w), x.dtype),
        in_specs=[pl.BlockSpec(memory_space=pltpu.VMEM)],
        out_specs=pl.BlockSpec(memory_space=pltpu.VMEM),
        scratch_shapes=[
            pltpu.VMEM((2, nx - 1, hz, rows, w), x.dtype),
            pltpu.VMEM((2, nx - 2, hz, rows, w), x.dtype),
            pltpu.VMEM((nz, rows, w), x.dtype),
            pltpu.VMEM((nz - 1, rows, w), x.dtype),
            pltpu.VMEM((rows, w), x.dtype),
            pltpu.VMEM((2, rows, w), x.dtype),
            pltpu.SemaphoreType.DMA((2, nx - 1)),
            pltpu.SemaphoreType.DMA((2, nx - 1)),
            pltpu.SemaphoreType.DMA((nz - 1,)),
            pltpu.SemaphoreType.DMA((nz - 1,)),
            pltpu.SemaphoreType.DMA((2,)),
            pltpu.SemaphoreType.DMA((2,)),
        ],
        compiler_params=pltpu.CompilerParams(collective_id=0, has_side_effects=True),
    )(x)


def fill_lags(mid_ref, lhs_ref, band):
    rows = mid_ref.shape[1]
    base = mid_ref[band].astype(jnp.float32)
    for q in range(NLAG):
        lhs_ref[band, q * rows : (q + 1) * rows, :] = pltpu.roll(base, q, 1).astype(lhs_ref.dtype)
    lhs_ref[band, NLAG * rows :, :] = jnp.zeros(
        ((LAG_PAD - NLAG) * rows, lhs_ref.shape[2]), lhs_ref.dtype
    )


def fold_group(g, group, lhs_ref, gath, out_ref, spread_ref, level_ref, t_dev):
    rows = lhs_ref.shape[1] // LAG_PAD
    kept = out_ref.shape[1]
    step = LAG_PAD // LAG_CHUNKS
    first = pl.multiple_of(g * group, 128)
    same = (level_ref[:, 0:1] == level_ref[:, pl.ds(pl.multiple_of(g * group + 128, 128), group)]).astype(jnp.float32)

    def one_band(band, carry):
        block = gath[band, pl.ds(first, group), :].astype(jnp.float32)
        rhs_wide = block.T
        rhs = rhs_wide.astype(jnp.bfloat16)
        middle = rhs_wide[LAG : LAG + t_dev, :]
        spread = lax.rsqrt(jnp.sum(middle * middle, axis=0, keepdims=True) / t_dev + EPSILON)
        acc = jnp.zeros((rows, group), jnp.float32)
        for h in range(LAG_CHUNKS):
            lhs = lhs_ref[band, h * step * rows : (h + 1) * step * rows, :]
            r = jnp.dot(lhs, rhs, preferred_element_type=jnp.float32)
            acc = acc + (r * r).reshape(step, rows, group).sum(axis=0)
        scale = spread_ref[band] * spread / t_dev
        out_ref[band, :, pl.ds(first, group)] = (acc * (scale * scale) * same / NLAG)[:kept]
        return carry

    lax.fori_loop(0, out_ref.shape[0], one_band, 0)


def gather_fold_kernel(nx, nz, t_dev, own_ref, mid_ref, spread_ref, level_ref, out_ref, gath, lhs_ref,
                       a_send, a_recv, b_send, b_recv, local_sem):
    me, tm, mx, mz = mesh_peers(nx, nz)
    rows = own_ref.shape[1]
    group = nz * rows
    greet(mx, mz, tm, nx, nz)
    mine = gath.at[:, pl.ds(me * rows, rows), :]
    own = pltpu.make_async_copy(own_ref, mine, local_sem)
    own.start()
    below, above = lax.rem(mz + nz - 1, nz), lax.rem(mz + 1, nz)

    def z_copy(src, dst, peer, slot):
        return pltpu.make_async_remote_copy(
            src_ref=src, dst_ref=dst, send_sem=a_send.at[slot], recv_sem=a_recv.at[slot],
            device_id=(mx * nz + peer, tm), device_id_type=pl.DeviceIdType.MESH,
        )

    near = [z_copy(own_ref, mine, above, 0), z_copy(own_ref, mine, below, 1)]
    for copy in near:
        copy.start()
    for band in range(mid_ref.shape[0]):
        fill_lags(mid_ref, lhs_ref, band)
    own.wait()
    for copy in near:
        copy.wait_recv()
    from_below = gath.at[pl.ds(0, 1), pl.ds((mx * nz + below) * rows, rows), :]
    from_above = gath.at[pl.ds(1, 1), pl.ds((mx * nz + above) * rows, rows), :]
    far = [z_copy(from_below, from_below, above, 2), z_copy(from_above, from_above, below, 3)]
    for copy in far:
        copy.start()
    for copy in far:
        copy.wait_recv()
    for copy in near + far:
        copy.wait_send()
    left, right = lax.rem(mx + nx - 1, nx), lax.rem(mx + 1, nx)
    half = group // 2

    def ring_copy(start, size, peer, slot):
        rows_at = gath.at[:, pl.ds(start, size), :]
        return pltpu.make_async_remote_copy(
            src_ref=rows_at, dst_ref=rows_at,
            send_sem=b_send.at[slot], recv_sem=b_recv.at[slot],
            device_id=(peer * nz + mz, tm), device_id_type=pl.DeviceIdType.MESH,
        )

    near = [ring_copy(mx * group, group, right, 0), ring_copy(mx * group, group, left, 1)]
    for copy in near:
        copy.start()
    fold_group(mx, group, lhs_ref, gath, out_ref, spread_ref, level_ref, t_dev)
    for copy in near:
        copy.wait_recv()
    far = [ring_copy(left * group, half, right, 2), ring_copy(right * group + half, half, left, 3)]
    for copy in far:
        copy.start()
    fold_group(left, group, lhs_ref, gath, out_ref, spread_ref, level_ref, t_dev)
    fold_group(right, group, lhs_ref, gath, out_ref, spread_ref, level_ref, t_dev)
    for copy in far:
        copy.wait_recv()
    fold_group(lax.rem(mx + 2, nx), group, lhs_ref, gath, out_ref, spread_ref, level_ref, t_dev)
    for copy in near + far:
        copy.wait_send()


def gather_fold(own, mid, spread, levels, nx, nz, t_dev, kept):
    assert nx == 4 and nz == 4 and own.shape[0] == 2
    bands, rows, width = own.shape
    cols = nx * nz * rows
    flops = 2 * bands * LAG_PAD * rows * width * cols
    return pl.pallas_call(
        partial(gather_fold_kernel, nx, nz, t_dev),
        out_shape=jax.ShapeDtypeStruct((bands, kept, cols), jnp.float32),
        in_specs=[pl.BlockSpec(memory_space=pltpu.VMEM)] * 4,
        out_specs=pl.BlockSpec(memory_space=pltpu.VMEM),
        scratch_shapes=[
            pltpu.VMEM((bands, cols, width), own.dtype),
            pltpu.VMEM((bands, LAG_PAD * rows, width), jnp.bfloat16),
            pltpu.SemaphoreType.DMA((4,)),
            pltpu.SemaphoreType.DMA((4,)),
            pltpu.SemaphoreType.DMA((4,)),
            pltpu.SemaphoreType.DMA((4,)),
            pltpu.SemaphoreType.DMA(()),
        ],
        compiler_params=pltpu.CompilerParams(
            collective_id=1, has_side_effects=True, vmem_limit_bytes=48 * 1024 * 1024
        ),
        cost_estimate=pl.CostEstimate(
            flops=flops, bytes_accessed=2 * (own.size + mid.size) + 4 * bands * rows * cols,
            transcendentals=0,
        ),
    )(own, mid, spread, levels)


def pool_kernel(par_dev, per_step, ids_ref, env_ref, out_ref):
    rows = out_ref.shape[1]
    r = lax.broadcasted_iota(jnp.int32, (rows, 1), 0)
    env = env_ref[...]
    for o in range(per_step):
        wanted = jnp.where(r < par_dev, (pl.program_id(0) * per_step + o) * par_dev + r, -1)
        hits = (ids_ref[0] == wanted).astype(jnp.float32)
        for level in range(1, ids_ref.shape[0]):
            hits = hits + (ids_ref[level] == wanted).astype(jnp.float32)
        out_ref[o] = jnp.dot(hits.astype(jnp.bfloat16), env, preferred_element_type=jnp.float32)


def pool(global_ids, flat_env, owners, par_dev):
    levels, vertices = global_ids.shape
    width = flat_env.shape[1]
    per_step = 4
    return pl.pallas_call(
        partial(pool_kernel, par_dev, per_step),
        out_shape=jax.ShapeDtypeStruct((owners, ROW_PAD, width), jnp.float32),
        grid=(owners // per_step,),
        in_specs=[
            pl.BlockSpec((levels, 1, vertices), lambda k: (0, 0, 0)),
            pl.BlockSpec((vertices, width), lambda k: (0, 0)),
        ],
        out_specs=pl.BlockSpec((per_step, ROW_PAD, width), lambda k: (k, 0, 0)),
        cost_estimate=pl.CostEstimate(
            flops=2 * owners * ROW_PAD * vertices * width,
            bytes_accessed=4 * levels * vertices + 2 * vertices * width + 4 * owners * ROW_PAD * width,
            transcendentals=0,
        ),
    )(global_ids.reshape(levels, 1, vertices), flat_env)


def local(source, band_taps, smooth_taps, parcel_ids):
    vert_dev, t_dev = source.shape
    owners = lax.axis_size("vert")
    total_par = (P1 + P2 + P3 + owners - 1) // owners * owners
    par_dev = total_par // owners
    n_mid = t_dev + 2 * HALF
    n_in = t_dev + 4 * HALF
    first_rows = jax.vmap(partial(toeplitz_band, n_out=n_mid, n_in=n_in))(
        band_taps.reshape(2 * BANDS, TAPS)
    )
    first_mat = first_rows.transpose(2, 0, 1).reshape(n_in, 2 * BANDS * n_mid)
    second_rows = jax.vmap(partial(toeplitz_band, n_out=t_dev, n_in=n_mid))(smooth_taps)
    second_mat = second_rows.transpose(0, 2, 1)
    widened = extended_2(source, (("tm", 1),), 2 * HALF)
    wave = jnp.dot(widened, first_mat, preferred_element_type=jnp.float32).reshape(
        vert_dev, 2, BANDS, n_mid
    )
    power = (wave[:, 0] * wave[:, 0] + wave[:, 1] * wave[:, 1]).astype(jnp.bfloat16)
    envelope = jnp.einsum(
        "vbu,but->vbt", power, second_mat, preferred_element_type=jnp.float32
    ).astype(jnp.bfloat16)
    flat_env = envelope.reshape(vert_dev, BANDS * t_dev)
    offsets = jnp.array([0, P1, P1 + P2], dtype=jnp.int32)
    global_ids = parcel_ids + offsets[:, None]
    owner_start = lax.axis_index("vert") * par_dev

    pooled = pool(global_ids, flat_env, owners, par_dev)
    nx = owners // VERT_MINOR
    n_tm = lax.axis_size("tm")
    tm = lax.axis_index("tm")
    sums3 = reduce_to_owner(pooled, nx, VERT_MINOR, n_tm)[:, :par_dev].reshape(3, par_dev, BANDS, t_dev)
    before = jnp.where(tm > 0, sums3[0, :, :, t_dev - LAG :], 0.0)
    after = jnp.where(tm < n_tm - 1, sums3[2, :, :, :LAG], 0.0)
    own_ext = jnp.concatenate([before, sums3[1], after], axis=2)
    centered, own_middle, own_spread = centered_rows(own_ext, t_dev)

    own = jnp.pad(centered.transpose(1, 0, 2), ((0, 0), (0, ROW_PAD - par_dev), (0, 0)))
    mid = jnp.pad(
        own_middle.transpose(1, 0, 2), ((0, 0), (0, ROW_PAD - par_dev), (0, t_dev))
    )
    spread = jnp.pad(own_spread.T, ((0, 0), (0, ROW_PAD - par_dev)))[:, :, None]
    r = lax.iota(jnp.int32, ROW_PAD)
    own_level = jnp.where(
        r < par_dev, resolution_of(owner_start + r), -2
    ).astype(jnp.float32)
    own_level = jnp.where(own_level < 3, own_level, -2.0)
    col = lax.iota(jnp.int32, owners * ROW_PAD)
    col_level = jnp.where(
        col % ROW_PAD < par_dev, resolution_of(col // ROW_PAD * par_dev + col % ROW_PAD), -1
    ).astype(jnp.float32)
    levels = jnp.concatenate(
        [jnp.broadcast_to(own_level[:, None], (ROW_PAD, 128)),
         jnp.broadcast_to(col_level[None, :], (ROW_PAD, owners * ROW_PAD))], axis=1
    )
    padded = gather_fold(own, mid, spread, levels, nx, VERT_MINOR, t_dev, par_dev)
    coupling = padded.reshape(BANDS, par_dev, owners, ROW_PAD)[:, :, :, :par_dev]
    coupling = coupling.reshape(BANDS, par_dev, total_par)
    return coupling[None]


def solution(mesh):
    return jax.shard_map(
        local,
        mesh=mesh,
        in_specs=(P("vert", "tm"), P(), P(), P(None, "vert")),
        out_specs=P("tm", None, "vert", None),
        check_vma=False,
    )
```

```python
from functools import partial

import jax
import jax.numpy as jnp
from jax import lax
from jax.experimental import pallas as pl
from jax.experimental.pallas import tpu as pltpu
from jax.sharding import PartitionSpec as P

P1 = 100
P2 = 400
P3 = 1000
BANDS = 2
TAPS = 65
HALF = 32
LAG = 64
LAG_STEP = 1
NLAG = 129

EPSILON = 1e-05

ROW_PAD = 96
LAG_CHUNKS = 11
LAG_PAD = 132
VERT_MINOR = 4


def extended_2(cells, sides, width):
    for axis, dim in sides:
        count = lax.axis_size(axis)
        ends = count - 1
        head = lax.slice_in_dim(cells, 0, width, axis=dim)
        tail = lax.slice_in_dim(cells, cells.shape[dim] - width, cells.shape[dim], axis=dim)
        cells = jnp.concatenate(
            [
                lax.ppermute(tail, axis, [(i, (i + 1) % count) for i in range(ends)]),
                cells,
                lax.ppermute(head, axis, [((i + 1) % count, i) for i in range(ends)]),
            ],
            axis=dim,
        )
    return cells


def toeplitz_band(taps, n_out, n_in):
    period = jnp.concatenate([taps, jnp.zeros((n_in + 1 - taps.shape[0],), taps.dtype)])
    return jnp.tile(period, n_out)[: n_out * n_in].reshape(n_out, n_in)


def resolution_of(parcel):
    first = (parcel >= P1).astype(jnp.int32)
    second = (parcel >= P1 + P2).astype(jnp.int32)
    third = (parcel >= P1 + P2 + P3).astype(jnp.int32)
    return first + second + third


def centered_rows(extended, length):
    level_mean = jnp.mean(extended[:, :, LAG : LAG + length], axis=2, keepdims=True)
    centered = (extended - level_mean).astype(jnp.bfloat16)
    middle = centered[:, :, LAG : LAG + length]
    middle_wide = middle.astype(jnp.float32)
    spread = lax.rsqrt(jnp.mean(middle_wide * middle_wide, axis=2) + EPSILON)
    return (centered, middle, spread)


def mesh_peers(nx, nz):
    me = lax.axis_index("vert")
    tm = lax.axis_index("tm")
    mx, mz = me // nz, me % nz
    return me, tm, mx, mz


def greet(mx, mz, tm, nx, nz, n_tm=0):
    barrier = pltpu.get_barrier_semaphore()
    me = mx * nz + mz
    peers = [(lax.rem(mx + k, nx) * nz + mz, tm) for k in range(1, nx)]
    peers += [(mx * nz + lax.rem(mz + k, nz), tm) for k in range(1, nz)]
    if n_tm:
        peers += [(me, lax.rem(tm + 1, n_tm)), (me, lax.rem(tm + n_tm - 1, n_tm))]
    for peer in peers:
        pl.semaphore_signal(barrier, inc=1, device_id=peer, device_id_type=pl.DeviceIdType.MESH)
    pl.semaphore_wait(barrier, len(peers))


def reduce_kernel(nx, nz, n_tm, par_dev, ids_ref, env_ref, out_ref, x_ref, recv_a, send_a, part, recv_b, mine,
                  halo, a_send, a_recv, b_send, b_recv, t_send, t_recv):
    me, tm, mx, mz = mesh_peers(nx, nz)
    greet(mx, mz, tm, nx, nz, n_tm)
    hz = nz // 2
    rows = x_ref.shape[1]
    r = lax.broadcasted_iota(jnp.int32, (rows, 1), 0)

    def pool_groups(first_offset, carry):
        def one(j, c):
            owner = lax.rem(mx + first_offset + 2 * (j // nz), nx) * nz + j % nz
            wanted = jnp.where(r < par_dev, owner * par_dev + r, -1)
            hits = (ids_ref[0] == wanted).astype(jnp.float32)
            for level in range(1, ids_ref.shape[0]):
                hits = hits + (ids_ref[level] == wanted).astype(jnp.float32)
            x_ref[owner] = jnp.dot(
                hits.astype(jnp.bfloat16), env_ref[...], preferred_element_type=jnp.float32
            )
            return c

        return lax.fori_loop(0, 2 * nz, one, carry)

    pool_groups(nx - 1, 0)
    peers = (lax.rem(mx + 1, nx), lax.rem(mx + nx - 1, nx))

    def owners_of(g, d):
        return pl.ds(g * nz + d * hz, hz)

    for s in range(1, nx):
        copies = []
        for d in range(2):
            g = lax.rem(mx + (s if d else nx * s - s), nx)
            if s == 1:
                src = x_ref.at[owners_of(g, d)]
            else:
                send_a[d, s - 2] = recv_a[d, s - 2] + x_ref[owners_of(g, d)]
                src = send_a.at[d, s - 2]
            copy = pltpu.make_async_remote_copy(
                src_ref=src, dst_ref=recv_a.at[d, s - 1],
                send_sem=a_send.at[d, s - 1], recv_sem=a_recv.at[d, s - 1],
                device_id=(peers[d] * nz + mz, tm), device_id_type=pl.DeviceIdType.MESH,
            )
            copy.start()
            copies.append(copy)
        if s == 1:
            pool_groups(2, 0)
        for copy in copies:
            copy.wait()
    for d in range(2):
        part[d * hz : (d + 1) * hz] = recv_a[d, nx - 2] + x_ref[owners_of(mx, d)]
    copies = []
    for k in range(1, nz):
        pz = lax.rem(mz + k, nz)
        copy = pltpu.make_async_remote_copy(
            src_ref=part.at[pz], dst_ref=recv_b.at[k - 1],
            send_sem=b_send.at[k - 1], recv_sem=b_recv.at[k - 1],
            device_id=(mx * nz + pz, tm), device_id_type=pl.DeviceIdType.MESH,
        )
        copy.start()
        copies.append(copy)
    for copy in copies:
        copy.wait()
    total = part[mz]
    for k in range(1, nz):
        total = total + recv_b[k - 1]
    mine[...] = total
    copies = []
    for d, step in enumerate((1, n_tm - 1)):
        copy = pltpu.make_async_remote_copy(
            src_ref=mine, dst_ref=halo.at[d],
            send_sem=t_send.at[d], recv_sem=t_recv.at[d],
            device_id=(me, lax.rem(tm + step, n_tm)), device_id_type=pl.DeviceIdType.MESH,
        )
        copy.start()
        copies.append(copy)
    out_ref[1] = total
    for copy in copies:
        copy.wait()
    out_ref[0] = halo[0]
    out_ref[2] = halo[1]


def reduce_to_owner(global_ids, flat_env, nx, nz, n_tm, par_dev):
    levels, vertices = global_ids.shape
    w = flat_env.shape[1]
    rows = ROW_PAD
    hz = nz // 2
    dtype = jnp.float32
    return pl.pallas_call(
        partial(reduce_kernel, nx, nz, n_tm, par_dev),
        out_shape=jax.ShapeDtypeStruct((3, rows, w), dtype),
        in_specs=[pl.BlockSpec(memory_space=pltpu.VMEM)] * 2,
        out_specs=pl.BlockSpec(memory_space=pltpu.VMEM),
        scratch_shapes=[
            pltpu.VMEM((nx * nz, rows, w), dtype),
            pltpu.VMEM((2, nx - 1, hz, rows, w), dtype),
            pltpu.VMEM((2, nx - 2, hz, rows, w), dtype),
            pltpu.VMEM((nz, rows, w), dtype),
            pltpu.VMEM((nz - 1, rows, w), dtype),
            pltpu.VMEM((rows, w), dtype),
            pltpu.VMEM((2, rows, w), dtype),
            pltpu.SemaphoreType.DMA((2, nx - 1)),
            pltpu.SemaphoreType.DMA((2, nx - 1)),
            pltpu.SemaphoreType.DMA((nz - 1,)),
            pltpu.SemaphoreType.DMA((nz - 1,)),
            pltpu.SemaphoreType.DMA((2,)),
            pltpu.SemaphoreType.DMA((2,)),
        ],
        compiler_params=pltpu.CompilerParams(collective_id=0, has_side_effects=True),
    )(global_ids.reshape(levels, 1, vertices), flat_env)


def fill_lags(mid_ref, lhs_ref, band):
    rows = mid_ref.shape[1]
    base = mid_ref[band].astype(jnp.float32)
    for q in range(NLAG):
        lhs_ref[band, q * rows : (q + 1) * rows, :] = pltpu.roll(base, q, 1).astype(lhs_ref.dtype)
    lhs_ref[band, NLAG * rows :, :] = jnp.zeros(
        ((LAG_PAD - NLAG) * rows, lhs_ref.shape[2]), lhs_ref.dtype
    )


def fold_group(g, group, lhs_ref, gath, out_ref, spread_ref, level_ref, t_dev):
    rows = lhs_ref.shape[1] // LAG_PAD
    kept = out_ref.shape[1]
    step = LAG_PAD // LAG_CHUNKS
    first = pl.multiple_of(g * group, 128)
    same = (level_ref[:, 0:1] == level_ref[:, pl.ds(pl.multiple_of(g * group + 128, 128), group)]).astype(jnp.float32)

    def one_band(band, carry):
        block = gath[band, pl.ds(first, group), :].astype(jnp.float32)
        rhs_wide = block.T
        rhs = rhs_wide.astype(jnp.bfloat16)
        middle = rhs_wide[LAG : LAG + t_dev, :]
        spread = lax.rsqrt(jnp.sum(middle * middle, axis=0, keepdims=True) / t_dev + EPSILON)
        acc = jnp.zeros((rows, group), jnp.float32)
        for h in range(LAG_CHUNKS):
            lhs = lhs_ref[band, h * step * rows : (h + 1) * step * rows, :]
            r = jnp.dot(lhs, rhs, preferred_element_type=jnp.float32)
            acc = acc + (r * r).reshape(step, rows, group).sum(axis=0)
        scale = spread_ref[band] * spread / t_dev
        out_ref[band, :, pl.ds(first, group)] = (acc * (scale * scale) * same / NLAG)[:kept]
        return carry

    lax.fori_loop(0, out_ref.shape[0], one_band, 0)


def gather_fold_kernel(nx, nz, t_dev, own_ref, mid_ref, spread_ref, level_ref, out_ref, gath, lhs_ref,
                       a_send, a_recv, b_send, b_recv, local_sem):
    me, tm, mx, mz = mesh_peers(nx, nz)
    rows = own_ref.shape[1]
    group = nz * rows
    greet(mx, mz, tm, nx, nz)
    mine = gath.at[:, pl.ds(me * rows, rows), :]
    own = pltpu.make_async_copy(own_ref, mine, local_sem)
    own.start()
    copies = []
    for k in range(1, nz):
        copy = pltpu.make_async_remote_copy(
            src_ref=own_ref, dst_ref=mine,
            send_sem=a_send.at[k - 1], recv_sem=a_recv.at[k - 1],
            device_id=(mx * nz + lax.rem(mz + k, nz), tm), device_id_type=pl.DeviceIdType.MESH,
        )
        copy.start()
        copies.append(copy)
    for band in range(mid_ref.shape[0]):
        fill_lags(mid_ref, lhs_ref, band)
    own.wait()
    for copy in copies:
        copy.wait()
    left, right = lax.rem(mx + nx - 1, nx), lax.rem(mx + 1, nx)
    half = group // 2

    def ring_copy(start, size, peer, slot):
        rows_at = gath.at[:, pl.ds(start, size), :]
        return pltpu.make_async_remote_copy(
            src_ref=rows_at, dst_ref=rows_at,
            send_sem=b_send.at[slot], recv_sem=b_recv.at[slot],
            device_id=(peer * nz + mz, tm), device_id_type=pl.DeviceIdType.MESH,
        )

    near = [ring_copy(mx * group, group, right, 0), ring_copy(mx * group, group, left, 1)]
    for copy in near:
        copy.start()
    fold_group(mx, group, lhs_ref, gath, out_ref, spread_ref, level_ref, t_dev)
    for copy in near:
        copy.wait_recv()
    far = [ring_copy(left * group, half, right, 2), ring_copy(right * group + half, half, left, 3)]
    for copy in far:
        copy.start()
    fold_group(left, group, lhs_ref, gath, out_ref, spread_ref, level_ref, t_dev)
    fold_group(right, group, lhs_ref, gath, out_ref, spread_ref, level_ref, t_dev)
    for copy in far:
        copy.wait_recv()
    fold_group(lax.rem(mx + 2, nx), group, lhs_ref, gath, out_ref, spread_ref, level_ref, t_dev)
    for copy in near + far:
        copy.wait_send()


def gather_fold(own, mid, spread, levels, nx, nz, t_dev, kept):
    assert nx == 4
    bands, rows, width = own.shape
    cols = nx * nz * rows
    flops = 2 * bands * LAG_PAD * rows * width * cols
    return pl.pallas_call(
        partial(gather_fold_kernel, nx, nz, t_dev),
        out_shape=jax.ShapeDtypeStruct((bands, kept, cols), jnp.float32),
        in_specs=[pl.BlockSpec(memory_space=pltpu.VMEM)] * 4,
        out_specs=pl.BlockSpec(memory_space=pltpu.VMEM),
        scratch_shapes=[
            pltpu.VMEM((bands, cols, width), own.dtype),
            pltpu.VMEM((bands, LAG_PAD * rows, width), jnp.bfloat16),
            pltpu.SemaphoreType.DMA((nz - 1,)),
            pltpu.SemaphoreType.DMA((nz - 1,)),
            pltpu.SemaphoreType.DMA((4,)),
            pltpu.SemaphoreType.DMA((4,)),
            pltpu.SemaphoreType.DMA(()),
        ],
        compiler_params=pltpu.CompilerParams(
            collective_id=1, has_side_effects=True, vmem_limit_bytes=48 * 1024 * 1024
        ),
        cost_estimate=pl.CostEstimate(
            flops=flops, bytes_accessed=2 * (own.size + mid.size) + 4 * bands * rows * cols,
            transcendentals=0,
        ),
    )(own, mid, spread, levels)


def local(source, band_taps, smooth_taps, parcel_ids):
    vert_dev, t_dev = source.shape
    owners = lax.axis_size("vert")
    total_par = (P1 + P2 + P3 + owners - 1) // owners * owners
    par_dev = total_par // owners
    n_mid = t_dev + 2 * HALF
    n_in = t_dev + 4 * HALF
    first_rows = jax.vmap(partial(toeplitz_band, n_out=n_mid, n_in=n_in))(
        band_taps.reshape(2 * BANDS, TAPS)
    )
    first_mat = first_rows.transpose(2, 0, 1).reshape(n_in, 2 * BANDS * n_mid)
    second_rows = jax.vmap(partial(toeplitz_band, n_out=t_dev, n_in=n_mid))(smooth_taps)
    second_mat = second_rows.transpose(0, 2, 1)
    widened = extended_2(source, (("tm", 1),), 2 * HALF)
    wave = jnp.dot(widened, first_mat, preferred_element_type=jnp.float32).reshape(
        vert_dev, 2, BANDS, n_mid
    )
    power = (wave[:, 0] * wave[:, 0] + wave[:, 1] * wave[:, 1]).astype(jnp.bfloat16)
    envelope = jnp.einsum(
        "vbu,but->vbt", power, second_mat, preferred_element_type=jnp.float32
    ).astype(jnp.bfloat16)
    flat_env = envelope.reshape(vert_dev, BANDS * t_dev)
    offsets = jnp.array([0, P1, P1 + P2], dtype=jnp.int32)
    global_ids = parcel_ids + offsets[:, None]
    owner_start = lax.axis_index("vert") * par_dev

    nx = owners // VERT_MINOR
    n_tm = lax.axis_size("tm")
    tm = lax.axis_index("tm")
    sums3 = reduce_to_owner(global_ids, flat_env, nx, VERT_MINOR, n_tm, par_dev)[:, :par_dev].reshape(3, par_dev, BANDS, t_dev)
    before = jnp.where(tm > 0, sums3[0, :, :, t_dev - LAG :], 0.0)
    after = jnp.where(tm < n_tm - 1, sums3[2, :, :, :LAG], 0.0)
    own_ext = jnp.concatenate([before, sums3[1], after], axis=2)
    centered, own_middle, own_spread = centered_rows(own_ext, t_dev)

    own = jnp.pad(centered.transpose(1, 0, 2), ((0, 0), (0, ROW_PAD - par_dev), (0, 0)))
    mid = jnp.pad(
        own_middle.transpose(1, 0, 2), ((0, 0), (0, ROW_PAD - par_dev), (0, t_dev))
    )
    spread = jnp.pad(own_spread.T, ((0, 0), (0, ROW_PAD - par_dev)))[:, :, None]
    r = lax.iota(jnp.int32, ROW_PAD)
    own_level = jnp.where(
        r < par_dev, resolution_of(owner_start + r), -2
    ).astype(jnp.float32)
    own_level = jnp.where(own_level < 3, own_level, -2.0)
    col = lax.iota(jnp.int32, owners * ROW_PAD)
    col_level = jnp.where(
        col % ROW_PAD < par_dev, resolution_of(col // ROW_PAD * par_dev + col % ROW_PAD), -1
    ).astype(jnp.float32)
    levels = jnp.concatenate(
        [jnp.broadcast_to(own_level[:, None], (ROW_PAD, 128)),
         jnp.broadcast_to(col_level[None, :], (ROW_PAD, owners * ROW_PAD))], axis=1
    )
    padded = gather_fold(own, mid, spread, levels, nx, VERT_MINOR, t_dev, par_dev)
    coupling = padded.reshape(BANDS, par_dev, owners, ROW_PAD)[:, :, :, :par_dev]
    coupling = coupling.reshape(BANDS, par_dev, total_par)
    return coupling[None]


def solution(mesh):
    return jax.shard_map(
        local,
        mesh=mesh,
        in_specs=(P("vert", "tm"), P(), P(), P(None, "vert")),
        out_specs=P("tm", None, "vert", None),
        check_vma=False,
    )
```

```python
from functools import partial

import jax
import jax.numpy as jnp
from jax import lax
from jax.experimental import pallas as pl
from jax.experimental.pallas import tpu as pltpu
from jax.sharding import PartitionSpec as P

P1 = 100
P2 = 400
P3 = 1000
BANDS = 2
TAPS = 65
HALF = 32
LAG = 64
LAG_STEP = 1
NLAG = 129

EPSILON = 1e-05

ROW_PAD = 96
LAG_CHUNKS = 11
LAG_PAD = 132
VERT_MINOR = 4


def extended_2(cells, sides, width):
    for axis, dim in sides:
        count = lax.axis_size(axis)
        ends = count - 1
        head = lax.slice_in_dim(cells, 0, width, axis=dim)
        tail = lax.slice_in_dim(cells, cells.shape[dim] - width, cells.shape[dim], axis=dim)
        cells = jnp.concatenate(
            [
                lax.ppermute(tail, axis, [(i, (i + 1) % count) for i in range(ends)]),
                cells,
                lax.ppermute(head, axis, [((i + 1) % count, i) for i in range(ends)]),
            ],
            axis=dim,
        )
    return cells


def toeplitz_band(taps, n_out, n_in):
    period = jnp.concatenate([taps, jnp.zeros((n_in + 1 - taps.shape[0],), taps.dtype)])
    return jnp.tile(period, n_out)[: n_out * n_in].reshape(n_out, n_in)


def resolution_of(parcel):
    first = (parcel >= P1).astype(jnp.int32)
    second = (parcel >= P1 + P2).astype(jnp.int32)
    third = (parcel >= P1 + P2 + P3).astype(jnp.int32)
    return first + second + third


def centered_rows(extended, length):
    level_mean = jnp.mean(extended[:, :, LAG : LAG + length], axis=2, keepdims=True)
    centered = (extended - level_mean).astype(jnp.bfloat16)
    middle = centered[:, :, LAG : LAG + length]
    middle_wide = middle.astype(jnp.float32)
    spread = lax.rsqrt(jnp.mean(middle_wide * middle_wide, axis=2) + EPSILON)
    return (centered, middle, spread)


def mesh_peers(nx, nz):
    me = lax.axis_index("vert")
    tm = lax.axis_index("tm")
    mx, mz = me // nz, me % nz
    return me, tm, mx, mz


def greet(mx, mz, tm, nx, nz, n_tm=0):
    barrier = pltpu.get_barrier_semaphore()
    me = mx * nz + mz
    peers = [(lax.rem(mx + k, nx) * nz + mz, tm) for k in range(1, nx)]
    peers += [(mx * nz + lax.rem(mz + k, nz), tm) for k in range(1, nz)]
    if n_tm:
        peers += [(me, lax.rem(tm + 1, n_tm)), (me, lax.rem(tm + n_tm - 1, n_tm))]
    for peer in peers:
        pl.semaphore_signal(barrier, inc=1, device_id=peer, device_id_type=pl.DeviceIdType.MESH)
    pl.semaphore_wait(barrier, len(peers))


def reduce_kernel(nx, nz, n_tm, par_dev, ids_ref, env_ref, out_ref, x_ref, recv_a, send_a, part, recv_b, mine,
                  halo, a_send, a_recv, b_send, b_recv, t_send, t_recv):
    me, tm, mx, mz = mesh_peers(nx, nz)
    greet(mx, mz, tm, nx, nz, n_tm)
    hz = nz // 2
    rows = x_ref.shape[1]
    r = lax.broadcasted_iota(jnp.int32, (rows, 1), 0)

    def pool_groups(first_offset, carry):
        def one(j, c):
            owner = lax.rem(mx + first_offset + 2 * (j // nz), nx) * nz + j % nz
            wanted = jnp.where(r < par_dev, owner * par_dev + r, -1)
            hits = (ids_ref[0] == wanted).astype(jnp.float32)
            for level in range(1, ids_ref.shape[0]):
                hits = hits + (ids_ref[level] == wanted).astype(jnp.float32)
            x_ref[owner] = jnp.dot(
                hits.astype(jnp.bfloat16), env_ref[...], preferred_element_type=jnp.float32
            )
            return c

        return lax.fori_loop(0, 2 * nz, one, carry)

    pool_groups(nx - 1, 0)
    peers = (lax.rem(mx + 1, nx), lax.rem(mx + nx - 1, nx))

    def owners_of(g, d):
        return pl.ds(g * nz + d * hz, hz)

    for s in range(1, nx):
        copies = []
        for d in range(2):
            g = lax.rem(mx + (s if d else nx * s - s), nx)
            if s == 1:
                src = x_ref.at[owners_of(g, d)]
            else:
                send_a[d, s - 2] = recv_a[d, s - 2] + x_ref[owners_of(g, d)]
                src = send_a.at[d, s - 2]
            copy = pltpu.make_async_remote_copy(
                src_ref=src, dst_ref=recv_a.at[d, s - 1],
                send_sem=a_send.at[d, s - 1], recv_sem=a_recv.at[d, s - 1],
                device_id=(peers[d] * nz + mz, tm), device_id_type=pl.DeviceIdType.MESH,
            )
            copy.start()
            copies.append(copy)
        if s == 1:
            pool_groups(2, 0)
        for copy in copies:
            copy.wait()
    for d in range(2):
        part[d * hz : (d + 1) * hz] = recv_a[d, nx - 2] + x_ref[owners_of(mx, d)]
    copies = []
    for k in range(1, nz):
        pz = lax.rem(mz + k, nz)
        copy = pltpu.make_async_remote_copy(
            src_ref=part.at[pz], dst_ref=recv_b.at[k - 1],
            send_sem=b_send.at[k - 1], recv_sem=b_recv.at[k - 1],
            device_id=(mx * nz + pz, tm), device_id_type=pl.DeviceIdType.MESH,
        )
        copy.start()
        copies.append(copy)
    for copy in copies:
        copy.wait()
    total = part[mz]
    for k in range(1, nz):
        total = total + recv_b[k - 1]
    mine[...] = total
    copies = []
    for d, step in enumerate((1, n_tm - 1)):
        copy = pltpu.make_async_remote_copy(
            src_ref=mine, dst_ref=halo.at[d],
            send_sem=t_send.at[d], recv_sem=t_recv.at[d],
            device_id=(me, lax.rem(tm + step, n_tm)), device_id_type=pl.DeviceIdType.MESH,
        )
        copy.start()
        copies.append(copy)
    out_ref[1] = total
    for copy in copies:
        copy.wait()
    out_ref[0] = halo[0]
    out_ref[2] = halo[1]


def reduce_to_owner(global_ids, flat_env, nx, nz, n_tm, par_dev):
    levels, vertices = global_ids.shape
    w = flat_env.shape[1]
    rows = ROW_PAD
    hz = nz // 2
    dtype = jnp.float32
    return pl.pallas_call(
        partial(reduce_kernel, nx, nz, n_tm, par_dev),
        out_shape=jax.ShapeDtypeStruct((3, rows, w), dtype),
        in_specs=[pl.BlockSpec(memory_space=pltpu.VMEM)] * 2,
        out_specs=pl.BlockSpec(memory_space=pltpu.VMEM),
        scratch_shapes=[
            pltpu.VMEM((nx * nz, rows, w), dtype),
            pltpu.VMEM((2, nx - 1, hz, rows, w), dtype),
            pltpu.VMEM((2, nx - 2, hz, rows, w), dtype),
            pltpu.VMEM((nz, rows, w), dtype),
            pltpu.VMEM((nz - 1, rows, w), dtype),
            pltpu.VMEM((rows, w), dtype),
            pltpu.VMEM((2, rows, w), dtype),
            pltpu.SemaphoreType.DMA((2, nx - 1)),
            pltpu.SemaphoreType.DMA((2, nx - 1)),
            pltpu.SemaphoreType.DMA((nz - 1,)),
            pltpu.SemaphoreType.DMA((nz - 1,)),
            pltpu.SemaphoreType.DMA((2,)),
            pltpu.SemaphoreType.DMA((2,)),
        ],
        compiler_params=pltpu.CompilerParams(collective_id=0, has_side_effects=True),
    )(global_ids.reshape(levels, 1, vertices), flat_env)


def fill_lags(mid_ref, lhs_ref, band):
    rows = mid_ref.shape[1]
    base = mid_ref[band].astype(jnp.float32)
    for q in range(NLAG):
        lhs_ref[band, q * rows : (q + 1) * rows, :] = pltpu.roll(base, q, 1).astype(lhs_ref.dtype)
    lhs_ref[band, NLAG * rows :, :] = jnp.zeros(
        ((LAG_PAD - NLAG) * rows, lhs_ref.shape[2]), lhs_ref.dtype
    )


def fold_group(g, group, lhs_ref, gath, out_ref, spread_ref, level_ref, t_dev):
    rows = lhs_ref.shape[1] // LAG_PAD
    kept = out_ref.shape[1]
    step = LAG_PAD // LAG_CHUNKS
    first = pl.multiple_of(g * group, 128)
    same = (level_ref[:, 0:1] == level_ref[:, pl.ds(pl.multiple_of(g * group + 128, 128), group)]).astype(jnp.float32)

    def one_band(band, carry):
        block = gath[band, pl.ds(first, group), :].astype(jnp.float32)
        rhs_wide = block.T
        rhs = rhs_wide.astype(jnp.bfloat16)
        middle = rhs_wide[LAG : LAG + t_dev, :]
        spread = lax.rsqrt(jnp.sum(middle * middle, axis=0, keepdims=True) / t_dev + EPSILON)
        acc = jnp.zeros((rows, group), jnp.float32)
        for h in range(LAG_CHUNKS):
            lhs = lhs_ref[band, h * step * rows : (h + 1) * step * rows, :]
            r = jnp.dot(lhs, rhs, preferred_element_type=jnp.float32)
            acc = acc + (r * r).reshape(step, rows, group).sum(axis=0)
        scale = spread_ref[band] * spread / t_dev
        out_ref[band, :, pl.ds(first, group)] = (acc * (scale * scale) * same / NLAG)[:kept]
        return carry

    lax.fori_loop(0, out_ref.shape[0], one_band, 0)


def gather_fold_kernel(nx, nz, t_dev, own_ref, mid_ref, spread_ref, level_ref, out_ref, gath, lhs_ref,
                       a_send, a_recv, b_send, b_recv, local_sem):
    me, tm, mx, mz = mesh_peers(nx, nz)
    rows = own_ref.shape[1]
    group = nz * rows
    greet(mx, mz, tm, nx, nz)
    mine = gath.at[:, pl.ds(me * rows, rows), :]
    own = pltpu.make_async_copy(own_ref, mine, local_sem)
    own.start()
    copies = []
    for k in range(1, nz):
        copy = pltpu.make_async_remote_copy(
            src_ref=own_ref, dst_ref=mine,
            send_sem=a_send.at[k - 1], recv_sem=a_recv.at[k - 1],
            device_id=(mx * nz + lax.rem(mz + k, nz), tm), device_id_type=pl.DeviceIdType.MESH,
        )
        copy.start()
        copies.append(copy)
    for band in range(mid_ref.shape[0]):
        fill_lags(mid_ref, lhs_ref, band)
    own.wait()
    for copy in copies:
        copy.wait()
    left, right = lax.rem(mx + nx - 1, nx), lax.rem(mx + 1, nx)
    half = group // 2

    def ring_copy(start, size, peer, slot):
        rows_at = gath.at[:, pl.ds(start, size), :]
        return pltpu.make_async_remote_copy(
            src_ref=rows_at, dst_ref=rows_at,
            send_sem=b_send.at[slot], recv_sem=b_recv.at[slot],
            device_id=(peer * nz + mz, tm), device_id_type=pl.DeviceIdType.MESH,
        )

    near = [ring_copy(mx * group, group, right, 0), ring_copy(mx * group, group, left, 1)]
    for copy in near:
        copy.start()
    fold_group(mx, group, lhs_ref, gath, out_ref, spread_ref, level_ref, t_dev)
    for copy in near:
        copy.wait_recv()
    far = [ring_copy(left * group, half, right, 2), ring_copy(right * group + half, half, left, 3)]
    for copy in far:
        copy.start()
    fold_group(left, group, lhs_ref, gath, out_ref, spread_ref, level_ref, t_dev)
    fold_group(right, group, lhs_ref, gath, out_ref, spread_ref, level_ref, t_dev)
    for copy in far:
        copy.wait_recv()
    fold_group(lax.rem(mx + 2, nx), group, lhs_ref, gath, out_ref, spread_ref, level_ref, t_dev)
    for copy in near + far:
        copy.wait_send()


def gather_fold(own, mid, spread, levels, nx, nz, t_dev, kept):
    assert nx == 4
    bands, rows, width = own.shape
    cols = nx * nz * rows
    flops = 2 * bands * LAG_PAD * rows * width * cols
    return pl.pallas_call(
        partial(gather_fold_kernel, nx, nz, t_dev),
        out_shape=jax.ShapeDtypeStruct((bands, kept, cols), jnp.float32),
        in_specs=[pl.BlockSpec(memory_space=pltpu.VMEM)] * 4,
        out_specs=pl.BlockSpec(memory_space=pltpu.VMEM),
        scratch_shapes=[
            pltpu.VMEM((bands, cols, width), own.dtype),
            pltpu.VMEM((bands, LAG_PAD * rows, width), jnp.bfloat16),
            pltpu.SemaphoreType.DMA((nz - 1,)),
            pltpu.SemaphoreType.DMA((nz - 1,)),
            pltpu.SemaphoreType.DMA((4,)),
            pltpu.SemaphoreType.DMA((4,)),
            pltpu.SemaphoreType.DMA(()),
        ],
        compiler_params=pltpu.CompilerParams(
            collective_id=1, has_side_effects=True, vmem_limit_bytes=48 * 1024 * 1024
        ),
        cost_estimate=pl.CostEstimate(
            flops=flops, bytes_accessed=2 * (own.size + mid.size) + 4 * bands * rows * cols,
            transcendentals=0,
        ),
    )(own, mid, spread, levels)


def local(source, band_taps, smooth_taps, parcel_ids):
    vert_dev, t_dev = source.shape
    owners = lax.axis_size("vert")
    total_par = (P1 + P2 + P3 + owners - 1) // owners * owners
    par_dev = total_par // owners
    n_mid = t_dev + 2 * HALF
    n_in = t_dev + 4 * HALF
    first_rows = jax.vmap(partial(toeplitz_band, n_out=n_mid, n_in=n_in))(
        band_taps.reshape(2 * BANDS, TAPS)
    )
    first_mat = first_rows.transpose(2, 0, 1).reshape(n_in, 2 * BANDS * n_mid)
    second_rows = jax.vmap(partial(toeplitz_band, n_out=t_dev, n_in=n_mid))(smooth_taps)
    second_mat = second_rows.transpose(0, 2, 1)
    count = lax.axis_size("tm")
    width = 2 * HALF
    before = lax.ppermute(
        source[:, t_dev - width :], "tm", [(i, i + 1) for i in range(count - 1)]
    )
    after = lax.ppermute(source[:, :width], "tm", [(i + 1, i) for i in range(count - 1)])
    wave = jnp.dot(source, first_mat[width : width + t_dev], preferred_element_type=jnp.float32)
    wave = wave + jnp.dot(before, first_mat[:width], preferred_element_type=jnp.float32)
    wave = wave + jnp.dot(after, first_mat[width + t_dev :], preferred_element_type=jnp.float32)
    wave = wave.reshape(vert_dev, 2, BANDS, n_mid)
    power = (wave[:, 0] * wave[:, 0] + wave[:, 1] * wave[:, 1]).astype(jnp.bfloat16)
    envelope = jnp.einsum(
        "vbu,but->vbt", power, second_mat, preferred_element_type=jnp.float32
    ).astype(jnp.bfloat16)
    flat_env = envelope.reshape(vert_dev, BANDS * t_dev)
    offsets = jnp.array([0, P1, P1 + P2], dtype=jnp.int32)
    global_ids = parcel_ids + offsets[:, None]
    owner_start = lax.axis_index("vert") * par_dev

    nx = owners // VERT_MINOR
    n_tm = lax.axis_size("tm")
    tm = lax.axis_index("tm")
    sums3 = reduce_to_owner(global_ids, flat_env, nx, VERT_MINOR, n_tm, par_dev)[:, :par_dev].reshape(3, par_dev, BANDS, t_dev)
    before = jnp.where(tm > 0, sums3[0, :, :, t_dev - LAG :], 0.0)
    after = jnp.where(tm < n_tm - 1, sums3[2, :, :, :LAG], 0.0)
    own_ext = jnp.concatenate([before, sums3[1], after], axis=2)
    centered, own_middle, own_spread = centered_rows(own_ext, t_dev)

    own = jnp.pad(centered.transpose(1, 0, 2), ((0, 0), (0, ROW_PAD - par_dev), (0, 0)))
    mid = jnp.pad(
        own_middle.transpose(1, 0, 2), ((0, 0), (0, ROW_PAD - par_dev), (0, t_dev))
    )
    spread = jnp.pad(own_spread.T, ((0, 0), (0, ROW_PAD - par_dev)))[:, :, None]
    r = lax.iota(jnp.int32, ROW_PAD)
    own_level = jnp.where(
        r < par_dev, resolution_of(owner_start + r), -2
    ).astype(jnp.float32)
    own_level = jnp.where(own_level < 3, own_level, -2.0)
    col = lax.iota(jnp.int32, owners * ROW_PAD)
    col_level = jnp.where(
        col % ROW_PAD < par_dev, resolution_of(col // ROW_PAD * par_dev + col % ROW_PAD), -1
    ).astype(jnp.float32)
    levels = jnp.concatenate(
        [jnp.broadcast_to(own_level[:, None], (ROW_PAD, 128)),
         jnp.broadcast_to(col_level[None, :], (ROW_PAD, owners * ROW_PAD))], axis=1
    )
    padded = gather_fold(own, mid, spread, levels, nx, VERT_MINOR, t_dev, par_dev)
    coupling = padded.reshape(BANDS, par_dev, owners, ROW_PAD)[:, :, :, :par_dev]
    coupling = coupling.reshape(BANDS, par_dev, total_par)
    return coupling[None]


def solution(mesh):
    return jax.shard_map(
        local,
        mesh=mesh,
        in_specs=(P("vert", "tm"), P(), P(), P(None, "vert")),
        out_specs=P("tm", None, "vert", None),
        check_vma=False,
    )
```

```python
from functools import partial

import jax
import jax.numpy as jnp
from jax import lax
from jax.experimental import pallas as pl
from jax.experimental.pallas import tpu as pltpu
from jax.sharding import PartitionSpec as P

P1 = 100
P2 = 400
P3 = 1000
BANDS = 2
TAPS = 65
HALF = 32
LAG = 64
LAG_STEP = 1
NLAG = 129

EPSILON = 1e-05

ROW_PAD = 96
LAG_CHUNKS = 11
LAG_PAD = 132
VERT_MINOR = 4


def extended_2(cells, sides, width):
    for axis, dim in sides:
        count = lax.axis_size(axis)
        ends = count - 1
        head = lax.slice_in_dim(cells, 0, width, axis=dim)
        tail = lax.slice_in_dim(cells, cells.shape[dim] - width, cells.shape[dim], axis=dim)
        cells = jnp.concatenate(
            [
                lax.ppermute(tail, axis, [(i, (i + 1) % count) for i in range(ends)]),
                cells,
                lax.ppermute(head, axis, [((i + 1) % count, i) for i in range(ends)]),
            ],
            axis=dim,
        )
    return cells


def toeplitz_band(taps, n_out, n_in):
    period = jnp.concatenate([taps, jnp.zeros((n_in + 1 - taps.shape[0],), taps.dtype)])
    return jnp.tile(period, n_out)[: n_out * n_in].reshape(n_out, n_in)


def resolution_of(parcel):
    first = (parcel >= P1).astype(jnp.int32)
    second = (parcel >= P1 + P2).astype(jnp.int32)
    third = (parcel >= P1 + P2 + P3).astype(jnp.int32)
    return first + second + third


def centered_rows(extended, length):
    level_mean = jnp.mean(extended[:, :, LAG : LAG + length], axis=2, keepdims=True)
    centered = (extended - level_mean).astype(jnp.bfloat16)
    middle = centered[:, :, LAG : LAG + length]
    middle_wide = middle.astype(jnp.float32)
    spread = lax.rsqrt(jnp.mean(middle_wide * middle_wide, axis=2) + EPSILON)
    return (centered, middle, spread)


def mesh_peers(nx, nz):
    me = lax.axis_index("vert")
    tm = lax.axis_index("tm")
    mx, mz = me // nz, me % nz
    return me, tm, mx, mz


def greet(mx, mz, tm, nx, nz, n_tm=0):
    barrier = pltpu.get_barrier_semaphore()
    me = mx * nz + mz
    peers = [(lax.rem(mx + k, nx) * nz + mz, tm) for k in range(1, nx)]
    peers += [(mx * nz + lax.rem(mz + k, nz), tm) for k in range(1, nz)]
    if n_tm:
        peers += [(me, lax.rem(tm + 1, n_tm)), (me, lax.rem(tm + n_tm - 1, n_tm))]
    for peer in peers:
        pl.semaphore_signal(barrier, inc=1, device_id=peer, device_id_type=pl.DeviceIdType.MESH)
    pl.semaphore_wait(barrier, len(peers))


def reduce_kernel(nx, nz, n_tm, par_dev, ids_ref, env_ref, out_ref, x_ref, recv_a, send_a, part, recv_b, mine,
                  halo, a_send, a_recv, b_send, b_recv, t_send, t_recv):
    me, tm, mx, mz = mesh_peers(nx, nz)
    greet(mx, mz, tm, nx, nz, n_tm)
    hz = nz // 2
    rows = x_ref.shape[1]
    r = lax.broadcasted_iota(jnp.int32, (rows, 1), 0)

    def pool_groups(first_offset, carry, count=2 * nz, part_of=None):
        def one(j, c):
            if part_of is None:
                owner = lax.rem(mx + first_offset + 2 * (j // nz), nx) * nz + j % nz
            else:
                side = j // hz
                owner = lax.rem(mx + first_offset + 2 * side, nx) * nz + (part_of + side - 2 * part_of * side) * hz + j % hz
            wanted = jnp.where(r < par_dev, owner * par_dev + r, -1)
            hits = (ids_ref[0] == wanted).astype(jnp.float32)
            for level in range(1, ids_ref.shape[0]):
                hits = hits + (ids_ref[level] == wanted).astype(jnp.float32)
            x_ref[owner] = jnp.dot(
                hits.astype(jnp.bfloat16), env_ref[...], preferred_element_type=jnp.float32
            )
            return c

        return lax.fori_loop(0, count, one, carry)

    pool_groups(nx - 1, 0, nz, 0)
    peers = (lax.rem(mx + 1, nx), lax.rem(mx + nx - 1, nx))

    def owners_of(g, d):
        return pl.ds(g * nz + d * hz, hz)

    for s in range(1, nx):
        copies = []
        for d in range(2):
            g = lax.rem(mx + (s if d else nx * s - s), nx)
            if s == 1:
                src = x_ref.at[owners_of(g, d)]
            else:
                send_a[d, s - 2] = recv_a[d, s - 2] + x_ref[owners_of(g, d)]
                src = send_a.at[d, s - 2]
            copy = pltpu.make_async_remote_copy(
                src_ref=src, dst_ref=recv_a.at[d, s - 1],
                send_sem=a_send.at[d, s - 1], recv_sem=a_recv.at[d, s - 1],
                device_id=(peers[d] * nz + mz, tm), device_id_type=pl.DeviceIdType.MESH,
            )
            copy.start()
            copies.append(copy)
        if s == 1:
            pool_groups(nx - 1, 0, nz, 1)
            pool_groups(2, 0)
        for copy in copies:
            copy.wait()
    for d in range(2):
        part[d * hz : (d + 1) * hz] = recv_a[d, nx - 2] + x_ref[owners_of(mx, d)]
    copies = []
    for k in range(1, nz):
        pz = lax.rem(mz + k, nz)
        copy = pltpu.make_async_remote_copy(
            src_ref=part.at[pz], dst_ref=recv_b.at[k - 1],
            send_sem=b_send.at[k - 1], recv_sem=b_recv.at[k - 1],
            device_id=(mx * nz + pz, tm), device_id_type=pl.DeviceIdType.MESH,
        )
        copy.start()
        copies.append(copy)
    for copy in copies:
        copy.wait()
    total = part[mz]
    for k in range(1, nz):
        total = total + recv_b[k - 1]
    mine[...] = total
    copies = []
    for d, step in enumerate((1, n_tm - 1)):
        copy = pltpu.make_async_remote_copy(
            src_ref=mine, dst_ref=halo.at[d],
            send_sem=t_send.at[d], recv_sem=t_recv.at[d],
            device_id=(me, lax.rem(tm + step, n_tm)), device_id_type=pl.DeviceIdType.MESH,
        )
        copy.start()
        copies.append(copy)
    out_ref[1] = total
    for copy in copies:
        copy.wait()
    out_ref[0] = halo[0]
    out_ref[2] = halo[1]


def reduce_to_owner(global_ids, flat_env, nx, nz, n_tm, par_dev):
    levels, vertices = global_ids.shape
    w = flat_env.shape[1]
    rows = ROW_PAD
    hz = nz // 2
    dtype = jnp.float32
    return pl.pallas_call(
        partial(reduce_kernel, nx, nz, n_tm, par_dev),
        out_shape=jax.ShapeDtypeStruct((3, rows, w), dtype),
        in_specs=[pl.BlockSpec(memory_space=pltpu.VMEM)] * 2,
        out_specs=pl.BlockSpec(memory_space=pltpu.VMEM),
        scratch_shapes=[
            pltpu.VMEM((nx * nz, rows, w), dtype),
            pltpu.VMEM((2, nx - 1, hz, rows, w), dtype),
            pltpu.VMEM((2, nx - 2, hz, rows, w), dtype),
            pltpu.VMEM((nz, rows, w), dtype),
            pltpu.VMEM((nz - 1, rows, w), dtype),
            pltpu.VMEM((rows, w), dtype),
            pltpu.VMEM((2, rows, w), dtype),
            pltpu.SemaphoreType.DMA((2, nx - 1)),
            pltpu.SemaphoreType.DMA((2, nx - 1)),
            pltpu.SemaphoreType.DMA((nz - 1,)),
            pltpu.SemaphoreType.DMA((nz - 1,)),
            pltpu.SemaphoreType.DMA((2,)),
            pltpu.SemaphoreType.DMA((2,)),
        ],
        compiler_params=pltpu.CompilerParams(collective_id=0, has_side_effects=True),
    )(global_ids.reshape(levels, 1, vertices), flat_env)


def fill_lags(mid_ref, lhs_ref, band):
    rows = mid_ref.shape[1]
    base = mid_ref[band].astype(jnp.float32)
    for q in range(NLAG):
        lhs_ref[band, q * rows : (q + 1) * rows, :] = pltpu.roll(base, q, 1).astype(lhs_ref.dtype)
    lhs_ref[band, NLAG * rows :, :] = jnp.zeros(
        ((LAG_PAD - NLAG) * rows, lhs_ref.shape[2]), lhs_ref.dtype
    )


def fold_group(g, group, lhs_ref, gath, out_ref, spread_ref, level_ref, t_dev):
    rows = lhs_ref.shape[1] // LAG_PAD
    kept = out_ref.shape[1]
    step = LAG_PAD // LAG_CHUNKS
    first = pl.multiple_of(g * group, 128)
    same = (level_ref[:, 0:1] == level_ref[:, pl.ds(pl.multiple_of(g * group + 128, 128), group)]).astype(jnp.float32)

    def one_band(band, carry):
        block = gath[band, pl.ds(first, group), :].astype(jnp.float32)
        rhs_wide = block.T
        rhs = rhs_wide.astype(jnp.bfloat16)
        middle = rhs_wide[LAG : LAG + t_dev, :]
        spread = lax.rsqrt(jnp.sum(middle * middle, axis=0, keepdims=True) / t_dev + EPSILON)
        acc = jnp.zeros((rows, group), jnp.float32)
        for h in range(LAG_CHUNKS):
            lhs = lhs_ref[band, h * step * rows : (h + 1) * step * rows, :]
            r = jnp.dot(lhs, rhs, preferred_element_type=jnp.float32)
            acc = acc + (r * r).reshape(step, rows, group).sum(axis=0)
        scale = spread_ref[band] * spread / t_dev
        out_ref[band, :, pl.ds(first, group)] = (acc * (scale * scale) * same / NLAG)[:kept]
        return carry

    lax.fori_loop(0, out_ref.shape[0], one_band, 0)


def gather_fold_kernel(nx, nz, t_dev, own_ref, mid_ref, spread_ref, level_ref, out_ref, gath, lhs_ref,
                       a_send, a_recv, b_send, b_recv, local_sem):
    me, tm, mx, mz = mesh_peers(nx, nz)
    rows = own_ref.shape[1]
    group = nz * rows
    greet(mx, mz, tm, nx, nz)
    mine = gath.at[:, pl.ds(me * rows, rows), :]
    own = pltpu.make_async_copy(own_ref, mine, local_sem)
    own.start()
    copies = []
    for k in range(1, nz):
        copy = pltpu.make_async_remote_copy(
            src_ref=own_ref, dst_ref=mine,
            send_sem=a_send.at[k - 1], recv_sem=a_recv.at[k - 1],
            device_id=(mx * nz + lax.rem(mz + k, nz), tm), device_id_type=pl.DeviceIdType.MESH,
        )
        copy.start()
        copies.append(copy)
    for band in range(mid_ref.shape[0]):
        fill_lags(mid_ref, lhs_ref, band)
    own.wait()
    for copy in copies:
        copy.wait()
    left, right = lax.rem(mx + nx - 1, nx), lax.rem(mx + 1, nx)
    half = group // 2

    def ring_copy(start, size, peer, slot):
        rows_at = gath.at[:, pl.ds(start, size), :]
        return pltpu.make_async_remote_copy(
            src_ref=rows_at, dst_ref=rows_at,
            send_sem=b_send.at[slot], recv_sem=b_recv.at[slot],
            device_id=(peer * nz + mz, tm), device_id_type=pl.DeviceIdType.MESH,
        )

    near = [ring_copy(mx * group, group, right, 0), ring_copy(mx * group, group, left, 1)]
    for copy in near:
        copy.start()
    fold_group(mx, group, lhs_ref, gath, out_ref, spread_ref, level_ref, t_dev)
    for copy in near:
        copy.wait_recv()
    far = [ring_copy(left * group, half, right, 2), ring_copy(right * group + half, half, left, 3)]
    for copy in far:
        copy.start()
    fold_group(left, group, lhs_ref, gath, out_ref, spread_ref, level_ref, t_dev)
    fold_group(right, group, lhs_ref, gath, out_ref, spread_ref, level_ref, t_dev)
    for copy in far:
        copy.wait_recv()
    fold_group(lax.rem(mx + 2, nx), group, lhs_ref, gath, out_ref, spread_ref, level_ref, t_dev)
    for copy in near + far:
        copy.wait_send()


def gather_fold(own, mid, spread, levels, nx, nz, t_dev, kept):
    assert nx == 4
    bands, rows, width = own.shape
    cols = nx * nz * rows
    flops = 2 * bands * LAG_PAD * rows * width * cols
    return pl.pallas_call(
        partial(gather_fold_kernel, nx, nz, t_dev),
        out_shape=jax.ShapeDtypeStruct((bands, kept, cols), jnp.float32),
        in_specs=[pl.BlockSpec(memory_space=pltpu.VMEM)] * 4,
        out_specs=pl.BlockSpec(memory_space=pltpu.VMEM),
        scratch_shapes=[
            pltpu.VMEM((bands, cols, width), own.dtype),
            pltpu.VMEM((bands, LAG_PAD * rows, width), jnp.bfloat16),
            pltpu.SemaphoreType.DMA((nz - 1,)),
            pltpu.SemaphoreType.DMA((nz - 1,)),
            pltpu.SemaphoreType.DMA((4,)),
            pltpu.SemaphoreType.DMA((4,)),
            pltpu.SemaphoreType.DMA(()),
        ],
        compiler_params=pltpu.CompilerParams(
            collective_id=1, has_side_effects=True, vmem_limit_bytes=48 * 1024 * 1024
        ),
        cost_estimate=pl.CostEstimate(
            flops=flops, bytes_accessed=2 * (own.size + mid.size) + 4 * bands * rows * cols,
            transcendentals=0,
        ),
    )(own, mid, spread, levels)


def local(source, band_taps, smooth_taps, parcel_ids):
    vert_dev, t_dev = source.shape
    owners = lax.axis_size("vert")
    total_par = (P1 + P2 + P3 + owners - 1) // owners * owners
    par_dev = total_par // owners
    n_mid = t_dev + 2 * HALF
    n_in = t_dev + 4 * HALF
    first_rows = jax.vmap(partial(toeplitz_band, n_out=n_mid, n_in=n_in))(
        band_taps.reshape(2 * BANDS, TAPS)
    )
    first_mat = first_rows.transpose(2, 0, 1).reshape(n_in, 2 * BANDS * n_mid)
    second_rows = jax.vmap(partial(toeplitz_band, n_out=t_dev, n_in=n_mid))(smooth_taps)
    second_mat = second_rows.transpose(0, 2, 1)
    widened = extended_2(source, (("tm", 1),), 2 * HALF)
    wave = jnp.dot(widened, first_mat, preferred_element_type=jnp.float32).reshape(
        vert_dev, 2, BANDS, n_mid
    )
    power = (wave[:, 0] * wave[:, 0] + wave[:, 1] * wave[:, 1]).astype(jnp.bfloat16)
    envelope = jnp.einsum(
        "vbu,but->vbt", power, second_mat, preferred_element_type=jnp.float32
    ).astype(jnp.bfloat16)
    flat_env = envelope.reshape(vert_dev, BANDS * t_dev)
    offsets = jnp.array([0, P1, P1 + P2], dtype=jnp.int32)
    global_ids = parcel_ids + offsets[:, None]
    owner_start = lax.axis_index("vert") * par_dev

    nx = owners // VERT_MINOR
    n_tm = lax.axis_size("tm")
    tm = lax.axis_index("tm")
    sums3 = reduce_to_owner(global_ids, flat_env, nx, VERT_MINOR, n_tm, par_dev)[:, :par_dev].reshape(3, par_dev, BANDS, t_dev)
    before = jnp.where(tm > 0, sums3[0, :, :, t_dev - LAG :], 0.0)
    after = jnp.where(tm < n_tm - 1, sums3[2, :, :, :LAG], 0.0)
    own_ext = jnp.concatenate([before, sums3[1], after], axis=2)
    centered, own_middle, own_spread = centered_rows(own_ext, t_dev)

    own = jnp.pad(centered.transpose(1, 0, 2), ((0, 0), (0, ROW_PAD - par_dev), (0, 0)))
    mid = jnp.pad(
        own_middle.transpose(1, 0, 2), ((0, 0), (0, ROW_PAD - par_dev), (0, t_dev))
    )
    spread = jnp.pad(own_spread.T, ((0, 0), (0, ROW_PAD - par_dev)))[:, :, None]
    r = lax.iota(jnp.int32, ROW_PAD)
    own_level = jnp.where(
        r < par_dev, resolution_of(owner_start + r), -2
    ).astype(jnp.float32)
    own_level = jnp.where(own_level < 3, own_level, -2.0)
    col = lax.iota(jnp.int32, owners * ROW_PAD)
    col_level = jnp.where(
        col % ROW_PAD < par_dev, resolution_of(col // ROW_PAD * par_dev + col % ROW_PAD), -1
    ).astype(jnp.float32)
    levels = jnp.concatenate(
        [jnp.broadcast_to(own_level[:, None], (ROW_PAD, 128)),
         jnp.broadcast_to(col_level[None, :], (ROW_PAD, owners * ROW_PAD))], axis=1
    )
    padded = gather_fold(own, mid, spread, levels, nx, VERT_MINOR, t_dev, par_dev)
    coupling = padded.reshape(BANDS, par_dev, owners, ROW_PAD)[:, :, :, :par_dev]
    coupling = coupling.reshape(BANDS, par_dev, total_par)
    return coupling[None]


def solution(mesh):
    return jax.shard_map(
        local,
        mesh=mesh,
        in_specs=(P("vert", "tm"), P(), P(), P(None, "vert")),
        out_specs=P("tm", None, "vert", None),
        check_vma=False,
    )
```

```python
from functools import partial

import jax
import jax.numpy as jnp
from jax import lax
from jax.experimental import pallas as pl
from jax.experimental.pallas import tpu as pltpu
from jax.sharding import PartitionSpec as P

P1 = 100
P2 = 400
P3 = 1000
BANDS = 2
TAPS = 65
HALF = 32
LAG = 64
LAG_STEP = 1
NLAG = 129

EPSILON = 1e-05

ROW_PAD = 96
LAG_CHUNKS = 12
LAG_PAD = 132
VERT_MINOR = 4


def extended_2(cells, sides, width):
    for axis, dim in sides:
        count = lax.axis_size(axis)
        ends = count - 1
        head = lax.slice_in_dim(cells, 0, width, axis=dim)
        tail = lax.slice_in_dim(cells, cells.shape[dim] - width, cells.shape[dim], axis=dim)
        cells = jnp.concatenate(
            [
                lax.ppermute(tail, axis, [(i, (i + 1) % count) for i in range(ends)]),
                cells,
                lax.ppermute(head, axis, [((i + 1) % count, i) for i in range(ends)]),
            ],
            axis=dim,
        )
    return cells


def toeplitz_band(taps, n_out, n_in):
    period = jnp.concatenate([taps, jnp.zeros((n_in + 1 - taps.shape[0],), taps.dtype)])
    return jnp.tile(period, n_out)[: n_out * n_in].reshape(n_out, n_in)


def resolution_of(parcel):
    first = (parcel >= P1).astype(jnp.int32)
    second = (parcel >= P1 + P2).astype(jnp.int32)
    third = (parcel >= P1 + P2 + P3).astype(jnp.int32)
    return first + second + third


def centered_rows(extended, length):
    level_mean = jnp.mean(extended[:, :, LAG : LAG + length], axis=2, keepdims=True)
    centered = (extended - level_mean).astype(jnp.bfloat16)
    middle = centered[:, :, LAG : LAG + length]
    middle_wide = middle.astype(jnp.float32)
    spread = lax.rsqrt(jnp.mean(middle_wide * middle_wide, axis=2) + EPSILON)
    return (centered, middle, spread)


def mesh_peers(nx, nz):
    me = lax.axis_index("vert")
    tm = lax.axis_index("tm")
    mx, mz = me // nz, me % nz
    return me, tm, mx, mz


def greet(mx, mz, tm, nx, nz, n_tm=0):
    barrier = pltpu.get_barrier_semaphore()
    me = mx * nz + mz
    peers = [(lax.rem(mx + k, nx) * nz + mz, tm) for k in range(1, nx)]
    peers += [(mx * nz + lax.rem(mz + k, nz), tm) for k in range(1, nz)]
    if n_tm:
        peers += [(me, lax.rem(tm + 1, n_tm)), (me, lax.rem(tm + n_tm - 1, n_tm))]
    for peer in peers:
        pl.semaphore_signal(barrier, inc=1, device_id=peer, device_id_type=pl.DeviceIdType.MESH)
    pl.semaphore_wait(barrier, len(peers))


def reduce_kernel(nx, nz, n_tm, par_dev, ids_ref, env_ref, out_ref, x_ref, recv_a, send_a, part, recv_b, mine,
                  halo, a_send, a_recv, b_send, b_recv, t_send, t_recv):
    me, tm, mx, mz = mesh_peers(nx, nz)
    greet(mx, mz, tm, nx, nz, n_tm)
    hz = nz // 2
    rows = x_ref.shape[1]
    r = lax.broadcasted_iota(jnp.int32, (rows, 1), 0)

    def pool_groups(first_offset, carry, count=2 * nz, part_of=None):
        def one(j, c):
            if part_of is None:
                owner = lax.rem(mx + first_offset + 2 * (j // nz), nx) * nz + j % nz
            else:
                side = j // hz
                owner = lax.rem(mx + first_offset + 2 * side, nx) * nz + (part_of + side - 2 * part_of * side) * hz + j % hz
            wanted = jnp.where(r < par_dev, owner * par_dev + r, -1)
            hits = (ids_ref[0] == wanted).astype(jnp.float32)
            for level in range(1, ids_ref.shape[0]):
                hits = hits + (ids_ref[level] == wanted).astype(jnp.float32)
            x_ref[owner] = jnp.dot(
                hits.astype(jnp.bfloat16), env_ref[...], preferred_element_type=jnp.float32
            )
            return c

        return lax.fori_loop(0, count, one, carry)

    pool_groups(nx - 1, 0, nz, 0)
    peers = (lax.rem(mx + 1, nx), lax.rem(mx + nx - 1, nx))

    def owners_of(g, d):
        return pl.ds(g * nz + d * hz, hz)

    for s in range(1, nx):
        copies = []
        for d in range(2):
            g = lax.rem(mx + (s if d else nx * s - s), nx)
            if s == 1:
                src = x_ref.at[owners_of(g, d)]
            else:
                send_a[d, s - 2] = recv_a[d, s - 2] + x_ref[owners_of(g, d)]
                src = send_a.at[d, s - 2]
            copy = pltpu.make_async_remote_copy(
                src_ref=src, dst_ref=recv_a.at[d, s - 1],
                send_sem=a_send.at[d, s - 1], recv_sem=a_recv.at[d, s - 1],
                device_id=(peers[d] * nz + mz, tm), device_id_type=pl.DeviceIdType.MESH,
            )
            copy.start()
            copies.append(copy)
        if s == 1:
            pool_groups(nx - 1, 0, nz, 1)
            pool_groups(2, 0)
        for copy in copies:
            copy.wait()
    for d in range(2):
        part[d * hz : (d + 1) * hz] = recv_a[d, nx - 2] + x_ref[owners_of(mx, d)]
    copies = []
    for k in range(1, nz):
        pz = lax.rem(mz + k, nz)
        copy = pltpu.make_async_remote_copy(
            src_ref=part.at[pz], dst_ref=recv_b.at[k - 1],
            send_sem=b_send.at[k - 1], recv_sem=b_recv.at[k - 1],
            device_id=(mx * nz + pz, tm), device_id_type=pl.DeviceIdType.MESH,
        )
        copy.start()
        copies.append(copy)
    for copy in copies:
        copy.wait()
    total = part[mz]
    for k in range(1, nz):
        total = total + recv_b[k - 1]
    mine[...] = total
    copies = []
    for d, step in enumerate((1, n_tm - 1)):
        copy = pltpu.make_async_remote_copy(
            src_ref=mine, dst_ref=halo.at[d],
            send_sem=t_send.at[d], recv_sem=t_recv.at[d],
            device_id=(me, lax.rem(tm + step, n_tm)), device_id_type=pl.DeviceIdType.MESH,
        )
        copy.start()
        copies.append(copy)
    out_ref[1] = total
    for copy in copies:
        copy.wait()
    out_ref[0] = halo[0]
    out_ref[2] = halo[1]


def reduce_to_owner(global_ids, flat_env, nx, nz, n_tm, par_dev):
    levels, vertices = global_ids.shape
    w = flat_env.shape[1]
    rows = ROW_PAD
    hz = nz // 2
    dtype = jnp.float32
    return pl.pallas_call(
        partial(reduce_kernel, nx, nz, n_tm, par_dev),
        out_shape=jax.ShapeDtypeStruct((3, rows, w), dtype),
        in_specs=[pl.BlockSpec(memory_space=pltpu.VMEM)] * 2,
        out_specs=pl.BlockSpec(memory_space=pltpu.VMEM),
        scratch_shapes=[
            pltpu.VMEM((nx * nz, rows, w), dtype),
            pltpu.VMEM((2, nx - 1, hz, rows, w), dtype),
            pltpu.VMEM((2, nx - 2, hz, rows, w), dtype),
            pltpu.VMEM((nz, rows, w), dtype),
            pltpu.VMEM((nz - 1, rows, w), dtype),
            pltpu.VMEM((rows, w), dtype),
            pltpu.VMEM((2, rows, w), dtype),
            pltpu.SemaphoreType.DMA((2, nx - 1)),
            pltpu.SemaphoreType.DMA((2, nx - 1)),
            pltpu.SemaphoreType.DMA((nz - 1,)),
            pltpu.SemaphoreType.DMA((nz - 1,)),
            pltpu.SemaphoreType.DMA((2,)),
            pltpu.SemaphoreType.DMA((2,)),
        ],
        compiler_params=pltpu.CompilerParams(collective_id=0, has_side_effects=True),
    )(global_ids.reshape(levels, 1, vertices), flat_env)


def fill_lags(mid_ref, lhs_ref, band):
    rows = mid_ref.shape[1]
    base = mid_ref[band].astype(jnp.float32)
    for q in range(NLAG):
        lhs_ref[band, q * rows : (q + 1) * rows, :] = pltpu.roll(base, q, 1).astype(lhs_ref.dtype)
    lhs_ref[band, NLAG * rows :, :] = jnp.zeros(
        ((LAG_PAD - NLAG) * rows, lhs_ref.shape[2]), lhs_ref.dtype
    )


def fold_group(g, group, lhs_ref, gath, out_ref, spread_ref, level_ref, t_dev):
    rows = lhs_ref.shape[1] // LAG_PAD
    kept = out_ref.shape[1]
    step = LAG_PAD // LAG_CHUNKS
    first = pl.multiple_of(g * group, 128)
    same = (level_ref[:, 0:1] == level_ref[:, pl.ds(pl.multiple_of(g * group + 128, 128), group)]).astype(jnp.float32)

    def one_band(band, carry):
        block = gath[band, pl.ds(first, group), :].astype(jnp.float32)
        rhs_wide = block.T
        rhs = rhs_wide.astype(jnp.bfloat16)
        middle = rhs_wide[LAG : LAG + t_dev, :]
        spread = lax.rsqrt(jnp.sum(middle * middle, axis=0, keepdims=True) / t_dev + EPSILON)
        acc = jnp.zeros((rows, group), jnp.float32)
        for h in range(LAG_CHUNKS):
            lhs = lhs_ref[band, h * step * rows : (h + 1) * step * rows, :]
            r = jnp.dot(lhs, rhs, preferred_element_type=jnp.float32)
            acc = acc + (r * r).reshape(step, rows, group).sum(axis=0)
        scale = spread_ref[band] * spread / t_dev
        out_ref[band, :, pl.ds(first, group)] = (acc * (scale * scale) * same / NLAG)[:kept]
        return carry

    lax.fori_loop(0, out_ref.shape[0], one_band, 0)


def gather_fold_kernel(nx, nz, t_dev, own_ref, mid_ref, spread_ref, level_ref, out_ref, gath, lhs_ref,
                       a_send, a_recv, b_send, b_recv, local_sem):
    me, tm, mx, mz = mesh_peers(nx, nz)
    rows = own_ref.shape[1]
    group = nz * rows
    greet(mx, mz, tm, nx, nz)
    mine = gath.at[:, pl.ds(me * rows, rows), :]
    own = pltpu.make_async_copy(own_ref, mine, local_sem)
    own.start()
    copies = []
    for k in range(1, nz):
        copy = pltpu.make_async_remote_copy(
            src_ref=own_ref, dst_ref=mine,
            send_sem=a_send.at[k - 1], recv_sem=a_recv.at[k - 1],
            device_id=(mx * nz + lax.rem(mz + k, nz), tm), device_id_type=pl.DeviceIdType.MESH,
        )
        copy.start()
        copies.append(copy)
    for band in range(mid_ref.shape[0]):
        fill_lags(mid_ref, lhs_ref, band)
    own.wait()
    for copy in copies:
        copy.wait()
    left, right = lax.rem(mx + nx - 1, nx), lax.rem(mx + 1, nx)
    half = group // 2

    def ring_copy(start, size, peer, slot):
        rows_at = gath.at[:, pl.ds(start, size), :]
        return pltpu.make_async_remote_copy(
            src_ref=rows_at, dst_ref=rows_at,
            send_sem=b_send.at[slot], recv_sem=b_recv.at[slot],
            device_id=(peer * nz + mz, tm), device_id_type=pl.DeviceIdType.MESH,
        )

    near = [ring_copy(mx * group, group, right, 0), ring_copy(mx * group, group, left, 1)]
    for copy in near:
        copy.start()
    fold_group(mx, group, lhs_ref, gath, out_ref, spread_ref, level_ref, t_dev)
    for copy in near:
        copy.wait_recv()
    far = [ring_copy(left * group, half, right, 2), ring_copy(right * group + half, half, left, 3)]
    for copy in far:
        copy.start()
    fold_group(left, group, lhs_ref, gath, out_ref, spread_ref, level_ref, t_dev)
    fold_group(right, group, lhs_ref, gath, out_ref, spread_ref, level_ref, t_dev)
    for copy in far:
        copy.wait_recv()
    fold_group(lax.rem(mx + 2, nx), group, lhs_ref, gath, out_ref, spread_ref, level_ref, t_dev)
    for copy in near + far:
        copy.wait_send()


def gather_fold(own, mid, spread, levels, nx, nz, t_dev, kept):
    assert nx == 4
    bands, rows, width = own.shape
    cols = nx * nz * rows
    flops = 2 * bands * LAG_PAD * rows * width * cols
    return pl.pallas_call(
        partial(gather_fold_kernel, nx, nz, t_dev),
        out_shape=jax.ShapeDtypeStruct((bands, kept, cols), jnp.float32),
        in_specs=[pl.BlockSpec(memory_space=pltpu.VMEM)] * 4,
        out_specs=pl.BlockSpec(memory_space=pltpu.VMEM),
        scratch_shapes=[
            pltpu.VMEM((bands, cols, width), own.dtype),
            pltpu.VMEM((bands, LAG_PAD * rows, width), jnp.bfloat16),
            pltpu.SemaphoreType.DMA((nz - 1,)),
            pltpu.SemaphoreType.DMA((nz - 1,)),
            pltpu.SemaphoreType.DMA((4,)),
            pltpu.SemaphoreType.DMA((4,)),
            pltpu.SemaphoreType.DMA(()),
        ],
        compiler_params=pltpu.CompilerParams(
            collective_id=1, has_side_effects=True, vmem_limit_bytes=48 * 1024 * 1024
        ),
        cost_estimate=pl.CostEstimate(
            flops=flops, bytes_accessed=2 * (own.size + mid.size) + 4 * bands * rows * cols,
            transcendentals=0,
        ),
    )(own, mid, spread, levels)


def local(source, band_taps, smooth_taps, parcel_ids):
    vert_dev, t_dev = source.shape
    owners = lax.axis_size("vert")
    total_par = (P1 + P2 + P3 + owners - 1) // owners * owners
    par_dev = total_par // owners
    n_mid = t_dev + 2 * HALF
    n_in = t_dev + 4 * HALF
    first_rows = jax.vmap(partial(toeplitz_band, n_out=n_mid, n_in=n_in))(
        band_taps.reshape(2 * BANDS, TAPS)
    )
    first_mat = first_rows.transpose(2, 0, 1).reshape(n_in, 2 * BANDS * n_mid)
    second_rows = jax.vmap(partial(toeplitz_band, n_out=t_dev, n_in=n_mid))(smooth_taps)
    second_mat = second_rows.transpose(0, 2, 1)
    widened = extended_2(source, (("tm", 1),), 2 * HALF)
    wave = jnp.dot(widened, first_mat, preferred_element_type=jnp.float32).reshape(
        vert_dev, 2, BANDS, n_mid
    )
    power = (wave[:, 0] * wave[:, 0] + wave[:, 1] * wave[:, 1]).astype(jnp.bfloat16)
    envelope = jnp.einsum(
        "vbu,but->vbt", power, second_mat, preferred_element_type=jnp.float32
    ).astype(jnp.bfloat16)
    flat_env = envelope.reshape(vert_dev, BANDS * t_dev)
    offsets = jnp.array([0, P1, P1 + P2], dtype=jnp.int32)
    global_ids = parcel_ids + offsets[:, None]
    owner_start = lax.axis_index("vert") * par_dev

    nx = owners // VERT_MINOR
    n_tm = lax.axis_size("tm")
    tm = lax.axis_index("tm")
    sums3 = reduce_to_owner(global_ids, flat_env, nx, VERT_MINOR, n_tm, par_dev)[:, :par_dev].reshape(3, par_dev, BANDS, t_dev)
    before = jnp.where(tm > 0, sums3[0, :, :, t_dev - LAG :], 0.0)
    after = jnp.where(tm < n_tm - 1, sums3[2, :, :, :LAG], 0.0)
    own_ext = jnp.concatenate([before, sums3[1], after], axis=2)
    centered, own_middle, own_spread = centered_rows(own_ext, t_dev)

    own = jnp.pad(centered.transpose(1, 0, 2), ((0, 0), (0, ROW_PAD - par_dev), (0, 0)))
    mid = jnp.pad(
        own_middle.transpose(1, 0, 2), ((0, 0), (0, ROW_PAD - par_dev), (0, t_dev))
    )
    spread = jnp.pad(own_spread.T, ((0, 0), (0, ROW_PAD - par_dev)))[:, :, None]
    r = lax.iota(jnp.int32, ROW_PAD)
    own_level = jnp.where(
        r < par_dev, resolution_of(owner_start + r), -2
    ).astype(jnp.float32)
    own_level = jnp.where(own_level < 3, own_level, -2.0)
    col = lax.iota(jnp.int32, owners * ROW_PAD)
    col_level = jnp.where(
        col % ROW_PAD < par_dev, resolution_of(col // ROW_PAD * par_dev + col % ROW_PAD), -1
    ).astype(jnp.float32)
    levels = jnp.concatenate(
        [jnp.broadcast_to(own_level[:, None], (ROW_PAD, 128)),
         jnp.broadcast_to(col_level[None, :], (ROW_PAD, owners * ROW_PAD))], axis=1
    )
    padded = gather_fold(own, mid, spread, levels, nx, VERT_MINOR, t_dev, par_dev)
    coupling = padded.reshape(BANDS, par_dev, owners, ROW_PAD)[:, :, :, :par_dev]
    coupling = coupling.reshape(BANDS, par_dev, total_par)
    return coupling[None]


def solution(mesh):
    return jax.shard_map(
        local,
        mesh=mesh,
        in_specs=(P("vert", "tm"), P(), P(), P(None, "vert")),
        out_specs=P("tm", None, "vert", None),
        check_vma=False,
    )
```

```python
from functools import partial

import jax
import jax.numpy as jnp
from jax import lax
from jax.experimental import pallas as pl
from jax.experimental.pallas import tpu as pltpu
from jax.sharding import PartitionSpec as P

P1 = 100
P2 = 400
P3 = 1000
BANDS = 2
TAPS = 65
HALF = 32
LAG = 64
LAG_STEP = 1
NLAG = 129

EPSILON = 1e-05

ROW_PAD = 96
LAG_CHUNKS = 22
LAG_PAD = 132
VERT_MINOR = 4


def extended_2(cells, sides, width):
    for axis, dim in sides:
        count = lax.axis_size(axis)
        ends = count - 1
        head = lax.slice_in_dim(cells, 0, width, axis=dim)
        tail = lax.slice_in_dim(cells, cells.shape[dim] - width, cells.shape[dim], axis=dim)
        cells = jnp.concatenate(
            [
                lax.ppermute(tail, axis, [(i, (i + 1) % count) for i in range(ends)]),
                cells,
                lax.ppermute(head, axis, [((i + 1) % count, i) for i in range(ends)]),
            ],
            axis=dim,
        )
    return cells


def toeplitz_band(taps, n_out, n_in):
    period = jnp.concatenate([taps, jnp.zeros((n_in + 1 - taps.shape[0],), taps.dtype)])
    return jnp.tile(period, n_out)[: n_out * n_in].reshape(n_out, n_in)


def resolution_of(parcel):
    first = (parcel >= P1).astype(jnp.int32)
    second = (parcel >= P1 + P2).astype(jnp.int32)
    third = (parcel >= P1 + P2 + P3).astype(jnp.int32)
    return first + second + third


def centered_rows(extended, length):
    level_mean = jnp.mean(extended[:, :, LAG : LAG + length], axis=2, keepdims=True)
    centered = (extended - level_mean).astype(jnp.bfloat16)
    middle = centered[:, :, LAG : LAG + length]
    middle_wide = middle.astype(jnp.float32)
    spread = lax.rsqrt(jnp.mean(middle_wide * middle_wide, axis=2) + EPSILON)
    return (centered, middle, spread)


def mesh_peers(nx, nz):
    me = lax.axis_index("vert")
    tm = lax.axis_index("tm")
    mx, mz = me // nz, me % nz
    return me, tm, mx, mz


def greet(mx, mz, tm, nx, nz, n_tm=0):
    barrier = pltpu.get_barrier_semaphore()
    me = mx * nz + mz
    peers = [(lax.rem(mx + k, nx) * nz + mz, tm) for k in range(1, nx)]
    peers += [(mx * nz + lax.rem(mz + k, nz), tm) for k in range(1, nz)]
    if n_tm:
        peers += [(me, lax.rem(tm + 1, n_tm)), (me, lax.rem(tm + n_tm - 1, n_tm))]
    for peer in peers:
        pl.semaphore_signal(barrier, inc=1, device_id=peer, device_id_type=pl.DeviceIdType.MESH)
    pl.semaphore_wait(barrier, len(peers))


def reduce_kernel(nx, nz, n_tm, par_dev, ids_ref, env_ref, out_ref, x_ref, recv_a, send_a, part, recv_b, mine,
                  halo, a_send, a_recv, b_send, b_recv, t_send, t_recv):
    me, tm, mx, mz = mesh_peers(nx, nz)
    greet(mx, mz, tm, nx, nz, n_tm)
    hz = nz // 2
    rows = x_ref.shape[1]
    r = lax.broadcasted_iota(jnp.int32, (rows, 1), 0)

    def pool_groups(first_offset, carry, count=2 * nz, part_of=None):
        def one(j, c):
            if part_of is None:
                owner = lax.rem(mx + first_offset + 2 * (j // nz), nx) * nz + j % nz
            else:
                side = j // hz
                owner = lax.rem(mx + first_offset + 2 * side, nx) * nz + (part_of + side - 2 * part_of * side) * hz + j % hz
            wanted = jnp.where(r < par_dev, owner * par_dev + r, -1)
            hits = (ids_ref[0] == wanted).astype(jnp.float32)
            for level in range(1, ids_ref.shape[0]):
                hits = hits + (ids_ref[level] == wanted).astype(jnp.float32)
            x_ref[owner] = jnp.dot(
                hits.astype(jnp.bfloat16), env_ref[...], preferred_element_type=jnp.float32
            )
            return c

        return lax.fori_loop(0, count, one, carry)

    pool_groups(nx - 1, 0, nz, 0)
    peers = (lax.rem(mx + 1, nx), lax.rem(mx + nx - 1, nx))

    def owners_of(g, d):
        return pl.ds(g * nz + d * hz, hz)

    for s in range(1, nx):
        copies = []
        for d in range(2):
            g = lax.rem(mx + (s if d else nx * s - s), nx)
            if s == 1:
                src = x_ref.at[owners_of(g, d)]
            else:
                send_a[d, s - 2] = recv_a[d, s - 2] + x_ref[owners_of(g, d)]
                src = send_a.at[d, s - 2]
            copy = pltpu.make_async_remote_copy(
                src_ref=src, dst_ref=recv_a.at[d, s - 1],
                send_sem=a_send.at[d, s - 1], recv_sem=a_recv.at[d, s - 1],
                device_id=(peers[d] * nz + mz, tm), device_id_type=pl.DeviceIdType.MESH,
            )
            copy.start()
            copies.append(copy)
        if s == 1:
            pool_groups(nx - 1, 0, nz, 1)
            pool_groups(2, 0)
        for copy in copies:
            copy.wait()
    for d in range(2):
        part[d * hz : (d + 1) * hz] = recv_a[d, nx - 2] + x_ref[owners_of(mx, d)]
    copies = []
    for k in range(1, nz):
        pz = lax.rem(mz + k, nz)
        copy = pltpu.make_async_remote_copy(
            src_ref=part.at[pz], dst_ref=recv_b.at[k - 1],
            send_sem=b_send.at[k - 1], recv_sem=b_recv.at[k - 1],
            device_id=(mx * nz + pz, tm), device_id_type=pl.DeviceIdType.MESH,
        )
        copy.start()
        copies.append(copy)
    for copy in copies:
        copy.wait()
    total = part[mz]
    for k in range(1, nz):
        total = total + recv_b[k - 1]
    mine[...] = total
    copies = []
    for d, step in enumerate((1, n_tm - 1)):
        copy = pltpu.make_async_remote_copy(
            src_ref=mine, dst_ref=halo.at[d],
            send_sem=t_send.at[d], recv_sem=t_recv.at[d],
            device_id=(me, lax.rem(tm + step, n_tm)), device_id_type=pl.DeviceIdType.MESH,
        )
        copy.start()
        copies.append(copy)
    out_ref[1] = total
    for copy in copies:
        copy.wait()
    out_ref[0] = halo[0]
    out_ref[2] = halo[1]


def reduce_to_owner(global_ids, flat_env, nx, nz, n_tm, par_dev):
    levels, vertices = global_ids.shape
    w = flat_env.shape[1]
    rows = ROW_PAD
    hz = nz // 2
    dtype = jnp.float32
    return pl.pallas_call(
        partial(reduce_kernel, nx, nz, n_tm, par_dev),
        out_shape=jax.ShapeDtypeStruct((3, rows, w), dtype),
        in_specs=[pl.BlockSpec(memory_space=pltpu.VMEM)] * 2,
        out_specs=pl.BlockSpec(memory_space=pltpu.VMEM),
        scratch_shapes=[
            pltpu.VMEM((nx * nz, rows, w), dtype),
            pltpu.VMEM((2, nx - 1, hz, rows, w), dtype),
            pltpu.VMEM((2, nx - 2, hz, rows, w), dtype),
            pltpu.VMEM((nz, rows, w), dtype),
            pltpu.VMEM((nz - 1, rows, w), dtype),
            pltpu.VMEM((rows, w), dtype),
            pltpu.VMEM((2, rows, w), dtype),
            pltpu.SemaphoreType.DMA((2, nx - 1)),
            pltpu.SemaphoreType.DMA((2, nx - 1)),
            pltpu.SemaphoreType.DMA((nz - 1,)),
            pltpu.SemaphoreType.DMA((nz - 1,)),
            pltpu.SemaphoreType.DMA((2,)),
            pltpu.SemaphoreType.DMA((2,)),
        ],
        compiler_params=pltpu.CompilerParams(collective_id=0, has_side_effects=True),
    )(global_ids.reshape(levels, 1, vertices), flat_env)


def fill_lags(mid_ref, lhs_ref, band):
    rows = mid_ref.shape[1]
    base = mid_ref[band].astype(jnp.float32)
    for q in range(NLAG):
        lhs_ref[band, q * rows : (q + 1) * rows, :] = pltpu.roll(base, q, 1).astype(lhs_ref.dtype)
    lhs_ref[band, NLAG * rows :, :] = jnp.zeros(
        ((LAG_PAD - NLAG) * rows, lhs_ref.shape[2]), lhs_ref.dtype
    )


def fold_group(g, group, lhs_ref, gath, out_ref, spread_ref, level_ref, t_dev):
    rows = lhs_ref.shape[1] // LAG_PAD
    kept = out_ref.shape[1]
    step = LAG_PAD // LAG_CHUNKS
    first = pl.multiple_of(g * group, 128)
    same = (level_ref[:, 0:1] == level_ref[:, pl.ds(pl.multiple_of(g * group + 128, 128), group)]).astype(jnp.float32)

    def one_band(band, carry):
        block = gath[band, pl.ds(first, group), :].astype(jnp.float32)
        rhs_wide = block.T
        rhs = rhs_wide.astype(jnp.bfloat16)
        middle = rhs_wide[LAG : LAG + t_dev, :]
        spread = lax.rsqrt(jnp.sum(middle * middle, axis=0, keepdims=True) / t_dev + EPSILON)
        acc = jnp.zeros((rows, group), jnp.float32)
        for h in range(LAG_CHUNKS):
            lhs = lhs_ref[band, h * step * rows : (h + 1) * step * rows, :]
            r = jnp.dot(lhs, rhs, preferred_element_type=jnp.float32)
            acc = acc + (r * r).reshape(step, rows, group).sum(axis=0)
        scale = spread_ref[band] * spread / t_dev
        out_ref[band, :, pl.ds(first, group)] = (acc * (scale * scale) * same / NLAG)[:kept]
        return carry

    lax.fori_loop(0, out_ref.shape[0], one_band, 0)


def gather_fold_kernel(nx, nz, t_dev, own_ref, mid_ref, spread_ref, level_ref, out_ref, gath, lhs_ref,
                       a_send, a_recv, b_send, b_recv, local_sem):
    me, tm, mx, mz = mesh_peers(nx, nz)
    rows = own_ref.shape[1]
    group = nz * rows
    greet(mx, mz, tm, nx, nz)
    mine = gath.at[:, pl.ds(me * rows, rows), :]
    own = pltpu.make_async_copy(own_ref, mine, local_sem)
    own.start()
    copies = []
    for k in range(1, nz):
        copy = pltpu.make_async_remote_copy(
            src_ref=own_ref, dst_ref=mine,
            send_sem=a_send.at[k - 1], recv_sem=a_recv.at[k - 1],
            device_id=(mx * nz + lax.rem(mz + k, nz), tm), device_id_type=pl.DeviceIdType.MESH,
        )
        copy.start()
        copies.append(copy)
    for band in range(mid_ref.shape[0]):
        fill_lags(mid_ref, lhs_ref, band)
    own.wait()
    for copy in copies:
        copy.wait()
    left, right = lax.rem(mx + nx - 1, nx), lax.rem(mx + 1, nx)
    half = group // 2

    def ring_copy(start, size, peer, slot):
        rows_at = gath.at[:, pl.ds(start, size), :]
        return pltpu.make_async_remote_copy(
            src_ref=rows_at, dst_ref=rows_at,
            send_sem=b_send.at[slot], recv_sem=b_recv.at[slot],
            device_id=(peer * nz + mz, tm), device_id_type=pl.DeviceIdType.MESH,
        )

    near = [ring_copy(mx * group, group, right, 0), ring_copy(mx * group, group, left, 1)]
    for copy in near:
        copy.start()
    fold_group(mx, group, lhs_ref, gath, out_ref, spread_ref, level_ref, t_dev)
    for copy in near:
        copy.wait_recv()
    far = [ring_copy(left * group, half, right, 2), ring_copy(right * group + half, half, left, 3)]
    for copy in far:
        copy.start()
    fold_group(left, group, lhs_ref, gath, out_ref, spread_ref, level_ref, t_dev)
    fold_group(right, group, lhs_ref, gath, out_ref, spread_ref, level_ref, t_dev)
    for copy in far:
        copy.wait_recv()
    fold_group(lax.rem(mx + 2, nx), group, lhs_ref, gath, out_ref, spread_ref, level_ref, t_dev)
    for copy in near + far:
        copy.wait_send()


def gather_fold(own, mid, spread, levels, nx, nz, t_dev, kept):
    assert nx == 4
    bands, rows, width = own.shape
    cols = nx * nz * rows
    flops = 2 * bands * LAG_PAD * rows * width * cols
    return pl.pallas_call(
        partial(gather_fold_kernel, nx, nz, t_dev),
        out_shape=jax.ShapeDtypeStruct((bands, kept, cols), jnp.float32),
        in_specs=[pl.BlockSpec(memory_space=pltpu.VMEM)] * 4,
        out_specs=pl.BlockSpec(memory_space=pltpu.VMEM),
        scratch_shapes=[
            pltpu.VMEM((bands, cols, width), own.dtype),
            pltpu.VMEM((bands, LAG_PAD * rows, width), jnp.bfloat16),
            pltpu.SemaphoreType.DMA((nz - 1,)),
            pltpu.SemaphoreType.DMA((nz - 1,)),
            pltpu.SemaphoreType.DMA((4,)),
            pltpu.SemaphoreType.DMA((4,)),
            pltpu.SemaphoreType.DMA(()),
        ],
        compiler_params=pltpu.CompilerParams(
            collective_id=1, has_side_effects=True, vmem_limit_bytes=48 * 1024 * 1024
        ),
        cost_estimate=pl.CostEstimate(
            flops=flops, bytes_accessed=2 * (own.size + mid.size) + 4 * bands * rows * cols,
            transcendentals=0,
        ),
    )(own, mid, spread, levels)


def local(source, band_taps, smooth_taps, parcel_ids):
    vert_dev, t_dev = source.shape
    owners = lax.axis_size("vert")
    total_par = (P1 + P2 + P3 + owners - 1) // owners * owners
    par_dev = total_par // owners
    n_mid = t_dev + 2 * HALF
    n_in = t_dev + 4 * HALF
    first_rows = jax.vmap(partial(toeplitz_band, n_out=n_mid, n_in=n_in))(
        band_taps.reshape(2 * BANDS, TAPS)
    )
    first_mat = first_rows.transpose(2, 0, 1).reshape(n_in, 2 * BANDS * n_mid)
    second_rows = jax.vmap(partial(toeplitz_band, n_out=t_dev, n_in=n_mid))(smooth_taps)
    second_mat = second_rows.transpose(0, 2, 1)
    widened = extended_2(source, (("tm", 1),), 2 * HALF)
    wave = jnp.dot(widened, first_mat, preferred_element_type=jnp.float32).reshape(
        vert_dev, 2, BANDS, n_mid
    )
    power = (wave[:, 0] * wave[:, 0] + wave[:, 1] * wave[:, 1]).astype(jnp.bfloat16)
    envelope = jnp.einsum(
        "vbu,but->vbt", power, second_mat, preferred_element_type=jnp.float32
    ).astype(jnp.bfloat16)
    flat_env = envelope.reshape(vert_dev, BANDS * t_dev)
    offsets = jnp.array([0, P1, P1 + P2], dtype=jnp.int32)
    global_ids = parcel_ids + offsets[:, None]
    owner_start = lax.axis_index("vert") * par_dev

    nx = owners // VERT_MINOR
    n_tm = lax.axis_size("tm")
    tm = lax.axis_index("tm")
    sums3 = reduce_to_owner(global_ids, flat_env, nx, VERT_MINOR, n_tm, par_dev)[:, :par_dev].reshape(3, par_dev, BANDS, t_dev)
    before = jnp.where(tm > 0, sums3[0, :, :, t_dev - LAG :], 0.0)
    after = jnp.where(tm < n_tm - 1, sums3[2, :, :, :LAG], 0.0)
    own_ext = jnp.concatenate([before, sums3[1], after], axis=2)
    centered, own_middle, own_spread = centered_rows(own_ext, t_dev)

    own = jnp.pad(centered.transpose(1, 0, 2), ((0, 0), (0, ROW_PAD - par_dev), (0, 0)))
    mid = jnp.pad(
        own_middle.transpose(1, 0, 2), ((0, 0), (0, ROW_PAD - par_dev), (0, t_dev))
    )
    spread = jnp.pad(own_spread.T, ((0, 0), (0, ROW_PAD - par_dev)))[:, :, None]
    r = lax.iota(jnp.int32, ROW_PAD)
    own_level = jnp.where(
        r < par_dev, resolution_of(owner_start + r), -2
    ).astype(jnp.float32)
    own_level = jnp.where(own_level < 3, own_level, -2.0)
    col = lax.iota(jnp.int32, owners * ROW_PAD)
    col_level = jnp.where(
        col % ROW_PAD < par_dev, resolution_of(col // ROW_PAD * par_dev + col % ROW_PAD), -1
    ).astype(jnp.float32)
    levels = jnp.concatenate(
        [jnp.broadcast_to(own_level[:, None], (ROW_PAD, 128)),
         jnp.broadcast_to(col_level[None, :], (ROW_PAD, owners * ROW_PAD))], axis=1
    )
    padded = gather_fold(own, mid, spread, levels, nx, VERT_MINOR, t_dev, par_dev)
    coupling = padded.reshape(BANDS, par_dev, owners, ROW_PAD)[:, :, :, :par_dev]
    coupling = coupling.reshape(BANDS, par_dev, total_par)
    return coupling[None]


def solution(mesh):
    return jax.shard_map(
        local,
        mesh=mesh,
        in_specs=(P("vert", "tm"), P(), P(), P(None, "vert")),
        out_specs=P("tm", None, "vert", None),
        check_vma=False,
    )
```
